128 devices in a mesh: tok: 32 (over y, x, core), mlp: 4 (over z).
Axes of the slice: x: 4, y: 4, z: 4, core: 2. Of those that a mesh axis runs over, the one named last changes fastest.
Arguments:
- layer_input: bfloat16 [16384, 4096], P('tok'), may hold values from -80 to 80
- input_norm_gain: float32 [4096], replicated, may hold values from 0.6 to 10
- query_weight: bfloat16 [4096, 4096], P(None, 'mlp'), may hold values from -0.09375 to 0.09375
- key_weight: bfloat16 [4096, 1024], P(None, 'mlp'), may hold values from -0.09375 to 0.09375
- value_weight: bfloat16 [4096, 1024], P(None, 'mlp'), may hold values from -0.09375 to 0.09375
- query_down_maps: bfloat16 [256, 16, 4096], P('tok', None, 'mlp'), may hold values from -0.09375 to 0.09375
- value_down_maps: bfloat16 [256, 16, 4096], P('tok', None, 'mlp'), may hold values from -0.09375 to 0.09375
- query_up_maps: bfloat16 [256, 16, 4096], P('tok', None, 'mlp'), may hold values from -1.5 to 1.5
- value_up_maps: bfloat16 [256, 16, 1024], P('tok', None, 'mlp'), may hold values from -1.5 to 1.5
- tenant_prompt_length: int32 [16], replicated, may hold values from 1 to 2048, 16384 in all
- tenant_adapter_id: int32 [16], replicated, may hold values from 0 to 255
- adapter_storage_slot: int32 [256], replicated, may hold values from 0 to 255, each once
Outputs:
- attended: bfloat16 [16384, 4096], P('tok', 'mlp')
The draws below stay inside these ranges and needn't reach their ends.
Inputs may be any that keep to these rules, and one draw needn't show every extreme that they name: `tenant_prompt_length`: the lengths sum to 16384; each is at most 2048 and one of them is exactly that. `tenant_adapter_id`: tenants may share an adapter. `adapter_storage_slot`: each storage slot holds exactly one adapter.
All inputs are finite; a program needn't handle non-finite values.
Results may differ from the reference program's by a relative error of at most 0.0045.
The reference program's roundings to bfloat16 on the way count: a program that leaves them out, or rounds other values in their place, can miss the bound.
Values may be sent and summed in bfloat16 or wider, within the bound.
A program may use at most 192 MiB of HBM per device.

```python
import math
import jax
import jax.numpy as jnp
import numpy as np
from jax import lax

MODEL_WIDTH = 4096
QUERY_HEADS = 32
KEY_VALUE_HEADS = 8
HEAD_WIDTH = 128
ADAPTER_RANK = 16
ADAPTER_COUNT = 256
TENANTS = 16
LONGEST_PROMPT = 4
TOKENS_PER_PART = 512
TOKENS = 16384
N_TOK = 32


def draw_layer_input(key, part):
    streams = jax.random.split(key, 1)
    values = jnp.clip(jax.random.normal(streams[0], (TOKENS, MODEL_WIDTH), jnp.float32), -6.0, 6.0)
    return values.astype(jnp.bfloat16)


def draw_input_norm_gain(key, part):
    values = jax.random.uniform(key, (MODEL_WIDTH,), jnp.float32, 0.6, 1.6)
    return values


def plant(array, rng, least, largest):
    shape = array.shape
    place = [jax.random.randint(jax.random.fold_in(rng, axis), (), 0, shape[axis]) for axis in range(len(shape))]
    array = array.at[tuple(place)].set(least)
    longest = shape.index(max(shape))
    place[longest] = (place[longest] + 1) % shape[longest]
    return array.at[tuple(place)].set(largest)


def block_scale(own_key, shape, pieces, least, top_value):
    def one(position, blocks):
        draws = jax.random.uniform(jax.random.fold_in(jax.random.fold_in(own_key, 6), position), (blocks,), jnp.float32, least / len(pieces), top_value / len(pieces))
        return jnp.repeat(jnp.exp(draws), shape[position] // blocks).reshape((-1,) + (1,) * (len(shape) - position - 1))

    loudness = one(*pieces[0])
    for cut in pieces[1:]:
        loudness = loudness * one(*cut)
    return loudness


def profile(number_of, total, limit, lean):
    weights = [(1 << 20) // math.isqrt(grade ** lean) + 1 for grade in range(2, number_of + 1)]
    surplus, holding = total - limit - (number_of - 1), [1] * (number_of - 1)
    while surplus > 0:
        candidates = [i for i in range(number_of - 1) if holding[i] < limit]
        whole, left = sum([weights[i] for i in candidates]), surplus
        for i in candidates:
            extra = min(limit - holding[i], max(1, left * weights[i] // whole), surplus)
            holding[i] = holding[i] + extra
            surplus = surplus - extra
    return np.array([limit] + holding)


def uneven_parts(own_key, count, total, most, skew):
    if count == 2:
        one = jax.random.randint(own_key, (), max(1, total - most), min(most, total - 1) + 1)
        return jnp.stack([one, total - one])
    sizes = jnp.asarray(profile(count, total, most, skew), jnp.int32)
    couples = (count - 1) // 2
    source_of, receiver = sizes[1:1 + 2 * couples:2], sizes[2:2 + 2 * couples:2]
    margin = jnp.minimum(source_of - 1, most - receiver)
    passed = jax.random.randint(jax.random.fold_in(own_key, 1), (couples,), 0, 1 << 20) % (margin + 1)
    sizes = sizes.at[1:1 + 2 * couples:2].set(source_of - passed).at[2:2 + 2 * couples:2].set(receiver + passed)
    return sizes[jax.random.permutation(jax.random.fold_in(own_key, 2), count)]


def gaussian(rng, shape, deviation, most, cuts=(), held_as=jnp.bfloat16):
    gain = block_scale(rng, shape, cuts, -0.22, 0.18) if cuts else 1.0
    array = jax.random.normal(rng, shape, jnp.float32) * deviation * gain
    return jnp.minimum(jnp.maximum(array, -most), most).astype(held_as)


def setup_inputs(seed: int = 0) -> dict:
    keys = jax.random.split(jax.random.key(seed), 13)
    layer_input = draw_layer_input(jax.random.fold_in(keys[12], 71), 0)
    input_norm_gain = draw_input_norm_gain(jax.random.fold_in(keys[12], 71), 0)
    query_weight = gaussian(keys[2], (MODEL_WIDTH, QUERY_HEADS * HEAD_WIDTH), MODEL_WIDTH ** -0.5, 0.09375, ((1, 4),))
    key_weight = gaussian(keys[3], (MODEL_WIDTH, KEY_VALUE_HEADS * HEAD_WIDTH), MODEL_WIDTH ** -0.5, 0.09375, ((1, 4),))
    value_weight = gaussian(keys[4], (MODEL_WIDTH, KEY_VALUE_HEADS * HEAD_WIDTH), MODEL_WIDTH ** -0.5, 0.09375, ((1, 4),))
    query_down_maps = gaussian(keys[5], (ADAPTER_COUNT, ADAPTER_RANK, MODEL_WIDTH), MODEL_WIDTH ** -0.5, 0.09375, ((0, 32), (2, 4)))
    value_down_maps = gaussian(keys[6], (ADAPTER_COUNT, ADAPTER_RANK, MODEL_WIDTH), MODEL_WIDTH ** -0.5, 0.09375, ((0, 32), (2, 4)))
    query_up_maps = gaussian(keys[7], (ADAPTER_COUNT, ADAPTER_RANK, QUERY_HEADS * HEAD_WIDTH), ADAPTER_RANK ** -0.5, 1.5, ((0, 32), (2, 4)))
    value_up_maps = gaussian(keys[8], (ADAPTER_COUNT, ADAPTER_RANK, KEY_VALUE_HEADS * HEAD_WIDTH), ADAPTER_RANK ** -0.5, 1.5, ((0, 32), (2, 4)))
    tenant_prompt_length = uneven_parts(keys[9], TENANTS, TOKENS, LONGEST_PROMPT * TOKENS_PER_PART, 2).astype(jnp.int32)
    tenant_adapter_id = plant(jax.random.randint(keys[10], (TENANTS,), 0, ADAPTER_COUNT), jax.random.fold_in(keys[10], 1), 0, ADAPTER_COUNT - 1).astype(jnp.int32)
    adapter_storage_slot = jax.random.permutation(keys[11], ADAPTER_COUNT).astype(jnp.int32)
    return {"layer_input": layer_input, "input_norm_gain": input_norm_gain, "query_weight": query_weight, "key_weight": key_weight, "value_weight": value_weight, "query_down_maps": query_down_maps, "value_down_maps": value_down_maps, "query_up_maps": query_up_maps, "value_up_maps": value_up_maps, "tenant_prompt_length": tenant_prompt_length, "tenant_adapter_id": tenant_adapter_id, "adapter_storage_slot": adapter_storage_slot}


NORM_EPS = 1e-05
ROPE_BASE = 500000.0
ADAPTER_SCALE = 0.5

def rotary(values, positions):
    half_width = values.shape[-1] // 2
    exponent = jnp.arange(half_width).astype(jnp.float32) * (2.0 / values.shape[-1])
    inverse = jnp.exp(-exponent * jnp.log(jnp.float32(ROPE_BASE)))
    angles = positions.astype(jnp.float32)[:, None] * inverse[None, :]
    cosine = jnp.cos(angles)[:, None, :]
    sine = jnp.sin(angles)[:, None, :]
    first_position = values[..., :half_width]
    second = values[..., half_width:]
    return jnp.concatenate([first_position * cosine - second * sine, second * cosine + first_position * sine], axis=-1)

def tenant_of(tenant_prompt_length, indices):
    prompt_ends = jnp.cumsum(tenant_prompt_length).astype(jnp.int32)
    prompt_starts = prompt_ends - tenant_prompt_length
    tenant_ids = lax.optimization_barrier(jnp.sum((indices[:, None] >= prompt_ends[None, :]).astype(jnp.int32), axis=1))
    member = tenant_ids[:, None] == jnp.arange(tenant_prompt_length.shape[0], dtype=jnp.int32)[None, :]
    row_start = lax.optimization_barrier(jnp.sum(jnp.where(member, prompt_starts[None, :], 0), axis=1)).astype(jnp.int32)
    return (member, row_start)

def projections(normed_input, chosen, positions, query_weight, key_weight, value_weight, shrink_q, shrink_v, query_up_table, value_up_table):
    row_count = normed_input.shape[0]
    shrink_q = jnp.where(chosen, shrink_q, 0.0).astype(jnp.bfloat16)
    shrink_v = jnp.where(chosen, shrink_v, 0.0).astype(jnp.bfloat16)
    query_delta = jnp.dot(shrink_q, query_up_table.reshape(-1, query_up_table.shape[2]), preferred_element_type=jnp.float32)
    value_delta = jnp.dot(shrink_v, value_up_table.reshape(-1, value_up_table.shape[2]), preferred_element_type=jnp.float32)
    query_rows = jnp.dot(normed_input, query_weight, preferred_element_type=jnp.float32) + ADAPTER_SCALE * query_delta
    query_rows = rotary(query_rows.reshape(row_count, -1, HEAD_WIDTH), positions).astype(jnp.bfloat16)
    key = jnp.dot(normed_input, key_weight, preferred_element_type=jnp.float32)
    key = rotary(key.reshape(row_count, -1, HEAD_WIDTH), positions).astype(jnp.bfloat16)
    value_rows = jnp.dot(normed_input, value_weight, preferred_element_type=jnp.float32) + ADAPTER_SCALE * value_delta
    value_rows = value_rows.astype(jnp.bfloat16).reshape(row_count, -1, HEAD_WIDTH)
    return (query_rows, key, value_rows)

def contract(left, table):
    flat = table.reshape(-1, table.shape[2])
    return lax.dot_general(left, flat, (((1,), (1,)), ((), ())), preferred_element_type=jnp.float32)

def attend(query_rows, key, value_rows, row_start):
    span = (LONGEST_PROMPT + 1) * TOKENS_PER_PART
    head_groups = QUERY_HEADS // KEY_VALUE_HEADS
    padding_rows = jnp.zeros((LONGEST_PROMPT * TOKENS_PER_PART, KEY_VALUE_HEADS, HEAD_WIDTH), jnp.bfloat16)
    pad_key = jnp.concatenate([padding_rows, key], axis=0)
    pad_value = jnp.concatenate([padding_rows, value_rows], axis=0)

    def one_block(index):
        first_position = (index * TOKENS_PER_PART).astype(jnp.int32)
        query_block = lax.dynamic_slice_in_dim(query_rows, first_position, TOKENS_PER_PART, 0).astype(jnp.float32).reshape(TOKENS_PER_PART, KEY_VALUE_HEADS, head_groups, HEAD_WIDTH)
        k_block = lax.dynamic_slice_in_dim(pad_key, first_position, span, 0).astype(jnp.float32)
        v_block = lax.dynamic_slice_in_dim(pad_value, first_position, span, 0).astype(jnp.float32)
        starts = lax.dynamic_slice_in_dim(row_start, first_position, TOKENS_PER_PART, 0)
        q_index = first_position + jnp.arange(TOKENS_PER_PART, dtype=jnp.int32)
        k_index = first_position - LONGEST_PROMPT * TOKENS_PER_PART + jnp.arange(span, dtype=jnp.int32)
        allowed = (k_index[None, :] >= starts[:, None]) & (k_index[None, :] <= q_index[:, None])
        scores = jnp.einsum('qhgd,khd->hgqk', query_block, k_block) * HEAD_WIDTH ** (-0.5)
        scores = jnp.where(allowed[None, None], scores, -jnp.inf)
        peak = lax.optimization_barrier(jnp.max(scores, axis=-1, keepdims=True))
        weights = jnp.exp(scores - peak)
        totals = lax.optimization_barrier(jnp.sum(weights, axis=-1))
        rounded = lax.optimization_barrier(weights.astype(jnp.bfloat16)).astype(jnp.float32)
        mixed = jnp.einsum('hgqk,khd->qhgd', rounded, v_block)
        result = mixed / jnp.transpose(totals, (2, 0, 1))[..., None]
        return result.astype(jnp.bfloat16).reshape(TOKENS_PER_PART, QUERY_HEADS * HEAD_WIDTH)
    blocks = lax.map(one_block, jnp.arange(N_TOK, dtype=jnp.int32))
    return blocks.reshape(TOKENS, QUERY_HEADS * HEAD_WIDTH)

def reference(layer_input, input_norm_gain, query_weight, key_weight, value_weight, query_down_maps, value_down_maps, query_up_maps, value_up_maps, tenant_prompt_length, tenant_adapter_id, adapter_storage_slot):
    widened = layer_input.astype(jnp.float32)
    scale_row = lax.rsqrt(lax.optimization_barrier(jnp.mean(widened * widened, axis=1, keepdims=True)) + NORM_EPS)
    normed_input = (widened * scale_row * input_norm_gain.astype(jnp.float32)[None, :]).astype(jnp.bfloat16)
    indices = jnp.arange(TOKENS, dtype=jnp.int32)
    member, row_start = tenant_of(tenant_prompt_length, indices)
    positions = indices - row_start
    chosen = jnp.repeat(member, ADAPTER_RANK, axis=1)
    storage_slots = adapter_storage_slot[tenant_adapter_id]
    query_down_table = query_down_maps[storage_slots]
    value_down_table = value_down_maps[storage_slots]
    query_up_table = query_up_maps[storage_slots]
    value_up_table = value_up_maps[storage_slots]
    shrink_q = contract(normed_input, query_down_table)
    shrink_v = contract(normed_input, value_down_table)
    query_rows, key, value_rows = projections(normed_input, chosen, positions, query_weight, key_weight, value_weight, shrink_q, shrink_v, query_up_table, value_up_table)
    return attend(query_rows, key, value_rows, row_start)
```

```python
import functools

import jax
import jax.numpy as jnp
import numpy as np
from jax import lax
from jax.experimental import pallas as pl
from jax.experimental.pallas import tpu as pltpu
from jax.sharding import PartitionSpec as P

WIDTH = 4096
HEAD = 128
RANK = 16
TENANTS = 16
ROWS = 512
HELD = 8
QCOLS = 1024
KVCOLS = 256
BACK = 4
N_TOK = 32
SIDE = 4
NORM_EPS = 1e-05
ROPE_BASE = 500000.0
ADAPTER_SCALE = 0.5
MESH = pl.DeviceIdType.MESH
F32 = jnp.float32
BF16 = jnp.bfloat16
SLAB = TENANTS * RANK
V_ROWS = (1024 + KVCOLS) // 128 * SLAB
Q_ROWS = (1024 + QCOLS) // 128 * SLAB
NORM_STEP = 32
COPIES = 14


def prompt_bounds(len_ref):
    starts, ends = [], []
    at = jnp.int32(0)
    for t in range(TENANTS):
        starts.append(at)
        at = at + len_ref[t]
        ends.append(at)
    return starts, ends


class AllReduce:
    def __init__(self, place, rows, mine, from_core, from_a, from_b, full, send, recv):
        self.place, self.rows = place, rows
        self.mine, self.from_core, self.from_a, self.from_b = mine, from_core, from_a, from_b
        self.full, self.send, self.recv = full, send, recv
        p = place
        half, quarter, piece = rows // 2, rows // 8, rows // 32
        self.half_at = pl.multiple_of(p["core"] * half, 16)
        self.other_at = pl.multiple_of((1 - p["core"]) * half, 16)
        self.a_at = pl.multiple_of(p["core"] * half + p["ca"] * quarter, 16)
        self.b_at = pl.multiple_of(p["core"] * half + p["ca"] * quarter + p["cb"] * piece, 16)

    def copy(self, slot, src, dst, dev):
        return pltpu.make_async_remote_copy(
            src_ref=src, dst_ref=dst, send_sem=self.send.at[slot], recv_sem=self.recv.at[slot],
            device_id=dev, device_id_type=MESH,
        )

    def copies(self, stage):
        p = self.place
        half, quarter, piece = self.rows // 2, self.rows // 8, self.rows // 32
        if stage == 0:
            return [self.copy(0, self.mine.at[pl.ds(self.other_at, half)], self.from_core, p["sib"])]
        if stage == 5:
            ref = self.full.at[pl.ds(self.half_at, half)]
            return [self.copy(13, ref, ref, p["sib"])]
        out = []
        for k in range(1, SIDE):
            a, b = (p["ca"] + k) % SIDE, (p["cb"] + k) % SIDE
            if stage == 1:
                at = pl.multiple_of(p["core"] * half + a * quarter, 16)
                out.append(self.copy(k, self.mine.at[pl.ds(at, quarter)], self.from_a.at[k - 1], p["peer_a"][k]))
            if stage == 2:
                at = pl.multiple_of(p["core"] * half + p["ca"] * quarter + b * piece, 16)
                out.append(self.copy(3 + k, self.mine.at[pl.ds(at, piece)], self.from_b.at[k - 1], p["peer_b"][k]))
            if stage == 3:
                ref = self.full.at[pl.ds(self.b_at, piece)]
                out.append(self.copy(6 + k, ref, ref, p["peer_b"][k]))
            if stage == 4:
                ref = self.full.at[pl.ds(self.a_at, quarter)]
                out.append(self.copy(9 + k, ref, ref, p["peer_a"][k]))
        return out

    def start(self, stage):
        for c in self.copies(stage):
            c.start()

    def arrive(self, stage):
        for c in self.copies(stage):
            c.wait()
        half, quarter, piece = self.rows // 2, self.rows // 8, self.rows // 32
        if stage == 0:
            at = pl.ds(self.half_at, half)
            self.mine[at, :] = self.mine[at, :] + self.from_core[...]
        if stage == 1:
            at = pl.ds(self.a_at, quarter)
            self.mine[at, :] = (self.mine[at, :] + self.from_a[0]) + (self.from_a[1] + self.from_a[2])
        if stage == 2:
            at = pl.ds(self.b_at, piece)
            self.full[at, :] = (self.mine[at, :] + self.from_b[0]) + (self.from_b[1] + self.from_b[2])

    def step(self, stage):
        self.arrive(stage)
        self.start(stage + 1)


def project_kernel(
    len_ref, tid_ref, table_ref,
    x_hbm, gain_ref, wq_hbm, wk_hbm, wv_hbm, qd_hbm, vd_hbm, qu_hbm, vu_hbm,
    q_out, k_win, v_win,
    x, normed, w, base, qd, vd, qu, vu,
    mine_v, core_v, a_v, b_v, full_v,
    mine_q, core_q, a_q, b_q, full_q,
    cosine, sine, fold_v, got_v, fold_q, got_q, spread, k_own, v_own, q_own,
    ad_sem, x_sem, w_sem, sv, rv, sq, rq, z_send, z_recv, kv_send, kv_recv, own_sem,
):
    me = lax.axis_index("tok")
    z = lax.axis_index("mlp")
    core = lax.rem(me, 2)
    chip = me // 2
    px, py = lax.rem(chip, SIDE), chip // SIDE

    def tok_of(yy, xx, cc):
        return (yy * SIDE + xx) * 2 + cc

    sib = (me + 1 - 2 * core, z)
    ca = px * (1 - core) + py * core
    cb = py * (1 - core) + px * core
    peer_a, peer_b, peer_z = {}, {}, {}
    for k in range(1, SIDE):
        xk, yk = (px + k) % SIDE, (py + k) % SIDE
        along_x = tok_of(py, xk, core)
        along_y = tok_of(yk, px, core)
        peer_a[k] = (along_x * (1 - core) + along_y * core, z)
        peer_b[k] = (along_y * (1 - core) + along_x * core, z)
        peer_z[k] = (me, (z + k) % SIDE)
    ahead = ((me + 2) % N_TOK, z)
    behind = ((me + N_TOK - 2) % N_TOK, z)
    place = dict(core=core, ca=ca, cb=cb, sib=sib, peer_a=peer_a, peer_b=peer_b)

    barrier = pltpu.get_barrier_semaphore()
    greeted = [sib, ahead, behind] + [d[k] for d in (peer_a, peer_b, peer_z) for k in range(1, SIDE)]
    for dev in greeted:
        pl.semaphore_signal(barrier, inc=1, device_id=dev, device_id_type=MESH)

    loads = [
        pltpu.make_async_copy(src, dst, ad_sem.at[i])
        for i, (src, dst) in enumerate([(vd_hbm, vd), (vu_hbm, vu), (qd_hbm, qd), (qu_hbm, qu)])
    ]
    for c in loads:
        c.start()
    x_loads = [
        pltpu.make_async_copy(x_hbm.at[pl.ds(64 * i, 64)], x.at[pl.ds(64 * i, 64)], x_sem.at[i])
        for i in range(8)
    ]
    for c in x_loads:
        c.start()
    w_loads = [
        pltpu.make_async_copy(wk_hbm, w.at[0], w_sem.at[0]),
        pltpu.make_async_copy(wv_hbm, w.at[1], w_sem.at[1]),
    ] + [
        pltpu.make_async_copy(wq_hbm.at[:, pl.ds(256 * i, 256)], w.at[2 + i], w_sem.at[2 + i])
        for i in range(4)
    ]
    for c in w_loads:
        c.start()

    starts, ends = prompt_bounds(len_ref)
    for c in loads:
        c.wait()

    def gather(t, carry):
        local = table_ref[tid_ref[t]] - me * HELD
        held = jnp.logical_and(local >= 0, local < HELD)
        at = jnp.clip(local, 0, HELD - 1)

        def put(stored, target, first, slabs):
            for s in range(slabs):
                tile = stored[at, :, s * 128 : (s + 1) * 128]
                row = pl.multiple_of((first + s) * SLAB + t * RANK, RANK)
                target[pl.ds(row, RANK), :] = jnp.where(held, tile, jnp.zeros_like(tile))

        put(vd, mine_v, 0, 8)
        put(vu, mine_v, 8, 2)
        put(qd, mine_q, 0, 8)
        put(qu, mine_q, 8, 8)
        return carry

    lax.fori_loop(0, TENANTS, gather, 0)

    pl.semaphore_wait(barrier, len(greeted))
    red_v = AllReduce(place, V_ROWS, mine_v, core_v, a_v, b_v, full_v, sv, rv)
    red_q = AllReduce(place, Q_ROWS, mine_q, core_q, a_q, b_q, full_q, sq, rq)
    red_v.start(0)
    red_q.start(0)

    def angles(i, carry):
        row = pl.multiple_of(i * 64, 64)
        token = me * ROWS + row + lax.broadcasted_iota(jnp.int32, (64, HEAD), 0)
        begin = jnp.zeros((64, HEAD), jnp.int32)
        for t in range(TENANTS):
            begin = jnp.where(token >= starts[t], starts[t], begin)
        lane = lax.broadcasted_iota(jnp.int32, (64, HEAD), 1)
        pair = jnp.where(lane >= HEAD // 2, lane - HEAD // 2, lane)
        inverse = jnp.exp(-(pair.astype(F32) * (2.0 / HEAD)) * np.float32(np.log(np.float32(ROPE_BASE))))
        angle = (token - begin).astype(F32) * inverse
        cosine[pl.ds(row, 64), :] = jnp.cos(angle)
        s = jnp.sin(angle)
        sine[pl.ds(row, 64), :] = jnp.where(lane >= HEAD // 2, s, -s)
        return carry

    lax.fori_loop(0, 8, angles, 0)

    def normalise(first, count):
        def one(i, carry):
            at = pl.ds(pl.multiple_of(i * NORM_STEP, NORM_STEP), NORM_STEP)
            wide = x[at, :].astype(F32)
            scale = lax.rsqrt(jnp.mean(wide * wide, axis=1, keepdims=True) + NORM_EPS)
            normed[at, :] = (wide * scale * gain_ref[...]).astype(BF16)
            return carry

        lax.fori_loop(first, first + count, one, 0)

    for i in range(4):
        x_loads[i].wait()
    normalise(0, 8)
    red_v.step(0)
    for i in range(4, 8):
        x_loads[i].wait()
    normalise(8, 8)
    red_q.step(0)

    def rope(block):
        return block * cosine[...] + pltpu.roll(block, HEAD // 2, 1) * sine[...]

    def win_copy(win, which, slot):
        group = 4 * which
        send, recv = kv_send.at[group + slot], kv_recv.at[group + slot]
        if slot == 0:
            src, dst, dev = win.at[4], win.at[2], ahead
        elif slot == 1:
            src, dst, dev = win.at[2], win.at[0], ahead
        elif slot == 2:
            src, dst, dev = win.at[4 - 2 * core], win.at[3], sib
        else:
            src, dst, dev = win.at[2 - 2 * core], win.at[1], sib
        return pltpu.make_async_remote_copy(
            src_ref=src, dst_ref=dst, send_sem=send, recv_sem=recv, device_id=dev, device_id_type=MESH
        )

    def product(j):
        w_loads_j = pltpu.make_async_copy(wk_hbm, w.at[j], w_sem.at[j])
        w_loads_j.wait()
        base[j] = jnp.dot(normed[...], w[j], preferred_element_type=F32)

    def table(full, first, slabs):
        return jnp.concatenate([full[(first + s) * SLAB : (first + s + 1) * SLAB, :] for s in range(slabs)], axis=1)

    def members():
        token = me * ROWS + lax.broadcasted_iota(jnp.int32, (RANK, ROWS), 1)
        return [jnp.logical_and(token >= starts[t], token < ends[t]) for t in range(TENANTS)]

    def shrink(full, fold, got, which):
        some = normed[:, pl.ds(pl.multiple_of(z * 1024, 1024), 1024)]
        sums = lax.dot_general(table(full, 0, 8), some, (((1,), (1,)), ((), ())), preferred_element_type=F32)
        mask = members()
        total = jnp.zeros((RANK, ROWS), F32)
        for t in range(TENANTS):
            total = total + jnp.where(mask[t], sums[t * RANK : (t + 1) * RANK, :], 0.0)
        fold[...] = total
        for c in shrink_copies(fold, got, which):
            c.start()

    def shrink_copies(fold, got, which):
        return [
            pltpu.make_async_remote_copy(
                src_ref=fold, dst_ref=got.at[k - 1], send_sem=z_send.at[3 * which + k - 1],
                recv_sem=z_recv.at[3 * which + k - 1], device_id=peer_z[k], device_id_type=MESH,
            )
            for k in range(1, SIDE)
        ]

    def expand(fold, got, which):
        for c in shrink_copies(fold, got, which):
            c.wait()
        total = ((fold[...] + got[0]) + (got[1] + got[2])).astype(BF16).astype(F32)
        mask = members()
        for t in range(TENANTS):
            spread[t * RANK : (t + 1) * RANK, :] = jnp.where(mask[t], total, 0.0).astype(BF16)

    def work(j, carry):
        product(j)

        @pl.when(j == 0)
        def _():
            for h in range(2):
                cols = slice(h * HEAD, (h + 1) * HEAD)
                k_own[:, cols] = rope(base[0, :, cols]).astype(BF16)
            c = pltpu.make_async_copy(k_own, k_win.at[4], own_sem.at[0])
            c.start()
            c.wait()
            win_copy(k_win, 0, 0).start()
            red_v.step(1)

        @pl.when(j == 1)
        def _():
            red_v.step(2)
            red_q.step(1)

        @pl.when(j == 2)
        def _():
            red_v.step(3)
            red_q.step(2)

        @pl.when(j == 3)
        def _():
            red_v.step(4)
            red_q.step(3)
        return carry

    lax.fori_loop(0, 6, work, 0)

    red_v.arrive(5)
    shrink(full_v, fold_v, got_v, 0)
    red_q.step(4)
    win_copy(k_win, 0, 0).wait()
    win_copy(k_win, 0, 1).start()
    win_copy(k_win, 0, 2).start()
    expand(fold_v, got_v, 0)
    delta = lax.dot_general(spread[...], table(full_v, 8, 2), (((0,), (0,)), ((), ())), preferred_element_type=F32)
    v_own[...] = (base[1] + ADAPTER_SCALE * delta).astype(BF16)
    c = pltpu.make_async_copy(v_own, v_win.at[4], own_sem.at[1])
    c.start()
    c.wait()
    win_copy(v_win, 1, 0).start()

    red_q.arrive(5)
    shrink(full_q, fold_q, got_q, 1)
    win_copy(k_win, 0, 1).wait()
    win_copy(k_win, 0, 3).start()
    win_copy(v_win, 1, 0).wait()
    win_copy(v_win, 1, 1).start()
    win_copy(v_win, 1, 2).start()
    expand(fold_q, got_q, 1)

    def query(j, carry):
        up = jnp.concatenate(
            [full_q[pl.ds(pl.multiple_of((8 + 2 * j + s) * SLAB, SLAB), SLAB), :] for s in range(2)], axis=1
        )
        delta = lax.dot_general(spread[...], up, (((0,), (0,)), ((), ())), preferred_element_type=F32)
        rows = base[2 + j] + ADAPTER_SCALE * delta
        q_own[j] = jnp.concatenate([rope(rows[:, :HEAD]), rope(rows[:, HEAD:])], axis=1).astype(BF16)
        c = pltpu.make_async_copy(q_own.at[j], q_out.at[:, pl.ds(pl.multiple_of(j * 256, 256), 256)], own_sem.at[2 + j])
        c.start()
        return carry

    lax.fori_loop(0, 4, query, 0)
    for j in range(4):
        pltpu.make_async_copy(q_own.at[j], q_out.at[:, pl.ds(j * 256, 256)], own_sem.at[2 + j]).wait()
    win_copy(v_win, 1, 1).wait()
    win_copy(v_win, 1, 3).start()
    for s in (2, 3):
        win_copy(k_win, 0, s).wait()
    for s in (2, 3):
        win_copy(v_win, 1, s).wait()


def project(x, gain, wq, wk, wv, qd, vd, qu, vu, lengths, tid, slots):
    any_space = pl.BlockSpec(memory_space=pl.ANY)
    smem = pl.BlockSpec(memory_space=pltpu.SMEM)
    vmem = pl.BlockSpec(memory_space=pltpu.VMEM)
    dma = pltpu.SemaphoreType.DMA

    def reduce_scratch(rows):
        return [
            pltpu.VMEM((rows, 128), BF16),
            pltpu.VMEM((rows // 2, 128), BF16),
            pltpu.VMEM((3, rows // 8, 128), BF16),
            pltpu.VMEM((3, rows // 32, 128), BF16),
            pltpu.VMEM((rows, 128), BF16),
        ]

    return pl.pallas_call(
        project_kernel,
        out_shape=(
            jax.ShapeDtypeStruct((ROWS, QCOLS), BF16),
            jax.ShapeDtypeStruct((BACK + 1, ROWS, KVCOLS), BF16),
            jax.ShapeDtypeStruct((BACK + 1, ROWS, KVCOLS), BF16),
        ),
        in_specs=[smem] * 3 + [any_space, vmem] + [any_space] * 7,
        out_specs=(any_space, any_space, any_space),
        scratch_shapes=[
            pltpu.VMEM((ROWS, WIDTH), BF16),
            pltpu.VMEM((ROWS, WIDTH), BF16),
            pltpu.VMEM((6, WIDTH, 256), BF16),
            pltpu.VMEM((6, ROWS, 256), F32),
            pltpu.VMEM((HELD, RANK, 1024), BF16),
            pltpu.VMEM((HELD, RANK, 1024), BF16),
            pltpu.VMEM((HELD, RANK, QCOLS), BF16),
            pltpu.VMEM((HELD, RANK, KVCOLS), BF16),
        ]
        + reduce_scratch(V_ROWS)
        + reduce_scratch(Q_ROWS)
        + [
            pltpu.VMEM((ROWS, HEAD), F32),
            pltpu.VMEM((ROWS, HEAD), F32),
            pltpu.VMEM((RANK, ROWS), F32),
            pltpu.VMEM((3, RANK, ROWS), F32),
            pltpu.VMEM((RANK, ROWS), F32),
            pltpu.VMEM((3, RANK, ROWS), F32),
            pltpu.VMEM((SLAB, ROWS), BF16),
            pltpu.VMEM((ROWS, KVCOLS), BF16),
            pltpu.VMEM((ROWS, KVCOLS), BF16),
            pltpu.VMEM((4, ROWS, 256), BF16),
            dma((4,)), dma((8,)), dma((6,)),
            dma((COPIES,)), dma((COPIES,)), dma((COPIES,)), dma((COPIES,)),
            dma((6,)), dma((6,)), dma((8,)), dma((8,)), dma((6,)),
        ],
        compiler_params=pltpu.CompilerParams(
            collective_id=0, has_side_effects=True, vmem_limit_bytes=56 * 1024 * 1024
        ),
        name="project",
    )(lengths, tid, slots, x, gain, wq, wk, wv, qd, vd, qu, vu)


QT = 256
KC = 256


def attend_kernel(len_ref, q_ref, k_ref, v_ref, o_ref, m_ref, l_ref, acc_ref):
    me = lax.axis_index("tok")
    r = pl.program_id(1)
    first = me * ROWS + r * QT
    origin = (me - BACK) * ROWS
    starts, _ = prompt_bounds(len_ref)
    lowest = jnp.int32(0)
    token = first + lax.broadcasted_iota(jnp.int32, (QT, KC), 0)
    begin = jnp.zeros((QT, KC), jnp.int32)
    for t in range(TENANTS):
        lowest = jnp.where(first >= starts[t], starts[t], lowest)
        begin = jnp.where(token >= starts[t], starts[t], begin)
    end = BACK * ROWS + (r + 1) * QT
    need = end - (lowest - origin)
    chunks = (need + KC - 1) // KC
    q = jnp.concatenate([q_ref[:, h * HEAD : (h + 1) * HEAD] for h in range(4)], axis=0)
    m_ref[...] = jnp.full(m_ref.shape, -1e30, F32)
    l_ref[...] = jnp.zeros(l_ref.shape, F32)
    acc_ref[...] = jnp.zeros(acc_ref.shape, F32)
    scale = np.float32(HEAD ** -0.5 * np.log2(np.e))

    def one(i, carry):
        at = pl.multiple_of(end - (i + 1) * KC, KC)
        kk = k_ref[pl.ds(at, KC), :]
        vv = v_ref[pl.ds(at, KC), :]
        s = lax.dot_general(q, kk, (((1,), (1,)), ((), ())), preferred_element_type=F32) * scale
        kpos = origin + at + lax.broadcasted_iota(jnp.int32, (QT, KC), 1)
        seen = jnp.logical_and(kpos >= begin, kpos <= token)
        bias = jnp.where(seen, 0.0, -jnp.inf)
        s = (s.reshape(4, QT, KC) + bias[None]).reshape(4 * QT, KC)
        old = m_ref[...]
        new = jnp.maximum(old, jnp.max(s, axis=1, keepdims=True))
        p = jnp.exp2(s - new[:, :1])
        fade = jnp.exp2(old - new)
        m_ref[...] = new
        l_ref[...] = l_ref[...] * fade + jnp.sum(p, axis=1, keepdims=True)
        acc_ref[...] = acc_ref[...] * fade + jnp.dot(p.astype(BF16), vv, preferred_element_type=F32)
        return carry

    lax.fori_loop(0, chunks, one, 0)
    out = acc_ref[...] / l_ref[...]
    for h in range(4):
        o_ref[:, h * HEAD : (h + 1) * HEAD] = out[h * QT : (h + 1) * QT, :].astype(BF16)


def attend(lengths, q, k_win, v_win):
    span = (BACK + 1) * ROWS
    k2 = k_win.reshape(span, KVCOLS)
    v2 = v_win.reshape(span, KVCOLS)
    return pl.pallas_call(
        attend_kernel,
        out_shape=jax.ShapeDtypeStruct((ROWS, QCOLS), BF16),
        grid=(2, ROWS // QT),
        in_specs=[
            pl.BlockSpec(memory_space=pltpu.SMEM),
            pl.BlockSpec((QT, 512), lambda g, r: (r, g)),
            pl.BlockSpec((span, HEAD), lambda g, r: (0, g)),
            pl.BlockSpec((span, HEAD), lambda g, r: (0, g)),
        ],
        out_specs=pl.BlockSpec((QT, 512), lambda g, r: (r, g)),
        scratch_shapes=[pltpu.VMEM((4 * QT, HEAD), F32)] * 3,
        compiler_params=pltpu.CompilerParams(vmem_limit_bytes=48 * 1024 * 1024),
        name="attend",
    )(lengths, q, k2, v2)


def body(
    layer_input, input_norm_gain, query_weight, key_weight, value_weight,
    query_down_maps, value_down_maps, query_up_maps, value_up_maps,
    tenant_prompt_length, tenant_adapter_id, adapter_storage_slot,
):
    q, k_win, v_win = project(
        layer_input, input_norm_gain.reshape(1, WIDTH), query_weight, key_weight, value_weight,
        query_down_maps, value_down_maps, query_up_maps, value_up_maps,
        tenant_prompt_length, tenant_adapter_id, adapter_storage_slot,
    )
    return attend(tenant_prompt_length, q, k_win, v_win)


def solution(mesh):
    placed = (
        P("tok", None), P(), P(None, "mlp"), P(None, "mlp"), P(None, "mlp"),
        P("tok", None, "mlp"), P("tok", None, "mlp"), P("tok", None, "mlp"), P("tok", None, "mlp"),
        P(), P(), P(),
    )
    return jax.shard_map(
        body, mesh=mesh, in_specs=placed, out_specs=P("tok", "mlp"), check_vma=False
    )
```

```python
import functools

import jax
import jax.numpy as jnp
import numpy as np
from jax import lax
from jax.experimental import pallas as pl
from jax.experimental.pallas import tpu as pltpu
from jax.sharding import PartitionSpec as P

WIDTH = 4096
HEAD = 128
RANK = 16
TENANTS = 16
ROWS = 512
HELD = 8
QCOLS = 1024
KVCOLS = 256
BACK = 4
N_TOK = 32
SIDE = 4
NORM_EPS = 1e-05
ROPE_BASE = 500000.0
ADAPTER_SCALE = 0.5
MESH = pl.DeviceIdType.MESH
F32 = jnp.float32
BF16 = jnp.bfloat16
SLAB = TENANTS * RANK
V_ROWS = (1024 + KVCOLS) // 128 * SLAB
Q_ROWS = (1024 + QCOLS) // 128 * SLAB
NORM_STEP = 32
SPAN = (BACK + 1) * ROWS
FAR = 1e30
QT = 256
KC = 1152
CHUNKS = (BACK * ROWS + QT) // KC
COPIES = 14


def prompt_bounds(len_ref):
    starts, ends = [], []
    at = jnp.int32(0)
    for t in range(TENANTS):
        starts.append(at)
        at = at + len_ref[t]
        ends.append(at)
    return starts, ends


class AllReduce:
    def __init__(self, place, rows, mine, from_core, from_a, from_b, full, send, recv):
        self.place, self.rows = place, rows
        self.mine, self.from_core, self.from_a, self.from_b = mine, from_core, from_a, from_b
        self.full, self.send, self.recv = full, send, recv
        p = place
        half, quarter, piece = rows // 2, rows // 8, rows // 32
        self.half_at = pl.multiple_of(p["core"] * half, 16)
        self.other_at = pl.multiple_of((1 - p["core"]) * half, 16)
        self.a_at = pl.multiple_of(p["core"] * half + p["ca"] * quarter, 16)
        self.b_at = pl.multiple_of(p["core"] * half + p["ca"] * quarter + p["cb"] * piece, 16)

    def copy(self, slot, src, dst, dev):
        return pltpu.make_async_remote_copy(
            src_ref=src, dst_ref=dst, send_sem=self.send.at[slot], recv_sem=self.recv.at[slot],
            device_id=dev, device_id_type=MESH,
        )

    def copies(self, stage):
        p = self.place
        half, quarter, piece = self.rows // 2, self.rows // 8, self.rows // 32
        if stage == 0:
            return [self.copy(0, self.mine.at[pl.ds(self.other_at, half)], self.from_core, p["sib"])]
        if stage == 5:
            ref = self.full.at[pl.ds(self.half_at, half)]
            return [self.copy(13, ref, ref, p["sib"])]
        out = []
        for k in range(1, SIDE):
            a, b = (p["ca"] + k) % SIDE, (p["cb"] + k) % SIDE
            if stage == 1:
                at = pl.multiple_of(p["core"] * half + a * quarter, 16)
                out.append(self.copy(k, self.mine.at[pl.ds(at, quarter)], self.from_a.at[k - 1], p["peer_a"][k]))
            if stage == 2:
                at = pl.multiple_of(p["core"] * half + p["ca"] * quarter + b * piece, 16)
                out.append(self.copy(3 + k, self.mine.at[pl.ds(at, piece)], self.from_b.at[k - 1], p["peer_b"][k]))
            if stage == 3:
                ref = self.full.at[pl.ds(self.b_at, piece)]
                out.append(self.copy(6 + k, ref, ref, p["peer_b"][k]))
            if stage == 4:
                ref = self.full.at[pl.ds(self.a_at, quarter)]
                out.append(self.copy(9 + k, ref, ref, p["peer_a"][k]))
        return out

    def start(self, stage):
        for c in self.copies(stage):
            c.start()

    def arrive(self, stage):
        for c in self.copies(stage):
            c.wait()
        half, quarter, piece = self.rows // 2, self.rows // 8, self.rows // 32
        if stage == 0:
            at = pl.ds(self.half_at, half)
            self.mine[at, :] = self.mine[at, :] + self.from_core[...]
        if stage == 1:
            at = pl.ds(self.a_at, quarter)
            self.mine[at, :] = (self.mine[at, :] + self.from_a[0]) + (self.from_a[1] + self.from_a[2])
        if stage == 2:
            at = pl.ds(self.b_at, piece)
            self.full[at, :] = (self.mine[at, :] + self.from_b[0]) + (self.from_b[1] + self.from_b[2])

    def step(self, stage):
        self.arrive(stage)
        self.start(stage + 1)


def block_kernel(
    len_ref, tid_ref, table_ref,
    x_hbm, gain_ref, wq_hbm, wk_hbm, wv_hbm, qd_hbm, vd_hbm, qu_hbm, vu_hbm,
    out,
    x, normed, w, base, qd, vd, qu, vu,
    mine_v, core_v, a_v, b_v, full_v,
    mine_q, core_q, a_q, b_q, full_q,
    cosine, sine, fold_v, got_v, fold_q, got_q, spread, k_win, v_win, q_own,
    q_mark, k_mark, marked, scores, highest, peak, sums, mixed,
    ad_sem, x_sem, w_sem, sv, rv, sq, rq, z_send, z_recv, kv_send, kv_recv,
):
    me = lax.axis_index("tok")
    z = lax.axis_index("mlp")
    core = lax.rem(me, 2)
    chip = me // 2
    px, py = lax.rem(chip, SIDE), chip // SIDE

    def tok_of(yy, xx, cc):
        return (yy * SIDE + xx) * 2 + cc

    sib = (me + 1 - 2 * core, z)
    ca = px * (1 - core) + py * core
    cb = py * (1 - core) + px * core
    peer_a, peer_b, peer_z = {}, {}, {}
    for k in range(1, SIDE):
        xk, yk = (px + k) % SIDE, (py + k) % SIDE
        along_x = tok_of(py, xk, core)
        along_y = tok_of(yk, px, core)
        peer_a[k] = (along_x * (1 - core) + along_y * core, z)
        peer_b[k] = (along_y * (1 - core) + along_x * core, z)
        peer_z[k] = (me, (z + k) % SIDE)
    ahead = ((me + 2) % N_TOK, z)
    behind = ((me + N_TOK - 2) % N_TOK, z)
    place = dict(core=core, ca=ca, cb=cb, sib=sib, peer_a=peer_a, peer_b=peer_b)

    barrier = pltpu.get_barrier_semaphore()
    greeted = [sib, ahead, behind] + [d[k] for d in (peer_a, peer_b, peer_z) for k in range(1, SIDE)]
    for dev in greeted:
        pl.semaphore_signal(barrier, inc=1, device_id=dev, device_id_type=MESH)

    loads = [
        pltpu.make_async_copy(src, dst, ad_sem.at[i])
        for i, (src, dst) in enumerate([(vd_hbm, vd), (vu_hbm, vu), (qd_hbm, qd), (qu_hbm, qu)])
    ]
    for c in loads:
        c.start()
    x_loads = [
        pltpu.make_async_copy(x_hbm.at[pl.ds(64 * i, 64)], x.at[pl.ds(64 * i, 64)], x_sem.at[i])
        for i in range(8)
    ]
    for c in x_loads:
        c.start()
    w_loads = [
        pltpu.make_async_copy(wk_hbm, w.at[0], w_sem.at[0]),
        pltpu.make_async_copy(wv_hbm, w.at[1], w_sem.at[1]),
    ] + [
        pltpu.make_async_copy(wq_hbm.at[:, pl.ds(256 * i, 256)], w.at[2 + i], w_sem.at[2 + i])
        for i in range(4)
    ]
    for c in w_loads:
        c.start()

    starts, ends = prompt_bounds(len_ref)
    for c in loads:
        c.wait()

    def gather(t, carry):
        local = table_ref[tid_ref[t]] - me * HELD
        held = jnp.logical_and(local >= 0, local < HELD)
        at = jnp.clip(local, 0, HELD - 1)

        def put(stored, target, first, slabs):
            for s in range(slabs):
                tile = stored[at, :, s * 128 : (s + 1) * 128]
                row = pl.multiple_of((first + s) * SLAB + t * RANK, RANK)
                target[pl.ds(row, RANK), :] = jnp.where(held, tile, jnp.zeros_like(tile))

        put(vd, mine_v, 0, 8)
        put(vu, mine_v, 8, 2)
        put(qd, mine_q, 0, 8)
        put(qu, mine_q, 8, 8)
        return carry

    lax.fori_loop(0, TENANTS, gather, 0)

    pl.semaphore_wait(barrier, len(greeted))
    red_v = AllReduce(place, V_ROWS, mine_v, core_v, a_v, b_v, full_v, sv, rv)
    red_q = AllReduce(place, Q_ROWS, mine_q, core_q, a_q, b_q, full_q, sq, rq)
    red_v.start(0)
    red_q.start(0)

    marks(starts, ends, me, q_mark, k_mark)

    def angles(i, carry):
        row = pl.multiple_of(i * 64, 64)
        token = me * ROWS + row + lax.broadcasted_iota(jnp.int32, (64, HEAD), 0)
        begin = jnp.zeros((64, HEAD), jnp.int32)
        for t in range(TENANTS):
            begin = jnp.where(token >= starts[t], starts[t], begin)
        lane = lax.broadcasted_iota(jnp.int32, (64, HEAD), 1)
        pair = jnp.where(lane >= HEAD // 2, lane - HEAD // 2, lane)
        inverse = jnp.exp(-(pair.astype(F32) * (2.0 / HEAD)) * np.float32(np.log(np.float32(ROPE_BASE))))
        angle = (token - begin).astype(F32) * inverse
        cosine[pl.ds(row, 64), :] = jnp.cos(angle)
        s = jnp.sin(angle)
        sine[pl.ds(row, 64), :] = jnp.where(lane >= HEAD // 2, s, -s)
        return carry

    lax.fori_loop(0, 8, angles, 0)

    def normalise(first, count):
        def one(i, carry):
            at = pl.ds(pl.multiple_of(i * NORM_STEP, NORM_STEP), NORM_STEP)
            wide = x[at, :].astype(F32)
            scale = lax.rsqrt(jnp.mean(wide * wide, axis=1, keepdims=True) + NORM_EPS)
            normed[at, :] = (wide * scale * gain_ref[...]).astype(BF16)
            return carry

        lax.fori_loop(first, first + count, one, 0)

    for i in range(4):
        x_loads[i].wait()
    normalise(0, 8)
    red_v.step(0)
    for i in range(4, 8):
        x_loads[i].wait()
    normalise(8, 8)
    red_q.step(0)

    def rope(block):
        return block * cosine[...] + pltpu.roll(block, HEAD // 2, 1) * sine[...]

    def block(win, i):
        return win.at[pl.ds(pl.multiple_of(i * ROWS, ROWS), ROWS)]

    def win_copy(win, which, slot):
        group = 4 * which
        send, recv = kv_send.at[group + slot], kv_recv.at[group + slot]
        if slot == 0:
            src, dst, dev = block(win, 4), block(win, 2), ahead
        elif slot == 1:
            src, dst, dev = block(win, 2), block(win, 0), ahead
        elif slot == 2:
            src, dst, dev = block(win, 4 - 2 * core), block(win, 3), sib
        else:
            src, dst, dev = block(win, 2 - 2 * core), block(win, 1), sib
        return pltpu.make_async_remote_copy(
            src_ref=src, dst_ref=dst, send_sem=send, recv_sem=recv, device_id=dev, device_id_type=MESH
        )

    def product(j):
        w_loads_j = pltpu.make_async_copy(wk_hbm, w.at[j], w_sem.at[j])
        w_loads_j.wait()
        base[j] = jnp.dot(normed[...], w[j], preferred_element_type=F32)

    def table(full, first, slabs):
        return jnp.concatenate([full[(first + s) * SLAB : (first + s + 1) * SLAB, :] for s in range(slabs)], axis=1)

    def members():
        token = me * ROWS + lax.broadcasted_iota(jnp.int32, (RANK, ROWS), 1)
        return [jnp.logical_and(token >= starts[t], token < ends[t]) for t in range(TENANTS)]

    def shrink(full, fold, got, which):
        some = normed[:, pl.ds(pl.multiple_of(z * 1024, 1024), 1024)]
        sums = lax.dot_general(table(full, 0, 8), some, (((1,), (1,)), ((), ())), preferred_element_type=F32)
        mask = members()
        total = jnp.zeros((RANK, ROWS), F32)
        for t in range(TENANTS):
            total = total + jnp.where(mask[t], sums[t * RANK : (t + 1) * RANK, :], 0.0)
        fold[...] = total
        for c in shrink_copies(fold, got, which):
            c.start()

    def shrink_copies(fold, got, which):
        return [
            pltpu.make_async_remote_copy(
                src_ref=fold, dst_ref=got.at[k - 1], send_sem=z_send.at[3 * which + k - 1],
                recv_sem=z_recv.at[3 * which + k - 1], device_id=peer_z[k], device_id_type=MESH,
            )
            for k in range(1, SIDE)
        ]

    def expand(fold, got, which):
        for c in shrink_copies(fold, got, which):
            c.wait()
        total = ((fold[...] + got[0]) + (got[1] + got[2])).astype(BF16).astype(F32)
        mask = members()
        for t in range(TENANTS):
            spread[t * RANK : (t + 1) * RANK, :] = jnp.where(mask[t], total, 0.0).astype(BF16)

    def work(j, carry):
        product(j)

        @pl.when(j == 0)
        def _():
            for h in range(2):
                cols = slice(h * HEAD, (h + 1) * HEAD)
                k_win[BACK * ROWS :, cols] = rope(base[0, :, cols]).astype(BF16)
            win_copy(k_win, 0, 0).start()
            red_v.step(1)

        @pl.when(j == 1)
        def _():
            red_v.step(2)
            red_q.step(1)

        @pl.when(j == 2)
        def _():
            red_v.step(3)
            red_q.step(2)

        @pl.when(j == 3)
        def _():
            red_v.step(4)
            red_q.step(3)
        return carry

    lax.fori_loop(0, 6, work, 0)

    red_v.arrive(5)
    shrink(full_v, fold_v, got_v, 0)
    red_q.step(4)
    win_copy(k_win, 0, 0).wait()
    win_copy(k_win, 0, 1).start()
    win_copy(k_win, 0, 2).start()
    expand(fold_v, got_v, 0)
    delta = lax.dot_general(spread[...], table(full_v, 8, 2), (((0,), (0,)), ((), ())), preferred_element_type=F32)
    v_win[BACK * ROWS :, :] = (base[1] + ADAPTER_SCALE * delta).astype(BF16)
    win_copy(v_win, 1, 0).start()

    red_q.arrive(5)
    shrink(full_q, fold_q, got_q, 1)
    win_copy(k_win, 0, 1).wait()
    win_copy(k_win, 0, 3).start()
    win_copy(v_win, 1, 0).wait()
    win_copy(v_win, 1, 1).start()
    win_copy(v_win, 1, 2).start()
    expand(fold_q, got_q, 1)

    def query(j, carry):
        up = jnp.concatenate(
            [full_q[pl.ds(pl.multiple_of((8 + 2 * j + s) * SLAB, SLAB), SLAB), :] for s in range(2)], axis=1
        )
        delta = lax.dot_general(spread[...], up, (((0,), (0,)), ((), ())), preferred_element_type=F32)
        rows = base[2 + j] + ADAPTER_SCALE * delta
        q_own[j] = jnp.concatenate([rope(rows[:, :HEAD]), rope(rows[:, HEAD:])], axis=1).astype(BF16)
        return carry

    lax.fori_loop(0, 4, query, 0)
    win_copy(v_win, 1, 1).wait()
    win_copy(v_win, 1, 3).start()
    for s in (2, 3):
        win_copy(k_win, 0, s).wait()
    for s in (2, 3):
        win_copy(v_win, 1, s).wait()
    attention(me, starts, ends, q_own, k_win, v_win, out, q_mark, k_mark, marked, scores, highest, peak, sums, mixed)


def marks(starts, ends, me, q_mark, k_mark):
    lane = lax.broadcasted_iota(jnp.int32, (1, HEAD), 1)
    begin = jnp.full((1, HEAD), 2**30, jnp.int32)
    end = jnp.full((1, HEAD), 2**30, jnp.int32)
    for t in range(TENANTS):
        begin = jnp.where(lane == t, starts[t], begin)
        end = jnp.where(lane == t, ends[t], end)
    begin = jnp.where(lane == TENANTS, -(2**30), begin)
    end = jnp.where(lane == TENANTS, 0, end)

    def inside(first, row):
        token = first + row + lax.broadcasted_iota(jnp.int32, (128, HEAD), 0)
        return jnp.logical_and(token >= begin, token < end)

    def keys(i, carry):
        row = pl.multiple_of(i * 128, 128)
        k_mark[pl.ds(row, 128), :] = jnp.where(inside((me - BACK) * ROWS, row), 1.0, 0.0).astype(BF16)
        return carry

    lax.fori_loop(0, SPAN // 128, keys, 0)

    def queries(i, carry):
        row = pl.multiple_of(i * 128, 128)
        open_to = jnp.logical_or(inside(me * ROWS, row), lane > TENANTS)
        q_mark[pl.ds(row, 128), :] = jnp.where(open_to, 0.0, -FAR).astype(BF16)
        return carry

    lax.fori_loop(0, ROWS // 128, queries, 0)


def attention(me, starts, ends, q_ref, k_win, v_win, out, q_mark, k_mark, marked, scores, highest, peak, sums, mixed):
    scale = np.float32(HEAD**-0.5 * np.log2(np.e))

    def unit(u, carry):
        group, part = u // 2, lax.rem(u, 2)
        rows = pl.ds(pl.multiple_of(part * QT, QT), QT)
        head_cols = pl.ds(pl.multiple_of(group * HEAD, HEAD), HEAD)
        for h in range(4):
            marked[h * QT : (h + 1) * QT, :HEAD] = q_ref[
                2 * group + h // 2, rows, (h % 2) * HEAD : (h % 2 + 1) * HEAD
            ]
            marked[h * QT : (h + 1) * QT, HEAD:] = q_mark[rows, :]
        for i in range(CHUNKS):
            at = pl.multiple_of(part * QT + i * KC, 128)
            keys = jnp.concatenate([k_win[pl.ds(at, KC), head_cols], k_mark[pl.ds(at, KC), :]], axis=1)
            s = lax.dot_general(marked[...], keys, (((1,), (1,)), ((), ())), preferred_element_type=F32)
            if i == CHUNKS - 1:
                seen = lax.broadcasted_iota(jnp.int32, (QT, QT), 0) >= lax.broadcasted_iota(jnp.int32, (QT, QT), 1)
                tail = s[:, KC - QT :]
                tail = jnp.concatenate(
                    [jnp.where(seen, tail[h * QT : (h + 1) * QT, :], -FAR) for h in range(4)], axis=0
                )
                s = jnp.concatenate([s[:, : KC - QT], tail], axis=1)
            scores[i] = s
            top = s[:, :128]
            for c in range(1, KC // 128):
                top = jnp.maximum(top, s[:, c * 128 : (c + 1) * 128])
            highest[...] = top if i == 0 else jnp.maximum(highest[...], top)
        peak[...] = jnp.broadcast_to(jnp.max(highest[...], axis=1, keepdims=True) * scale, peak.shape)
        for i in range(CHUNKS):
            at = pl.multiple_of(part * QT + i * KC, 128)
            s = scores[i]
            ps = [jnp.exp2(s[:, c * 128 : (c + 1) * 128] * scale - peak[...]) for c in range(KC // 128)]
            total = ps[0]
            for p in ps[1:]:
                total = total + p
            probs = jnp.concatenate([p.astype(BF16) for p in ps], axis=1)
            mix = jnp.dot(probs, v_win[pl.ds(at, KC), head_cols], preferred_element_type=F32)
            sums[...] = total if i == 0 else sums[...] + total
            mixed[...] = mix if i == 0 else mixed[...] + mix
        result = mixed[...] / jnp.sum(sums[...], axis=1, keepdims=True)
        for h in range(4):
            cols = pl.ds(pl.multiple_of(group * 512 + h * HEAD, HEAD), HEAD)
            out[rows, cols] = result[h * QT : (h + 1) * QT, :].astype(BF16)
        return carry

    lax.fori_loop(0, 4, unit, 0)


def block(x, gain, wq, wk, wv, qd, vd, qu, vu, lengths, tid, slots):
    any_space = pl.BlockSpec(memory_space=pl.ANY)
    smem = pl.BlockSpec(memory_space=pltpu.SMEM)
    vmem = pl.BlockSpec(memory_space=pltpu.VMEM)
    dma = pltpu.SemaphoreType.DMA

    def reduce_scratch(rows):
        return [
            pltpu.VMEM((rows, 128), BF16),
            pltpu.VMEM((rows // 2, 128), BF16),
            pltpu.VMEM((3, rows // 8, 128), BF16),
            pltpu.VMEM((3, rows // 32, 128), BF16),
            pltpu.VMEM((rows, 128), BF16),
        ]

    return pl.pallas_call(
        block_kernel,
        out_shape=jax.ShapeDtypeStruct((ROWS, QCOLS), BF16),
        in_specs=[smem] * 3 + [any_space, vmem] + [any_space] * 7,
        out_specs=vmem,
        scratch_shapes=[
            pltpu.VMEM((ROWS, WIDTH), BF16),
            pltpu.VMEM((ROWS, WIDTH), BF16),
            pltpu.VMEM((6, WIDTH, 256), BF16),
            pltpu.VMEM((6, ROWS, 256), F32),
            pltpu.VMEM((HELD, RANK, 1024), BF16),
            pltpu.VMEM((HELD, RANK, 1024), BF16),
            pltpu.VMEM((HELD, RANK, QCOLS), BF16),
            pltpu.VMEM((HELD, RANK, KVCOLS), BF16),
        ]
        + reduce_scratch(V_ROWS)
        + reduce_scratch(Q_ROWS)
        + [
            pltpu.VMEM((ROWS, HEAD), F32),
            pltpu.VMEM((ROWS, HEAD), F32),
            pltpu.VMEM((RANK, ROWS), F32),
            pltpu.VMEM((3, RANK, ROWS), F32),
            pltpu.VMEM((RANK, ROWS), F32),
            pltpu.VMEM((3, RANK, ROWS), F32),
            pltpu.VMEM((SLAB, ROWS), BF16),
            pltpu.VMEM((SPAN, KVCOLS), BF16),
            pltpu.VMEM((SPAN, KVCOLS), BF16),
            pltpu.VMEM((4, ROWS, 256), BF16),
            pltpu.VMEM((ROWS, HEAD), BF16),
            pltpu.VMEM((SPAN, HEAD), BF16),
            pltpu.VMEM((4 * QT, 2 * HEAD), BF16),
            pltpu.VMEM((CHUNKS, 4 * QT, KC), F32),
        ]
        + [pltpu.VMEM((4 * QT, HEAD), F32)] * 4
        + [
            dma((4,)), dma((8,)), dma((6,)),
            dma((COPIES,)), dma((COPIES,)), dma((COPIES,)), dma((COPIES,)),
            dma((6,)), dma((6,)), dma((8,)), dma((8,)),
        ],
        compiler_params=pltpu.CompilerParams(
            collective_id=0, has_side_effects=True, vmem_limit_bytes=60 * 1024 * 1024
        ),
        name="block",
    )(lengths, tid, slots, x, gain, wq, wk, wv, qd, vd, qu, vu)


def body(
    layer_input, input_norm_gain, query_weight, key_weight, value_weight,
    query_down_maps, value_down_maps, query_up_maps, value_up_maps,
    tenant_prompt_length, tenant_adapter_id, adapter_storage_slot,
):
    return block(
        layer_input, input_norm_gain.reshape(1, WIDTH), query_weight, key_weight, value_weight,
        query_down_maps, value_down_maps, query_up_maps, value_up_maps,
        tenant_prompt_length, tenant_adapter_id, adapter_storage_slot,
    )


def solution(mesh):
    placed = (
        P("tok", None), P(), P(None, "mlp"), P(None, "mlp"), P(None, "mlp"),
        P("tok", None, "mlp"), P("tok", None, "mlp"), P("tok", None, "mlp"), P("tok", None, "mlp"),
        P(), P(), P(),
    )
    return jax.shard_map(
        body, mesh=mesh, in_specs=placed, out_specs=P("tok", "mlp"), check_vma=False
    )
```

```python
import functools

import jax
import jax.numpy as jnp
import numpy as np
from jax import lax
from jax.experimental import pallas as pl
from jax.experimental.pallas import tpu as pltpu
from jax.sharding import PartitionSpec as P

WIDTH = 4096
HEAD = 128
RANK = 16
TENANTS = 16
ROWS = 512
HELD = 8
QCOLS = 1024
KVCOLS = 256
BACK = 4
N_TOK = 32
SIDE = 4
NORM_EPS = 1e-05
ROPE_BASE = 500000.0
ADAPTER_SCALE = 0.5
MESH = pl.DeviceIdType.MESH
F32 = jnp.float32
BF16 = jnp.bfloat16
SLAB = TENANTS * RANK
DOWN_ROWS = 2 * 1024 // 128 * SLAB
UP_ROWS = (QCOLS + KVCOLS) // 128 * SLAB
AHEAD = 3
NORM_STEP = 32
SPAN = (BACK + 1) * ROWS
FAR = 1e30
QT = 256
KC = 1152
CHUNKS = (BACK * ROWS + QT) // KC
UNITS = 4
SCALE = np.float32(HEAD**-0.5 * np.log2(np.e))
COPIES = 11
PARTS = 4


def prompt_bounds(len_ref):
    starts, ends = [], []
    at = jnp.int32(0)
    for t in range(TENANTS):
        starts.append(at)
        at = at + len_ref[t]
        ends.append(at)
    return starts, ends


class AllReduce:
    def __init__(self, place, rows, mine, from_core, from_a, from_b, full, send, recv):
        self.place, self.rows = place, rows
        self.mine, self.from_core, self.from_a, self.from_b = mine, from_core, from_a, from_b
        self.full, self.send, self.recv = full, send, recv
        p = place
        half, quarter = rows // 2, rows // 8
        self.half_at = pl.multiple_of(p["core"] * half, 16)
        self.other_at = pl.multiple_of((1 - p["core"]) * half, 16)
        self.a_at = pl.multiple_of(p["core"] * half + p["ca"] * quarter, 16)

    def copy(self, slot, src, dst, dev):
        return pltpu.make_async_remote_copy(
            src_ref=src, dst_ref=dst, send_sem=self.send.at[slot], recv_sem=self.recv.at[slot],
            device_id=dev, device_id_type=MESH,
        )

    def copies(self, stage):
        p = self.place
        half, quarter = self.rows // 2, self.rows // 8
        if stage == 0:
            return [self.copy(0, self.mine.at[pl.ds(self.other_at, half)], self.from_core, p["sib"])]
        if stage == 4:
            ref = self.full.at[pl.ds(self.half_at, half)]
            return [self.copy(10, ref, ref, p["sib"])]
        out = []
        for k in range(1, SIDE):
            if stage == 1:
                a = (p["ca"] + k) % SIDE
                at = pl.multiple_of(p["core"] * half + a * quarter, 16)
                out.append(self.copy(k, self.mine.at[pl.ds(at, quarter)], self.from_a.at[k - 1], p["peer_a"][k]))
            if stage == 2:
                ref = self.mine.at[pl.ds(self.a_at, quarter)]
                out.append(self.copy(3 + k, ref, self.from_b.at[k - 1], p["peer_b"][k]))
            if stage == 3:
                ref = self.full.at[pl.ds(self.a_at, quarter)]
                out.append(self.copy(6 + k, ref, ref, p["peer_a"][k]))
        return out

    def start(self, stage):
        for c in self.copies(stage):
            c.start()

    def arrive(self, stage):
        for c in self.copies(stage):
            c.wait()
        half, quarter = self.rows // 2, self.rows // 8
        if stage == 0:
            at = pl.ds(self.half_at, half)
            self.mine[at, :] = self.mine[at, :] + self.from_core[...]
        if stage == 1:
            at = pl.ds(self.a_at, quarter)
            self.mine[at, :] = (self.mine[at, :] + self.from_a[0]) + (self.from_a[1] + self.from_a[2])
        if stage == 2:
            at = pl.ds(self.a_at, quarter)
            self.full[at, :] = (self.mine[at, :] + self.from_b[0]) + (self.from_b[1] + self.from_b[2])

    def step(self, stage):
        self.arrive(stage)
        self.start(stage + 1)


def block_kernel(
    len_ref, tid_ref, table_ref,
    x_hbm, gain_ref, wq_hbm, wk_hbm, wv_hbm, qd_hbm, vd_hbm, qu_hbm, vu_hbm,
    out,
    base, quarter,
    mine_d, core_d, a_d, b_d, down,
    mine_u, core_u, a_u, b_u, up,
    cosine, sine, fold, got, shrunk_v, spread, k_win, v_win, passing, q_own,
    q_mark, k_mark, marked, highest, peak, sums, mixed,
    ad_sem, x_sem, w_sem, sd, rd, su, ru, z_send, z_recv, kv_send, kv_recv, pass_send, pass_recv, share_send, share_recv, s_send, s_recv,
):
    me = lax.axis_index("tok")
    z = lax.axis_index("mlp")
    core = lax.rem(me, 2)
    chip = me // 2
    px, py = lax.rem(chip, SIDE), chip // SIDE

    def tok_of(yy, xx, cc):
        return (yy * SIDE + xx) * 2 + cc

    sib = (me + 1 - 2 * core, z)
    x_first = 1 - core
    ca = px * x_first + py * (1 - x_first)
    cb = py * x_first + px * (1 - x_first)
    peer_a, peer_b, peer_z = {}, {}, {}
    for k in range(1, SIDE):
        xk, yk = (px + k) % SIDE, (py + k) % SIDE
        along_x = tok_of(py, xk, core)
        along_y = tok_of(yk, px, core)
        peer_a[k] = (along_x * x_first + along_y * (1 - x_first), z)
        peer_b[k] = (along_y * x_first + along_x * (1 - x_first), z)
        peer_z[k] = (me, (z + k) % SIDE)
    later = {k: ((me + k) % N_TOK, z) for k in range(1, BACK + 1)}
    earlier = {k: ((me + N_TOK - k) % N_TOK, z) for k in range(1, BACK + 1)}
    place = dict(core=core, ca=ca, cb=cb, sib=sib, peer_a=peer_a, peer_b=peer_b)

    barrier = pltpu.get_barrier_semaphore()
    over = (tok_of((py + px // 2) % SIDE, (px + 3) % SIDE, core), z)
    goal = (tok_of(py, (px + 3) % SIDE, core), z)
    under_x = (px + 1) % SIDE
    under = (tok_of((py + SIDE - under_x // 2) % SIDE, under_x, core), z)
    greeted = [sib, over, under] + [d[k] for d in (peer_a, peer_b, peer_z) for k in range(1, SIDE)]
    greeted += [d[k] for d in (later, earlier) for k in range(1, BACK + 1)]
    for dev in greeted:
        pl.semaphore_signal(barrier, inc=1, device_id=dev, device_id_type=MESH)

    starts, ends = prompt_bounds(len_ref)
    red_d = AllReduce(place, DOWN_ROWS, mine_d, core_d, a_d, b_d, down, sd, rd)
    red_u = AllReduce(place, UP_ROWS, mine_u, core_u, a_u, b_u, up, su, ru)

    def angles(i, carry):
        row = pl.multiple_of(i * 64, 64)
        token = me * ROWS + row + lax.broadcasted_iota(jnp.int32, (64, HEAD), 0)
        begin = jnp.zeros((64, HEAD), jnp.int32)
        for t in range(TENANTS):
            begin = jnp.where(token >= starts[t], starts[t], begin)
        lane = lax.broadcasted_iota(jnp.int32, (64, HEAD), 1)
        pair = jnp.where(lane >= HEAD // 2, lane - HEAD // 2, lane)
        inverse = jnp.exp(-(pair.astype(F32) * (2.0 / HEAD)) * np.float32(np.log(np.float32(ROPE_BASE))))
        angle = (token - begin).astype(F32) * inverse
        cosine[pl.ds(row, 64), :] = jnp.cos(angle)
        s = jnp.sin(angle)
        sine[pl.ds(row, 64), :] = jnp.where(lane >= HEAD // 2, s, -s)
        return carry


    def rope(block):
        return block * cosine[...] + pltpu.roll(block, HEAD // 2, 1) * sine[...]

    def rows_of(win, block, part, parts):
        size = ROWS // parts
        return win.at[pl.ds(pl.multiple_of(block * ROWS + part * size, size), size)]

    def win_copy(win, which, slot, part):
        at = (2 * which + slot) * PARTS + part
        if which == 0 or slot == 0:
            src, dst = rows_of(win, BACK - 2 * slot, part, PARTS), rows_of(win, 2 - 2 * slot, part, PARTS)
            dev = later[2]
        else:
            src, dst = rows_of(passing, 0, part, PARTS), rows_of(win, 0, part, PARTS)
            dev = goal
        return pltpu.make_async_remote_copy(
            src_ref=src, dst_ref=dst, send_sem=kv_send.at[at], recv_sem=kv_recv.at[at],
            device_id=dev, device_id_type=MESH,
        )

    def pass_copy(part):
        return pltpu.make_async_remote_copy(
            src_ref=rows_of(v_win, BACK, part, PARTS), dst_ref=rows_of(passing, 0, part, PARTS),
            send_sem=pass_send.at[part], recv_sem=pass_recv.at[part], device_id=over, device_id_type=MESH,
        )

    def share_copy(win, which, slot):
        src, dst = (4 - 2 * core, 3) if slot == 0 else (2 - 2 * core, 1)
        at = 2 * which + slot
        return pltpu.make_async_remote_copy(
            src_ref=rows_of(win, src, 0, 1), dst_ref=rows_of(win, dst, 0, 1),
            send_sem=share_send.at[at], recv_sem=share_recv.at[at], device_id=sib, device_id_type=MESH,
        )

    def table(full, first, slabs):
        return jnp.concatenate([full[(first + s) * SLAB : (first + s + 1) * SLAB, :] for s in range(slabs)], axis=1)

    def members(first):
        token = first + lax.broadcasted_iota(jnp.int32, (RANK, ROWS), 1)
        return [jnp.logical_and(token >= starts[t], token < ends[t]) for t in range(TENANTS)]

    def z_copies():
        return [
            pltpu.make_async_remote_copy(
                src_ref=fold, dst_ref=got.at[k - 1], send_sem=z_send.at[k - 1], recv_sem=z_recv.at[k - 1],
                device_id=peer_z[k], device_id_type=MESH,
            )
            for k in range(1, SIDE)
        ]

    def shrunk_copies():
        return [
            pltpu.make_async_remote_copy(
                src_ref=shrunk_v.at[BACK], dst_ref=shrunk_v.at[BACK - k], send_sem=s_send.at[k - 1],
                recv_sem=s_recv.at[k - 1], device_id=later[k], device_id_type=MESH,
            )
            for k in range(1, BACK + 1)
        ]

    def shrink():
        maps = jnp.concatenate([table(down, 0, 8), table(down, 8, 8)], axis=0)
        part = lax.dot_general(maps, quarter[...], (((1,), (1,)), ((), ())), preferred_element_type=F32)
        mask = members(me * ROWS)
        for i in range(2):
            total = jnp.zeros((RANK, ROWS), F32)
            for t in range(TENANTS):
                row = i * SLAB + t * RANK
                total = total + jnp.where(mask[t], part[row : row + RANK, :], 0.0)
            fold[i * RANK : (i + 1) * RANK, :] = total
        for c in z_copies():
            c.start()

    def shrunk():
        for c in z_copies():
            c.wait()
        total = ((fold[...] + got[0]) + (got[1] + got[2])).astype(BF16)
        shrunk_v[BACK] = total[RANK:, :]
        for c in shrunk_copies():
            c.start()
        spread_out(total[:RANK, :].astype(F32), me * ROWS)

    def step(reduction, stage):
        return lambda: reduction.step(stage)

    def spread_out(values, first):
        mask = members(first)
        for t in range(TENANTS):
            spread[t * RANK : (t + 1) * RANK, :] = jnp.where(mask[t], values, 0.0).astype(BF16)

    def keys():
        for h in range(2):
            cols = slice(h * HEAD, (h + 1) * HEAD)
            k_win[BACK * ROWS :, cols] = rope(base[0, :, cols]).astype(BF16)

    def values():
        v_win[BACK * ROWS :, :] = base[1].astype(BF16)

    def send(win, which, slot, *parts):
        def act():
            for part in parts:
                win_copy(win, which, slot, part).start()

        return act

    def send_k(*parts):
        return send(k_win, 0, 0, *parts)

    def send_v(*parts):
        return send(v_win, 1, 0, *parts)

    def forward_k(*parts):
        def act():
            for part in parts:
                win_copy(k_win, 0, 0, part).wait()
                win_copy(k_win, 0, 1, part).start()

        return act

    def pass_v(*parts):
        def act():
            for part in parts:
                pass_copy(part).start()

        return act

    def forward_v(*parts):
        def act():
            for part in parts:
                pass_copy(part).wait()
                win_copy(v_win, 1, 1, part).start()

        return act

    def share(win, which, slot):
        for part in range(PARTS):
            if which or slot:
                win_copy(win, which, slot, part).wait()
        share_copy(win, which, slot).start()

    def query(j, carry):
        cols = jnp.concatenate(
            [up[pl.ds(pl.multiple_of((2 * j + s) * SLAB, SLAB), SLAB), :] for s in range(2)], axis=1
        )
        delta = lax.dot_general(spread[...], cols, (((0,), (0,)), ((), ())), preferred_element_type=F32)
        rows = base[2 + j] + ADAPTER_SCALE * delta
        q_own[j] = jnp.concatenate([rope(rows[:, :HEAD]), rope(rows[:, HEAD:])], axis=1).astype(BF16)
        return carry

    def value(i, carry):
        at = pl.ds(pl.multiple_of(i * ROWS, ROWS), ROWS)
        spread_out(shrunk_v[i].astype(F32), (me - BACK + i) * ROWS)
        delta = lax.dot_general(
            spread[...], table(up, 8, 2), (((0,), (0,)), ((), ())), preferred_element_type=F32
        )
        own = jnp.where(i == BACK, base[1], v_win[at, :].astype(F32))
        v_win[at, :] = (own + ADAPTER_SCALE * delta).astype(BF16)
        return carry

    def wait_keys():
        for slot in range(2):
            share(k_win, 0, slot)
        for slot in range(2):
            share_copy(k_win, 0, slot).wait()

    def wait_values():
        for slot in range(2):
            share(v_win, 1, slot)
        for slot in range(2):
            share_copy(v_win, 1, slot).wait()
        for c in shrunk_copies():
            c.wait()
        lax.fori_loop(0, BACK + 1, value, 0)

    def last_part(scores):
        wait_keys()

        def ahead(u, carry):
            score(u, q_own, k_win, q_mark, k_mark, marked, scores, highest, peak)
            return carry

        lax.fori_loop(0, AHEAD, ahead, 0)
        wait_values()

        def behind(u, carry):
            mix(u, v_win, out, scores, peak, sums, mixed)

            @pl.when(u + AHEAD < UNITS)
            def _():
                score(u + AHEAD, q_own, k_win, q_mark, k_mark, marked, scores, highest, peak)

            return carry

        lax.fori_loop(0, UNITS, behind, 0)

    def first_part(x, normed, w, qd, vd, qu, vu):
        loads = [
            pltpu.make_async_copy(src, dst, ad_sem.at[i])
            for i, (src, dst) in enumerate([(qd_hbm, qd), (vd_hbm, vd), (qu_hbm, qu), (vu_hbm, vu)])
        ]
        for c in loads:
            c.start()
        x_loads = [
            pltpu.make_async_copy(x_hbm.at[pl.ds(64 * i, 64)], x.at[pl.ds(64 * i, 64)], x_sem.at[i])
            for i in range(8)
        ]
        for c in x_loads:
            c.start()
        w_loads = [
            pltpu.make_async_copy(wk_hbm, w.at[0], w_sem.at[0]),
            pltpu.make_async_copy(wv_hbm, w.at[1], w_sem.at[1]),
        ] + [
            pltpu.make_async_copy(wq_hbm.at[:, pl.ds(256 * i, 256)], w.at[2 + i], w_sem.at[2 + i])
            for i in range(4)
        ]
        for c in w_loads:
            c.start()


        def gather(target, pieces):
            def one(t, carry):
                local = table_ref[tid_ref[t]] - me * HELD
                held = jnp.logical_and(local >= 0, local < HELD)
                at = jnp.clip(local, 0, HELD - 1)
                for stored, first, slabs in pieces:
                    for s in range(slabs):
                        tile = stored[at, :, s * 128 : (s + 1) * 128]
                        row = pl.multiple_of((first + s) * SLAB + t * RANK, RANK)
                        target[pl.ds(row, RANK), :] = jnp.where(held, tile, jnp.zeros_like(tile))
                return carry

            lax.fori_loop(0, TENANTS, one, 0)


        for c in loads[:2]:
            c.wait()
        gather(mine_d, [(qd, 0, 8), (vd, 8, 8)])
        pl.semaphore_wait(barrier, len(greeted))
        red_d.start(0)
        for c in loads[2:]:
            c.wait()
        gather(mine_u, [(qu, 0, 8), (vu, 8, 2)])
        red_u.start(0)

        def normalise(first, count):
            def one(i, carry):
                at = pl.ds(pl.multiple_of(i * NORM_STEP, NORM_STEP), NORM_STEP)
                wide = x[at, :].astype(F32)
                scale = lax.rsqrt(jnp.mean(wide * wide, axis=1, keepdims=True) + NORM_EPS)
                normed[at, :] = (wide * scale * gain_ref[...]).astype(BF16)
                return carry

            lax.fori_loop(first, first + count, one, 0)


        red_d.step(0)
        for i in range(4):
            x_loads[i].wait()
        normalise(0, 8)
        for i in range(4, 8):
            x_loads[i].wait()
        normalise(8, 8)
        quarter[...] = normed[:, pl.ds(pl.multiple_of(z * 1024, 1024), 1024)]
        lax.fori_loop(0, 8, angles, 0)
        red_u.step(0)
        marks(starts, ends, me, q_mark, k_mark)

        def product(j):
            w_loads_j = pltpu.make_async_copy(wk_hbm, w.at[j], w_sem.at[j])
            w_loads_j.wait()
            base[j] = jnp.dot(normed[...], w[j], preferred_element_type=F32)


        plan = [
            [keys, step(red_d, 1), send_k(0, 1)],
            [values, send_k(2, 3), pass_v(0, 1)],
            [step(red_d, 2), step(red_u, 1), send_v(0, 1), pass_v(2, 3)],
            [forward_k(0, 1, 2, 3)],
            [step(red_d, 3), step(red_u, 2), forward_v(0, 1)],
            [send_v(2, 3)],
        ]

        def work(j, carry):
            product(j)
            for at, acts in enumerate(plan):

                @pl.when(j == at)
                def _(acts=acts):
                    for act in acts:
                        act()

            return carry

        lax.fori_loop(0, 6, work, 0)
        red_d.arrive(4)
        shrink()
        red_u.step(3)
        forward_v(2, 3)()
        shrunk()
        red_u.arrive(4)
        lax.fori_loop(0, 4, query, 0)

    pl.run_scoped(
        first_part,
        pltpu.VMEM((ROWS, WIDTH), BF16),
        pltpu.VMEM((ROWS, WIDTH), BF16),
        pltpu.VMEM((6, WIDTH, 256), BF16),
        pltpu.VMEM((HELD, RANK, 1024), BF16),
        pltpu.VMEM((HELD, RANK, 1024), BF16),
        pltpu.VMEM((HELD, RANK, QCOLS), BF16),
        pltpu.VMEM((HELD, RANK, KVCOLS), BF16),
    )
    pl.run_scoped(last_part, pltpu.VMEM((AHEAD, CHUNKS, 4 * QT, KC), F32))


def marks(starts, ends, me, q_mark, k_mark):
    lane = lax.broadcasted_iota(jnp.int32, (1, HEAD), 1)
    begin = jnp.full((1, HEAD), 2**30, jnp.int32)
    end = jnp.full((1, HEAD), 2**30, jnp.int32)
    for t in range(TENANTS):
        begin = jnp.where(lane == t, starts[t], begin)
        end = jnp.where(lane == t, ends[t], end)
    begin = jnp.where(lane == TENANTS, -(2**30), begin)
    end = jnp.where(lane == TENANTS, 0, end)

    def inside(first, row):
        token = first + row + lax.broadcasted_iota(jnp.int32, (128, HEAD), 0)
        return jnp.logical_and(token >= begin, token < end)

    def keys(i, carry):
        row = pl.multiple_of(i * 128, 128)
        k_mark[pl.ds(row, 128), :] = jnp.where(inside((me - BACK) * ROWS, row), 1.0, 0.0).astype(BF16)
        return carry

    lax.fori_loop(0, SPAN // 128, keys, 0)

    def queries(i, carry):
        row = pl.multiple_of(i * 128, 128)
        open_to = jnp.logical_or(inside(me * ROWS, row), lane > TENANTS)
        q_mark[pl.ds(row, 128), :] = jnp.where(open_to, 0.0, -FAR).astype(BF16)
        return carry

    lax.fori_loop(0, ROWS // 128, queries, 0)


def unit_of(u):
    group, part = u // 2, lax.rem(u, 2)
    rows = pl.ds(pl.multiple_of(part * QT, QT), QT)
    head_cols = pl.ds(pl.multiple_of(group * HEAD, HEAD), HEAD)
    return group, part, rows, head_cols


def score(u, q_ref, k_win, q_mark, k_mark, marked, scores, highest, peak):
    group, part, rows, head_cols = unit_of(u)
    slot = lax.rem(u, AHEAD)
    for h in range(4):
        marked[h * QT : (h + 1) * QT, :HEAD] = q_ref[
            2 * group + h // 2, rows, (h % 2) * HEAD : (h % 2 + 1) * HEAD
        ]
        marked[h * QT : (h + 1) * QT, HEAD:] = q_mark[rows, :]
    for i in range(CHUNKS):
        at = pl.multiple_of(part * QT + i * KC, 128)
        keys = jnp.concatenate([k_win[pl.ds(at, KC), head_cols], k_mark[pl.ds(at, KC), :]], axis=1)
        s = lax.dot_general(marked[...], keys, (((1,), (1,)), ((), ())), preferred_element_type=F32)
        if i == CHUNKS - 1:
            seen = lax.broadcasted_iota(jnp.int32, (QT, QT), 0) >= lax.broadcasted_iota(jnp.int32, (QT, QT), 1)
            tail = s[:, KC - QT :]
            tail = jnp.concatenate(
                [jnp.where(seen, tail[h * QT : (h + 1) * QT, :], -FAR) for h in range(4)], axis=0
            )
            s = jnp.concatenate([s[:, : KC - QT], tail], axis=1)
        scores[slot, i] = s
        top = s[:, :128]
        for c in range(1, KC // 128):
            top = jnp.maximum(top, s[:, c * 128 : (c + 1) * 128])
        highest[...] = top if i == 0 else jnp.maximum(highest[...], top)
    peak[slot] = jnp.broadcast_to(jnp.max(highest[...], axis=1, keepdims=True) * SCALE, highest.shape)


def mix(u, v_win, out, scores, peak, sums, mixed):
    group, part, rows, head_cols = unit_of(u)
    slot = lax.rem(u, AHEAD)
    for i in range(CHUNKS):
        at = pl.multiple_of(part * QT + i * KC, 128)
        s = scores[slot, i]
        top = peak[slot]
        ps = [jnp.exp2(s[:, c * 128 : (c + 1) * 128] * SCALE - top) for c in range(KC // 128)]
        total = ps[0]
        for p in ps[1:]:
            total = total + p
        probs = jnp.concatenate([p.astype(BF16) for p in ps], axis=1)
        product = jnp.dot(probs, v_win[pl.ds(at, KC), head_cols], preferred_element_type=F32)
        sums[...] = total if i == 0 else sums[...] + total
        mixed[...] = product if i == 0 else mixed[...] + product
    result = mixed[...] / jnp.sum(sums[...], axis=1, keepdims=True)
    for h in range(4):
        cols = pl.ds(pl.multiple_of(group * 512 + h * HEAD, HEAD), HEAD)
        out[rows, cols] = result[h * QT : (h + 1) * QT, :].astype(BF16)


def block(x, gain, wq, wk, wv, qd, vd, qu, vu, lengths, tid, slots):
    any_space = pl.BlockSpec(memory_space=pl.ANY)
    smem = pl.BlockSpec(memory_space=pltpu.SMEM)
    vmem = pl.BlockSpec(memory_space=pltpu.VMEM)
    dma = pltpu.SemaphoreType.DMA

    def reduce_scratch(rows):
        return [
            pltpu.VMEM((rows, 128), BF16),
            pltpu.VMEM((rows // 2, 128), BF16),
            pltpu.VMEM((3, rows // 8, 128), BF16),
            pltpu.VMEM((3, rows // 8, 128), BF16),
            pltpu.VMEM((rows, 128), BF16),
        ]

    return pl.pallas_call(
        block_kernel,
        out_shape=jax.ShapeDtypeStruct((ROWS, QCOLS), BF16),
        in_specs=[smem] * 3 + [any_space, vmem] + [any_space] * 7,
        out_specs=vmem,
        scratch_shapes=[
            pltpu.VMEM((6, ROWS, 256), F32),
            pltpu.VMEM((ROWS, 1024), BF16),
        ]
        + reduce_scratch(DOWN_ROWS)
        + reduce_scratch(UP_ROWS)
        + [
            pltpu.VMEM((ROWS, HEAD), F32),
            pltpu.VMEM((ROWS, HEAD), F32),
            pltpu.VMEM((2 * RANK, ROWS), F32),
            pltpu.VMEM((3, 2 * RANK, ROWS), F32),
            pltpu.VMEM((BACK + 1, RANK, ROWS), BF16),
            pltpu.VMEM((SLAB, ROWS), BF16),
            pltpu.VMEM((SPAN, KVCOLS), BF16),
            pltpu.VMEM((SPAN, KVCOLS), BF16),
            pltpu.VMEM((ROWS, KVCOLS), BF16),
            pltpu.VMEM((4, ROWS, 256), BF16),
            pltpu.VMEM((ROWS, HEAD), BF16),
            pltpu.VMEM((SPAN, HEAD), BF16),
            pltpu.VMEM((4 * QT, 2 * HEAD), BF16),
            pltpu.VMEM((4 * QT, HEAD), F32),
            pltpu.VMEM((AHEAD, 4 * QT, HEAD), F32),
        ]
        + [pltpu.VMEM((4 * QT, HEAD), F32)] * 2
        + [
            dma((4,)), dma((8,)), dma((6,)),
            *[dma((COPIES,))] * 4,
            dma((3,)), dma((3,)), dma((4 * PARTS,)), dma((4 * PARTS,)), dma((PARTS,)), dma((PARTS,)),
            dma((4,)), dma((4,)), dma((4,)), dma((4,)),
        ],
        compiler_params=pltpu.CompilerParams(
            collective_id=0, has_side_effects=True, vmem_limit_bytes=60 * 1024 * 1024
        ),
        name="block",
    )(lengths, tid, slots, x, gain, wq, wk, wv, qd, vd, qu, vu)


def body(
    layer_input, input_norm_gain, query_weight, key_weight, value_weight,
    query_down_maps, value_down_maps, query_up_maps, value_up_maps,
    tenant_prompt_length, tenant_adapter_id, adapter_storage_slot,
):
    return block(
        layer_input, input_norm_gain.reshape(1, WIDTH), query_weight, key_weight, value_weight,
        query_down_maps, value_down_maps, query_up_maps, value_up_maps,
        tenant_prompt_length, tenant_adapter_id, adapter_storage_slot,
    )


def solution(mesh):
    placed = (
        P("tok", None), P(), P(None, "mlp"), P(None, "mlp"), P(None, "mlp"),
        P("tok", None, "mlp"), P("tok", None, "mlp"), P("tok", None, "mlp"), P("tok", None, "mlp"),
        P(), P(), P(),
    )
    return jax.shard_map(
        body, mesh=mesh, in_specs=placed, out_specs=P("tok", "mlp"), check_vma=False
    )
```

```python
import functools

import jax
import jax.numpy as jnp
import numpy as np
from jax import lax
from jax.experimental import pallas as pl
from jax.experimental.pallas import tpu as pltpu
from jax.sharding import PartitionSpec as P

WIDTH = 4096
HEAD = 128
RANK = 16
TENANTS = 16
ROWS = 512
HELD = 8
QCOLS = 1024
KVCOLS = 256
BACK = 4
N_TOK = 32
SIDE = 4
NORM_EPS = 1e-05
ROPE_BASE = 500000.0
ADAPTER_SCALE = 0.5
MESH = pl.DeviceIdType.MESH
F32 = jnp.float32
BF16 = jnp.bfloat16
SLAB = TENANTS * RANK
DOWN_ROWS = 2 * 1024 // 128 * SLAB
UP_ROWS = (QCOLS + KVCOLS) // 128 * SLAB
AHEAD = 3
NORM_STEP = 32
SPAN = (BACK + 1) * ROWS
FAR = 1e30
QT = 256
KC = 1152
CHUNKS = (BACK * ROWS + QT) // KC
UNITS = 4
SCALE = np.float32(HEAD**-0.5 * np.log2(np.e))
COPIES = 11
PARTS = 4


def prompt_bounds(len_ref):
    starts, ends = [], []
    at = jnp.int32(0)
    for t in range(TENANTS):
        starts.append(at)
        at = at + len_ref[t]
        ends.append(at)
    return starts, ends


class AllReduce:
    def __init__(self, place, rows, mine, from_core, from_a, from_b, full, send, recv):
        self.place, self.rows = place, rows
        self.mine, self.from_core, self.from_a, self.from_b = mine, from_core, from_a, from_b
        self.full, self.send, self.recv = full, send, recv
        p = place
        half, quarter = rows // 2, rows // 8
        self.half_at = pl.multiple_of(p["core"] * half, 16)
        self.other_at = pl.multiple_of((1 - p["core"]) * half, 16)
        self.a_at = pl.multiple_of(p["core"] * half + p["ca"] * quarter, 16)

    def copy(self, slot, src, dst, dev):
        return pltpu.make_async_remote_copy(
            src_ref=src, dst_ref=dst, send_sem=self.send.at[slot], recv_sem=self.recv.at[slot],
            device_id=dev, device_id_type=MESH,
        )

    def copies(self, stage):
        p = self.place
        half, quarter = self.rows // 2, self.rows // 8
        if stage == 0:
            return [self.copy(0, self.mine.at[pl.ds(self.other_at, half)], self.from_core, p["sib"])]
        if stage == 4:
            ref = self.full.at[pl.ds(self.half_at, half)]
            return [self.copy(10, ref, ref, p["sib"])]
        out = []
        for k in range(1, SIDE):
            if stage == 1:
                a = (p["ca"] + k) % SIDE
                at = pl.multiple_of(p["core"] * half + a * quarter, 16)
                out.append(self.copy(k, self.mine.at[pl.ds(at, quarter)], self.from_a.at[k - 1], p["peer_a"][k]))
            if stage == 2:
                ref = self.mine.at[pl.ds(self.a_at, quarter)]
                out.append(self.copy(3 + k, ref, self.from_b.at[k - 1], p["peer_b"][k]))
            if stage == 3:
                ref = self.full.at[pl.ds(self.a_at, quarter)]
                out.append(self.copy(6 + k, ref, ref, p["peer_a"][k]))
        return out

    def start(self, stage):
        for c in self.copies(stage):
            c.start()

    def arrive(self, stage):
        for c in self.copies(stage):
            c.wait()
        half, quarter = self.rows // 2, self.rows // 8
        if stage == 0:
            at = pl.ds(self.half_at, half)
            self.mine[at, :] = self.mine[at, :] + self.from_core[...]
        if stage == 1:
            at = pl.ds(self.a_at, quarter)
            self.mine[at, :] = (self.mine[at, :] + self.from_a[0]) + (self.from_a[1] + self.from_a[2])
        if stage == 2:
            at = pl.ds(self.a_at, quarter)
            self.full[at, :] = (self.mine[at, :] + self.from_b[0]) + (self.from_b[1] + self.from_b[2])

    def step(self, stage):
        self.arrive(stage)
        self.start(stage + 1)


def block_kernel(
    len_ref, tid_ref, table_ref,
    x_hbm, gain_ref, wq_hbm, wk_hbm, wv_hbm, qd_hbm, vd_hbm, qu_hbm, vu_hbm,
    out,
    base, quarter,
    mine_d, core_d, a_d, b_d, down,
    mine_u, core_u, a_u, b_u, up,
    cosine, sine, fold, got, shrunk_v, spread, k_win, v_win, passing, turning, q_own,
    q_mark, k_mark, marked, highest, peak, sums, mixed,
    ad_sem, x_sem, w_sem, sd, rd, su, ru, z_send, z_recv, kv_send, kv_recv, pass_send, pass_recv, turn_send, turn_recv, turned, share_send, share_recv, s_send, s_recv,
):
    me = lax.axis_index("tok")
    z = lax.axis_index("mlp")
    core = lax.rem(me, 2)
    chip = me // 2
    px, py = lax.rem(chip, SIDE), chip // SIDE

    def tok_of(yy, xx, cc):
        return (yy * SIDE + xx) * 2 + cc

    sib = (me + 1 - 2 * core, z)
    x_first = 1 - core
    ca = px * x_first + py * (1 - x_first)
    cb = py * x_first + px * (1 - x_first)
    peer_a, peer_b, peer_z = {}, {}, {}
    for k in range(1, SIDE):
        xk, yk = (px + k) % SIDE, (py + k) % SIDE
        along_x = tok_of(py, xk, core)
        along_y = tok_of(yk, px, core)
        peer_a[k] = (along_x * x_first + along_y * (1 - x_first), z)
        peer_b[k] = (along_y * x_first + along_x * (1 - x_first), z)
        peer_z[k] = (me, (z + k) % SIDE)
    later = {k: ((me + k) % N_TOK, z) for k in range(1, BACK + 1)}
    earlier = {k: ((me + N_TOK - k) % N_TOK, z) for k in range(1, BACK + 1)}
    place = dict(core=core, ca=ca, cb=cb, sib=sib, peer_a=peer_a, peer_b=peer_b)

    barrier = pltpu.get_barrier_semaphore()
    over = (tok_of((py + px // 2) % SIDE, (px + 3) % SIDE, core), z)
    goal = (tok_of(py, (px + 3) % SIDE, core), z)
    under_x = (px + 1) % SIDE
    under = (tok_of((py + SIDE - under_x // 2) % SIDE, under_x, core), z)
    greeted = [sib, over, under] + [d[k] for d in (peer_a, peer_b, peer_z) for k in range(1, SIDE)]
    greeted += [d[k] for d in (later, earlier) for k in range(1, BACK + 1)]
    for dev in greeted:
        pl.semaphore_signal(barrier, inc=1, device_id=dev, device_id_type=MESH)

    starts, ends = prompt_bounds(len_ref)
    red_d = AllReduce(place, DOWN_ROWS, mine_d, core_d, a_d, b_d, down, sd, rd)
    red_u = AllReduce(place, UP_ROWS, mine_u, core_u, a_u, b_u, up, su, ru)

    def angles(i, carry):
        row = pl.multiple_of(i * 64, 64)
        token = me * ROWS + row + lax.broadcasted_iota(jnp.int32, (64, HEAD), 0)
        begin = jnp.zeros((64, HEAD), jnp.int32)
        for t in range(TENANTS):
            begin = jnp.where(token >= starts[t], starts[t], begin)
        lane = lax.broadcasted_iota(jnp.int32, (64, HEAD), 1)
        pair = jnp.where(lane >= HEAD // 2, lane - HEAD // 2, lane)
        inverse = jnp.exp(-(pair.astype(F32) * (2.0 / HEAD)) * np.float32(np.log(np.float32(ROPE_BASE))))
        angle = (token - begin).astype(F32) * inverse
        cosine[pl.ds(row, 64), :] = jnp.cos(angle)
        s = jnp.sin(angle)
        sine[pl.ds(row, 64), :] = jnp.where(lane >= HEAD // 2, s, -s)
        return carry


    def rope(block):
        return block * cosine[...] + pltpu.roll(block, HEAD // 2, 1) * sine[...]

    def rows_of(win, block, part, parts):
        size = ROWS // parts
        return win.at[pl.ds(pl.multiple_of(block * ROWS + part * size, size), size)]

    def win_copy(win, which, slot, part):
        at = (2 * which + slot) * PARTS + part
        if which == 0 or slot == 0:
            src, dst = rows_of(win, BACK - 2 * slot, part, PARTS), rows_of(win, 2 - 2 * slot, part, PARTS)
            dev = later[2]
        else:
            src, dst = rows_of(passing, 0, part, PARTS), rows_of(win, 0, part, PARTS)
            dev = goal
        return pltpu.make_async_remote_copy(
            src_ref=src, dst_ref=dst, send_sem=kv_send.at[at], recv_sem=kv_recv.at[at],
            device_id=dev, device_id_type=MESH,
        )

    def pass_copy(part):
        return pltpu.make_async_remote_copy(
            src_ref=rows_of(v_win, BACK, part, PARTS), dst_ref=rows_of(passing, 0, part, PARTS),
            send_sem=pass_send.at[part], recv_sem=pass_recv.at[part], device_id=over, device_id_type=MESH,
        )

    at_turn = px == SIDE - 1
    below = (tok_of((py + 1) % SIDE, px, core), z)
    row_start = (tok_of(py, 0, core), z)

    def turn_copy(part):
        return pltpu.make_async_remote_copy(
            src_ref=rows_of(v_win, BACK, part, PARTS), dst_ref=rows_of(turning, 0, part, PARTS),
            send_sem=turn_send.at[part], recv_sem=turn_recv.at[part], device_id=below, device_id_type=MESH,
        )

    def turned_copy(part):
        return pltpu.make_async_remote_copy(
            src_ref=rows_of(turning, 0, part, PARTS), dst_ref=rows_of(v_win, 2, part, PARTS),
            send_sem=turned.at[part], recv_sem=kv_recv.at[2 * PARTS + part], device_id=row_start,
            device_id_type=MESH,
        )

    def share_copy(win, which, slot):
        src, dst = (4 - 2 * core, 3) if slot == 0 else (2 - 2 * core, 1)
        at = 2 * which + slot
        return pltpu.make_async_remote_copy(
            src_ref=rows_of(win, src, 0, 1), dst_ref=rows_of(win, dst, 0, 1),
            send_sem=share_send.at[at], recv_sem=share_recv.at[at], device_id=sib, device_id_type=MESH,
        )

    def table(full, first, slabs):
        return jnp.concatenate([full[(first + s) * SLAB : (first + s + 1) * SLAB, :] for s in range(slabs)], axis=1)

    def members(first):
        token = first + lax.broadcasted_iota(jnp.int32, (RANK, ROWS), 1)
        return [jnp.logical_and(token >= starts[t], token < ends[t]) for t in range(TENANTS)]

    def z_copies():
        return [
            pltpu.make_async_remote_copy(
                src_ref=fold, dst_ref=got.at[k - 1], send_sem=z_send.at[k - 1], recv_sem=z_recv.at[k - 1],
                device_id=peer_z[k], device_id_type=MESH,
            )
            for k in range(1, SIDE)
        ]

    def shrunk_copies():
        return [
            pltpu.make_async_remote_copy(
                src_ref=shrunk_v.at[BACK], dst_ref=shrunk_v.at[BACK - k], send_sem=s_send.at[k - 1],
                recv_sem=s_recv.at[k - 1], device_id=later[k], device_id_type=MESH,
            )
            for k in range(1, BACK + 1)
        ]

    def shrink():
        maps = jnp.concatenate([table(down, 0, 8), table(down, 8, 8)], axis=0)
        part = lax.dot_general(maps, quarter[...], (((1,), (1,)), ((), ())), preferred_element_type=F32)
        mask = members(me * ROWS)
        for i in range(2):
            total = jnp.zeros((RANK, ROWS), F32)
            for t in range(TENANTS):
                row = i * SLAB + t * RANK
                total = total + jnp.where(mask[t], part[row : row + RANK, :], 0.0)
            fold[i * RANK : (i + 1) * RANK, :] = total
        for c in z_copies():
            c.start()

    def shrunk():
        for c in z_copies():
            c.wait()
        total = ((fold[...] + got[0]) + (got[1] + got[2])).astype(BF16)
        shrunk_v[BACK] = total[RANK:, :]
        for c in shrunk_copies():
            c.start()
        spread_out(total[:RANK, :].astype(F32), me * ROWS)

    def step(reduction, stage):
        return lambda: reduction.step(stage)

    def spread_out(values, first):
        mask = members(first)
        for t in range(TENANTS):
            spread[t * RANK : (t + 1) * RANK, :] = jnp.where(mask[t], values, 0.0).astype(BF16)

    def keys():
        for h in range(2):
            cols = slice(h * HEAD, (h + 1) * HEAD)
            k_win[BACK * ROWS :, cols] = rope(base[0, :, cols]).astype(BF16)

    def values():
        v_win[BACK * ROWS :, :] = base[1].astype(BF16)

    def send(win, which, slot, *parts):
        def act():
            for part in parts:
                win_copy(win, which, slot, part).start()

        return act

    def send_k(*parts):
        return send(k_win, 0, 0, *parts)

    def send_v(*parts):
        def act():
            @pl.when(jnp.logical_not(at_turn))
            def _():
                send(v_win, 1, 0, *parts)()

        return act

    def turn_v(*parts):
        def act():
            @pl.when(at_turn)
            def _():
                for part in parts:
                    turn_copy(part).start()

        return act

    def after_turn(*parts):
        def act():
            @pl.when(at_turn)
            def _():
                for part in parts:
                    turn_copy(part).wait()
                    turned_copy(part).start()

        return act

    def forward_k(*parts):
        def act():
            for part in parts:
                win_copy(k_win, 0, 0, part).wait()
                win_copy(k_win, 0, 1, part).start()

        return act

    def pass_v(*parts):
        def act():
            for part in parts:
                pass_copy(part).start()

        return act

    def forward_v(*parts):
        def act():
            for part in parts:
                pass_copy(part).wait()
                win_copy(v_win, 1, 1, part).start()

        return act

    def share(win, which, slot):
        for part in range(PARTS):
            if which == 1 and slot == 0:
                win_copy(win, which, slot, part).wait_recv()

                @pl.when(at_turn)
                def _(part=part):
                    turned_copy(part).wait_send()

                @pl.when(jnp.logical_not(at_turn))
                def _(part=part):
                    win_copy(win, which, slot, part).wait_send()

            elif which or slot:
                win_copy(win, which, slot, part).wait()
        share_copy(win, which, slot).start()

    def query(j, carry):
        cols = jnp.concatenate(
            [up[pl.ds(pl.multiple_of((2 * j + s) * SLAB, SLAB), SLAB), :] for s in range(2)], axis=1
        )
        delta = lax.dot_general(spread[...], cols, (((0,), (0,)), ((), ())), preferred_element_type=F32)
        rows = base[2 + j] + ADAPTER_SCALE * delta
        q_own[j] = jnp.concatenate([rope(rows[:, :HEAD]), rope(rows[:, HEAD:])], axis=1).astype(BF16)
        return carry

    def value(i, carry):
        at = pl.ds(pl.multiple_of(i * ROWS, ROWS), ROWS)
        spread_out(shrunk_v[i].astype(F32), (me - BACK + i) * ROWS)
        delta = lax.dot_general(
            spread[...], table(up, 8, 2), (((0,), (0,)), ((), ())), preferred_element_type=F32
        )
        own = jnp.where(i == BACK, base[1], v_win[at, :].astype(F32))
        v_win[at, :] = (own + ADAPTER_SCALE * delta).astype(BF16)
        return carry

    def wait_keys():
        for slot in range(2):
            share(k_win, 0, slot)
        for slot in range(2):
            share_copy(k_win, 0, slot).wait()

    def wait_values():
        for slot in range(2):
            share(v_win, 1, slot)
        for slot in range(2):
            share_copy(v_win, 1, slot).wait()
        for c in shrunk_copies():
            c.wait()
        lax.fori_loop(0, BACK + 1, value, 0)

    def last_part(scores):
        wait_keys()

        def ahead(u, carry):
            score(u, q_own, k_win, q_mark, k_mark, marked, scores, highest, peak)
            return carry

        lax.fori_loop(0, AHEAD, ahead, 0)
        wait_values()

        def behind(u, carry):
            mix(u, v_win, out, scores, peak, sums, mixed)

            @pl.when(u + AHEAD < UNITS)
            def _():
                score(u + AHEAD, q_own, k_win, q_mark, k_mark, marked, scores, highest, peak)

            return carry

        lax.fori_loop(0, UNITS, behind, 0)

    def first_part(x, normed, w, qd, vd, qu, vu):
        loads = [
            pltpu.make_async_copy(src, dst, ad_sem.at[i])
            for i, (src, dst) in enumerate([(qd_hbm, qd), (vd_hbm, vd), (qu_hbm, qu), (vu_hbm, vu)])
        ]
        for c in loads:
            c.start()
        x_loads = [
            pltpu.make_async_copy(x_hbm.at[pl.ds(64 * i, 64)], x.at[pl.ds(64 * i, 64)], x_sem.at[i])
            for i in range(8)
        ]
        for c in x_loads:
            c.start()
        w_loads = [
            pltpu.make_async_copy(wk_hbm, w.at[0], w_sem.at[0]),
            pltpu.make_async_copy(wv_hbm, w.at[1], w_sem.at[1]),
        ] + [
            pltpu.make_async_copy(wq_hbm.at[:, pl.ds(256 * i, 256)], w.at[2 + i], w_sem.at[2 + i])
            for i in range(4)
        ]
        for c in w_loads:
            c.start()


        def gather(target, pieces):
            def one(t, carry):
                local = table_ref[tid_ref[t]] - me * HELD
                held = jnp.logical_and(local >= 0, local < HELD)
                at = jnp.clip(local, 0, HELD - 1)
                for stored, first, slabs in pieces:
                    for s in range(slabs):
                        tile = stored[at, :, s * 128 : (s + 1) * 128]
                        row = pl.multiple_of((first + s) * SLAB + t * RANK, RANK)
                        target[pl.ds(row, RANK), :] = jnp.where(held, tile, jnp.zeros_like(tile))
                return carry

            lax.fori_loop(0, TENANTS, one, 0)


        for c in loads[:2]:
            c.wait()
        gather(mine_d, [(qd, 0, 8), (vd, 8, 8)])
        pl.semaphore_wait(barrier, len(greeted))
        red_d.start(0)
        for c in loads[2:]:
            c.wait()
        gather(mine_u, [(qu, 0, 8), (vu, 8, 2)])
        red_u.start(0)

        def normalise(first, count):
            def one(i, carry):
                at = pl.ds(pl.multiple_of(i * NORM_STEP, NORM_STEP), NORM_STEP)
                wide = x[at, :].astype(F32)
                scale = lax.rsqrt(jnp.mean(wide * wide, axis=1, keepdims=True) + NORM_EPS)
                normed[at, :] = (wide * scale * gain_ref[...]).astype(BF16)
                return carry

            lax.fori_loop(first, first + count, one, 0)


        red_d.step(0)
        for i in range(4):
            x_loads[i].wait()
        normalise(0, 8)
        for i in range(4, 8):
            x_loads[i].wait()
        normalise(8, 8)
        quarter[...] = normed[:, pl.ds(pl.multiple_of(z * 1024, 1024), 1024)]
        lax.fori_loop(0, 8, angles, 0)
        red_u.step(0)
        marks(starts, ends, me, q_mark, k_mark)

        def product(j):
            w_loads_j = pltpu.make_async_copy(wk_hbm, w.at[j], w_sem.at[j])
            w_loads_j.wait()
            base[j] = jnp.dot(normed[...], w[j], preferred_element_type=F32)


        plan = [
            [keys, step(red_d, 1), send_k(0, 1)],
            [values, turn_v(0, 1), send_k(2, 3)],
            [step(red_d, 2), step(red_u, 1), pass_v(0, 1), turn_v(2, 3)],
            [pass_v(2, 3)],
            [step(red_d, 3), step(red_u, 2), forward_k(0, 1, 2, 3), after_turn(0, 1)],
            [forward_v(0, 1), send_v(0, 1, 2, 3), after_turn(2, 3)],
        ]

        def work(j, carry):
            product(j)
            for at, acts in enumerate(plan):

                @pl.when(j == at)
                def _(acts=acts):
                    for act in acts:
                        act()

            return carry

        lax.fori_loop(0, 6, work, 0)
        red_d.arrive(4)
        shrink()
        red_u.step(3)
        forward_v(2, 3)()
        shrunk()
        red_u.arrive(4)
        lax.fori_loop(0, 4, query, 0)

    pl.run_scoped(
        first_part,
        pltpu.VMEM((ROWS, WIDTH), BF16),
        pltpu.VMEM((ROWS, WIDTH), BF16),
        pltpu.VMEM((6, WIDTH, 256), BF16),
        pltpu.VMEM((HELD, RANK, 1024), BF16),
        pltpu.VMEM((HELD, RANK, 1024), BF16),
        pltpu.VMEM((HELD, RANK, QCOLS), BF16),
        pltpu.VMEM((HELD, RANK, KVCOLS), BF16),
    )
    pl.run_scoped(last_part, pltpu.VMEM((AHEAD, CHUNKS, 4 * QT, KC), F32))


def marks(starts, ends, me, q_mark, k_mark):
    lane = lax.broadcasted_iota(jnp.int32, (1, HEAD), 1)
    begin = jnp.full((1, HEAD), 2**30, jnp.int32)
    end = jnp.full((1, HEAD), 2**30, jnp.int32)
    for t in range(TENANTS):
        begin = jnp.where(lane == t, starts[t], begin)
        end = jnp.where(lane == t, ends[t], end)
    begin = jnp.where(lane == TENANTS, -(2**30), begin)
    end = jnp.where(lane == TENANTS, 0, end)

    def inside(first, row):
        token = first + row + lax.broadcasted_iota(jnp.int32, (128, HEAD), 0)
        return jnp.logical_and(token >= begin, token < end)

    def keys(i, carry):
        row = pl.multiple_of(i * 128, 128)
        k_mark[pl.ds(row, 128), :] = jnp.where(inside((me - BACK) * ROWS, row), 1.0, 0.0).astype(BF16)
        return carry

    lax.fori_loop(0, SPAN // 128, keys, 0)

    def queries(i, carry):
        row = pl.multiple_of(i * 128, 128)
        open_to = jnp.logical_or(inside(me * ROWS, row), lane > TENANTS)
        q_mark[pl.ds(row, 128), :] = jnp.where(open_to, 0.0, -FAR).astype(BF16)
        return carry

    lax.fori_loop(0, ROWS // 128, queries, 0)


def unit_of(u):
    group, part = u // 2, lax.rem(u, 2)
    rows = pl.ds(pl.multiple_of(part * QT, QT), QT)
    head_cols = pl.ds(pl.multiple_of(group * HEAD, HEAD), HEAD)
    return group, part, rows, head_cols


def score(u, q_ref, k_win, q_mark, k_mark, marked, scores, highest, peak):
    group, part, rows, head_cols = unit_of(u)
    slot = lax.rem(u, AHEAD)
    for h in range(4):
        marked[h * QT : (h + 1) * QT, :HEAD] = q_ref[
            2 * group + h // 2, rows, (h % 2) * HEAD : (h % 2 + 1) * HEAD
        ]
        marked[h * QT : (h + 1) * QT, HEAD:] = q_mark[rows, :]
    for i in range(CHUNKS):
        at = pl.multiple_of(part * QT + i * KC, 128)
        keys = jnp.concatenate([k_win[pl.ds(at, KC), head_cols], k_mark[pl.ds(at, KC), :]], axis=1)
        s = lax.dot_general(marked[...], keys, (((1,), (1,)), ((), ())), preferred_element_type=F32)
        if i == CHUNKS - 1:
            seen = lax.broadcasted_iota(jnp.int32, (QT, QT), 0) >= lax.broadcasted_iota(jnp.int32, (QT, QT), 1)
            tail = s[:, KC - QT :]
            tail = jnp.concatenate(
                [jnp.where(seen, tail[h * QT : (h + 1) * QT, :], -FAR) for h in range(4)], axis=0
            )
            s = jnp.concatenate([s[:, : KC - QT], tail], axis=1)
        scores[slot, i] = s
        top = s[:, :128]
        for c in range(1, KC // 128):
            top = jnp.maximum(top, s[:, c * 128 : (c + 1) * 128])
        highest[...] = top if i == 0 else jnp.maximum(highest[...], top)
    peak[slot] = jnp.broadcast_to(jnp.max(highest[...], axis=1, keepdims=True) * SCALE, highest.shape)


def mix(u, v_win, out, scores, peak, sums, mixed):
    group, part, rows, head_cols = unit_of(u)
    slot = lax.rem(u, AHEAD)
    for i in range(CHUNKS):
        at = pl.multiple_of(part * QT + i * KC, 128)
        s = scores[slot, i]
        top = peak[slot]
        ps = [jnp.exp2(s[:, c * 128 : (c + 1) * 128] * SCALE - top) for c in range(KC // 128)]
        total = ps[0]
        for p in ps[1:]:
            total = total + p
        probs = jnp.concatenate([p.astype(BF16) for p in ps], axis=1)
        product = jnp.dot(probs, v_win[pl.ds(at, KC), head_cols], preferred_element_type=F32)
        sums[...] = total if i == 0 else sums[...] + total
        mixed[...] = product if i == 0 else mixed[...] + product
    result = mixed[...] / jnp.sum(sums[...], axis=1, keepdims=True)
    for h in range(4):
        cols = pl.ds(pl.multiple_of(group * 512 + h * HEAD, HEAD), HEAD)
        out[rows, cols] = result[h * QT : (h + 1) * QT, :].astype(BF16)


def block(x, gain, wq, wk, wv, qd, vd, qu, vu, lengths, tid, slots):
    any_space = pl.BlockSpec(memory_space=pl.ANY)
    smem = pl.BlockSpec(memory_space=pltpu.SMEM)
    vmem = pl.BlockSpec(memory_space=pltpu.VMEM)
    dma = pltpu.SemaphoreType.DMA

    def reduce_scratch(rows):
        return [
            pltpu.VMEM((rows, 128), BF16),
            pltpu.VMEM((rows // 2, 128), BF16),
            pltpu.VMEM((3, rows // 8, 128), BF16),
            pltpu.VMEM((3, rows // 8, 128), BF16),
            pltpu.VMEM((rows, 128), BF16),
        ]

    return pl.pallas_call(
        block_kernel,
        out_shape=jax.ShapeDtypeStruct((ROWS, QCOLS), BF16),
        in_specs=[smem] * 3 + [any_space, vmem] + [any_space] * 7,
        out_specs=vmem,
        scratch_shapes=[
            pltpu.VMEM((6, ROWS, 256), F32),
            pltpu.VMEM((ROWS, 1024), BF16),
        ]
        + reduce_scratch(DOWN_ROWS)
        + reduce_scratch(UP_ROWS)
        + [
            pltpu.VMEM((ROWS, HEAD), F32),
            pltpu.VMEM((ROWS, HEAD), F32),
            pltpu.VMEM((2 * RANK, ROWS), F32),
            pltpu.VMEM((3, 2 * RANK, ROWS), F32),
            pltpu.VMEM((BACK + 1, RANK, ROWS), BF16),
            pltpu.VMEM((SLAB, ROWS), BF16),
            pltpu.VMEM((SPAN, KVCOLS), BF16),
            pltpu.VMEM((SPAN, KVCOLS), BF16),
            pltpu.VMEM((ROWS, KVCOLS), BF16),
            pltpu.VMEM((ROWS, KVCOLS), BF16),
            pltpu.VMEM((4, ROWS, 256), BF16),
            pltpu.VMEM((ROWS, HEAD), BF16),
            pltpu.VMEM((SPAN, HEAD), BF16),
            pltpu.VMEM((4 * QT, 2 * HEAD), BF16),
            pltpu.VMEM((4 * QT, HEAD), F32),
            pltpu.VMEM((AHEAD, 4 * QT, HEAD), F32),
        ]
        + [pltpu.VMEM((4 * QT, HEAD), F32)] * 2
        + [
            dma((4,)), dma((8,)), dma((6,)),
            *[dma((COPIES,))] * 4,
            dma((3,)), dma((3,)), dma((4 * PARTS,)), dma((4 * PARTS,)), *[dma((PARTS,))] * 5,
            dma((4,)), dma((4,)), dma((4,)), dma((4,)),
        ],
        compiler_params=pltpu.CompilerParams(
            collective_id=0, has_side_effects=True, vmem_limit_bytes=60 * 1024 * 1024
        ),
        name="block",
    )(lengths, tid, slots, x, gain, wq, wk, wv, qd, vd, qu, vu)


def body(
    layer_input, input_norm_gain, query_weight, key_weight, value_weight,
    query_down_maps, value_down_maps, query_up_maps, value_up_maps,
    tenant_prompt_length, tenant_adapter_id, adapter_storage_slot,
):
    return block(
        layer_input, input_norm_gain.reshape(1, WIDTH), query_weight, key_weight, value_weight,
        query_down_maps, value_down_maps, query_up_maps, value_up_maps,
        tenant_prompt_length, tenant_adapter_id, adapter_storage_slot,
    )


def solution(mesh):
    placed = (
        P("tok", None), P(), P(None, "mlp"), P(None, "mlp"), P(None, "mlp"),
        P("tok", None, "mlp"), P("tok", None, "mlp"), P("tok", None, "mlp"), P("tok", None, "mlp"),
        P(), P(), P(),
    )
    return jax.shard_map(
        body, mesh=mesh, in_specs=placed, out_specs=P("tok", "mlp"), check_vma=False
    )
```

```python
import functools

import jax
import jax.numpy as jnp
import numpy as np
from jax import lax
from jax.experimental import pallas as pl
from jax.experimental.pallas import tpu as pltpu
from jax.sharding import PartitionSpec as P

WIDTH = 4096
HEAD = 128
RANK = 16
TENANTS = 16
ROWS = 512
HELD = 8
QCOLS = 1024
KVCOLS = 256
BACK = 4
N_TOK = 32
SIDE = 4
NORM_EPS = 1e-05
ROPE_BASE = 500000.0
ADAPTER_SCALE = 0.5
MESH = pl.DeviceIdType.MESH
F32 = jnp.float32
BF16 = jnp.bfloat16
SLAB = TENANTS * RANK
DOWN_ROWS = 2 * 1024 // 128 * SLAB
UP_ROWS = (QCOLS + KVCOLS) // 128 * SLAB
AHEAD = 3
NORM_STEP = 32
SPAN = (BACK + 1) * ROWS
FAR = 1e30
QT = 256
KC = 1152
CHUNKS = (BACK * ROWS + QT) // KC
UNITS = 4
SCALE = np.float32(HEAD**-0.5 * np.log2(np.e))
COPIES = 11
PARTS = 4


def prompt_bounds(len_ref):
    starts, ends = [], []
    at = jnp.int32(0)
    for t in range(TENANTS):
        starts.append(at)
        at = at + len_ref[t]
        ends.append(at)
    return starts, ends


class AllReduce:
    def __init__(self, place, rows, mine, from_core, from_a, from_b, full, send, recv):
        self.place, self.rows = place, rows
        self.mine, self.from_core, self.from_a, self.from_b = mine, from_core, from_a, from_b
        self.full, self.send, self.recv = full, send, recv
        p = place
        half, quarter = rows // 2, rows // 8
        self.half_at = pl.multiple_of(p["core"] * half, 16)
        self.other_at = pl.multiple_of((1 - p["core"]) * half, 16)
        self.a_at = pl.multiple_of(p["core"] * half + p["ca"] * quarter, 16)

    def copy(self, slot, src, dst, dev):
        return pltpu.make_async_remote_copy(
            src_ref=src, dst_ref=dst, send_sem=self.send.at[slot], recv_sem=self.recv.at[slot],
            device_id=dev, device_id_type=MESH,
        )

    def copies(self, stage):
        p = self.place
        half, quarter = self.rows // 2, self.rows // 8
        if stage == 0:
            return [self.copy(0, self.mine.at[pl.ds(self.other_at, half)], self.from_core, p["sib"])]
        if stage == 4:
            ref = self.full.at[pl.ds(self.half_at, half)]
            return [self.copy(10, ref, ref, p["sib"])]
        out = []
        for k in range(1, SIDE):
            if stage == 1:
                a = (p["ca"] + k) % SIDE
                at = pl.multiple_of(p["core"] * half + a * quarter, 16)
                out.append(self.copy(k, self.mine.at[pl.ds(at, quarter)], self.from_a.at[k - 1], p["peer_a"][k]))
            if stage == 2:
                ref = self.mine.at[pl.ds(self.a_at, quarter)]
                out.append(self.copy(3 + k, ref, self.from_b.at[k - 1], p["peer_b"][k]))
            if stage == 3:
                ref = self.full.at[pl.ds(self.a_at, quarter)]
                out.append(self.copy(6 + k, ref, ref, p["peer_a"][k]))
        return out

    def start(self, stage):
        for c in self.copies(stage):
            c.start()

    def arrive(self, stage):
        for c in self.copies(stage):
            c.wait()
        half, quarter = self.rows // 2, self.rows // 8
        if stage == 0:
            at = pl.ds(self.half_at, half)
            self.mine[at, :] = self.mine[at, :] + self.from_core[...]
        if stage == 1:
            at = pl.ds(self.a_at, quarter)
            self.mine[at, :] = (self.mine[at, :] + self.from_a[0]) + (self.from_a[1] + self.from_a[2])
        if stage == 2:
            at = pl.ds(self.a_at, quarter)
            self.full[at, :] = (self.mine[at, :] + self.from_b[0]) + (self.from_b[1] + self.from_b[2])

    def step(self, stage):
        self.arrive(stage)
        self.start(stage + 1)


def block_kernel(
    len_ref, tid_ref, table_ref,
    x_hbm, gain_hbm, wq_hbm, wk_hbm, wv_hbm, qd_hbm, vd_hbm, qu_hbm, vu_hbm,
    out_hbm,
    out, gain_ref, base, quarter,
    mine_d, core_d, a_d, b_d, down,
    mine_u, core_u, a_u, b_u, up,
    cosine, sine, fold, got, shrunk_v, spread, k_win, v_win, passing, turning, q_own,
    q_mark, k_mark, marked, highest, peak, sums, mixed,
    ad_sem, x_sem, w_sem, sd, rd, su, ru, gain_sem, out_sem, z_send, z_recv, kv_send, kv_recv, pass_send, pass_recv, turn_send, turn_recv, turned, share_send, share_recv, s_send, s_recv,
):
    me = lax.axis_index("tok")
    z = lax.axis_index("mlp")
    core = lax.rem(me, 2)
    chip = me // 2
    px, py = lax.rem(chip, SIDE), chip // SIDE

    def tok_of(yy, xx, cc):
        return (yy * SIDE + xx) * 2 + cc

    sib = (me + 1 - 2 * core, z)
    x_first = 1 - core
    ca = px * x_first + py * (1 - x_first)
    cb = py * x_first + px * (1 - x_first)
    peer_a, peer_b, peer_z = {}, {}, {}
    for k in range(1, SIDE):
        xk, yk = (px + k) % SIDE, (py + k) % SIDE
        along_x = tok_of(py, xk, core)
        along_y = tok_of(yk, px, core)
        peer_a[k] = (along_x * x_first + along_y * (1 - x_first), z)
        peer_b[k] = (along_y * x_first + along_x * (1 - x_first), z)
        peer_z[k] = (me, (z + k) % SIDE)
    later = {k: ((me + k) % N_TOK, z) for k in range(1, BACK + 1)}
    earlier = {k: ((me + N_TOK - k) % N_TOK, z) for k in range(1, BACK + 1)}
    place = dict(core=core, ca=ca, cb=cb, sib=sib, peer_a=peer_a, peer_b=peer_b)

    barrier = pltpu.get_barrier_semaphore()
    over = (tok_of((py + px // 2) % SIDE, (px + 3) % SIDE, core), z)
    goal = (tok_of(py, (px + 3) % SIDE, core), z)
    under_x = (px + 1) % SIDE
    under = (tok_of((py + SIDE - under_x // 2) % SIDE, under_x, core), z)
    greeted = [sib, over, under] + [d[k] for d in (peer_a, peer_b, peer_z) for k in range(1, SIDE)]
    greeted += [d[k] for d in (later, earlier) for k in range(1, BACK + 1)]
    for dev in greeted:
        pl.semaphore_signal(barrier, inc=1, device_id=dev, device_id_type=MESH)

    starts, ends = prompt_bounds(len_ref)
    red_d = AllReduce(place, DOWN_ROWS, mine_d, core_d, a_d, b_d, down, sd, rd)
    red_u = AllReduce(place, UP_ROWS, mine_u, core_u, a_u, b_u, up, su, ru)

    def angles(i, carry):
        row = pl.multiple_of(i * 64, 64)
        token = me * ROWS + row + lax.broadcasted_iota(jnp.int32, (64, HEAD), 0)
        begin = jnp.zeros((64, HEAD), jnp.int32)
        for t in range(TENANTS):
            begin = jnp.where(token >= starts[t], starts[t], begin)
        lane = lax.broadcasted_iota(jnp.int32, (64, HEAD), 1)
        pair = jnp.where(lane >= HEAD // 2, lane - HEAD // 2, lane)
        inverse = jnp.exp(-(pair.astype(F32) * (2.0 / HEAD)) * np.float32(np.log(np.float32(ROPE_BASE))))
        angle = (token - begin).astype(F32) * inverse
        cosine[pl.ds(row, 64), :] = jnp.cos(angle)
        s = jnp.sin(angle)
        sine[pl.ds(row, 64), :] = jnp.where(lane >= HEAD // 2, s, -s)
        return carry


    def rope(block):
        return block * cosine[...] + pltpu.roll(block, HEAD // 2, 1) * sine[...]

    def rows_of(win, block, part, parts):
        size = ROWS // parts
        return win.at[pl.ds(pl.multiple_of(block * ROWS + part * size, size), size)]

    def win_copy(win, which, slot, part):
        at = (2 * which + slot) * PARTS + part
        if which == 0 or slot == 0:
            src, dst = rows_of(win, BACK - 2 * slot, part, PARTS), rows_of(win, 2 - 2 * slot, part, PARTS)
            dev = later[2]
        else:
            src, dst = rows_of(passing, 0, part, PARTS), rows_of(win, 0, part, PARTS)
            dev = goal
        return pltpu.make_async_remote_copy(
            src_ref=src, dst_ref=dst, send_sem=kv_send.at[at], recv_sem=kv_recv.at[at],
            device_id=dev, device_id_type=MESH,
        )

    def pass_copy(part):
        return pltpu.make_async_remote_copy(
            src_ref=rows_of(v_win, BACK, part, PARTS), dst_ref=rows_of(passing, 0, part, PARTS),
            send_sem=pass_send.at[part], recv_sem=pass_recv.at[part], device_id=over, device_id_type=MESH,
        )

    at_turn = px == SIDE - 1
    below = (tok_of((py + 1) % SIDE, px, core), z)
    row_start = (tok_of(py, 0, core), z)

    def turn_copy(part):
        return pltpu.make_async_remote_copy(
            src_ref=rows_of(v_win, BACK, part, PARTS), dst_ref=rows_of(turning, 0, part, PARTS),
            send_sem=turn_send.at[part], recv_sem=turn_recv.at[part], device_id=below, device_id_type=MESH,
        )

    def turned_copy(part):
        return pltpu.make_async_remote_copy(
            src_ref=rows_of(turning, 0, part, PARTS), dst_ref=rows_of(v_win, 2, part, PARTS),
            send_sem=turned.at[part], recv_sem=kv_recv.at[2 * PARTS + part], device_id=row_start,
            device_id_type=MESH,
        )

    def share_copy(win, which, slot):
        src, dst = (4 - 2 * core, 3) if slot == 0 else (2 - 2 * core, 1)
        at = 2 * which + slot
        return pltpu.make_async_remote_copy(
            src_ref=rows_of(win, src, 0, 1), dst_ref=rows_of(win, dst, 0, 1),
            send_sem=share_send.at[at], recv_sem=share_recv.at[at], device_id=sib, device_id_type=MESH,
        )

    def table(full, first, slabs):
        return jnp.concatenate([full[(first + s) * SLAB : (first + s + 1) * SLAB, :] for s in range(slabs)], axis=1)

    def members(first):
        token = first + lax.broadcasted_iota(jnp.int32, (RANK, ROWS), 1)
        return [jnp.logical_and(token >= starts[t], token < ends[t]) for t in range(TENANTS)]

    def z_copies():
        return [
            pltpu.make_async_remote_copy(
                src_ref=fold, dst_ref=got.at[k - 1], send_sem=z_send.at[k - 1], recv_sem=z_recv.at[k - 1],
                device_id=peer_z[k], device_id_type=MESH,
            )
            for k in range(1, SIDE)
        ]

    def shrunk_copies():
        return [
            pltpu.make_async_remote_copy(
                src_ref=shrunk_v.at[BACK], dst_ref=shrunk_v.at[BACK - k], send_sem=s_send.at[k - 1],
                recv_sem=s_recv.at[k - 1], device_id=later[k], device_id_type=MESH,
            )
            for k in range(1, BACK + 1)
        ]

    def shrink():
        maps = jnp.concatenate([table(down, 0, 8), table(down, 8, 8)], axis=0)
        part = lax.dot_general(maps, quarter[...], (((1,), (1,)), ((), ())), preferred_element_type=F32)
        mask = members(me * ROWS)
        for i in range(2):
            total = jnp.zeros((RANK, ROWS), F32)
            for t in range(TENANTS):
                row = i * SLAB + t * RANK
                total = total + jnp.where(mask[t], part[row : row + RANK, :], 0.0)
            fold[i * RANK : (i + 1) * RANK, :] = total
        for c in z_copies():
            c.start()

    def shrunk():
        for c in z_copies():
            c.wait()
        total = ((fold[...] + got[0]) + (got[1] + got[2])).astype(BF16)
        shrunk_v[BACK] = total[RANK:, :]
        for c in shrunk_copies():
            c.start()
        spread_out(total[:RANK, :].astype(F32), me * ROWS)

    def step(reduction, stage):
        return lambda: reduction.step(stage)

    def spread_out(values, first):
        mask = members(first)
        for t in range(TENANTS):
            spread[t * RANK : (t + 1) * RANK, :] = jnp.where(mask[t], values, 0.0).astype(BF16)

    def keys():
        for h in range(2):
            cols = slice(h * HEAD, (h + 1) * HEAD)
            k_win[BACK * ROWS :, cols] = rope(base[0, :, cols]).astype(BF16)

    def values():
        v_win[BACK * ROWS :, :] = base[1].astype(BF16)

    def send(win, which, slot, *parts):
        def act():
            for part in parts:
                win_copy(win, which, slot, part).start()

        return act

    def send_k(*parts):
        return send(k_win, 0, 0, *parts)

    def send_v(*parts):
        def act():
            @pl.when(jnp.logical_not(at_turn))
            def _():
                send(v_win, 1, 0, *parts)()

        return act

    def turn_v(*parts):
        def act():
            @pl.when(at_turn)
            def _():
                for part in parts:
                    turn_copy(part).start()

        return act

    def after_turn(*parts):
        def act():
            @pl.when(at_turn)
            def _():
                for part in parts:
                    turn_copy(part).wait()
                    turned_copy(part).start()

        return act

    def forward_k(*parts):
        def act():
            for part in parts:
                win_copy(k_win, 0, 0, part).wait()
                win_copy(k_win, 0, 1, part).start()

        return act

    def pass_v(*parts):
        def act():
            for part in parts:
                pass_copy(part).start()

        return act

    def forward_v(*parts):
        def act():
            for part in parts:
                pass_copy(part).wait()
                win_copy(v_win, 1, 1, part).start()

        return act

    def share(win, which, slot):
        for part in range(PARTS):
            if which == 1 and slot == 0:
                win_copy(win, which, slot, part).wait_recv()

                @pl.when(at_turn)
                def _(part=part):
                    turned_copy(part).wait_send()

                @pl.when(jnp.logical_not(at_turn))
                def _(part=part):
                    win_copy(win, which, slot, part).wait_send()

            elif which or slot:
                win_copy(win, which, slot, part).wait()
        share_copy(win, which, slot).start()

    def query(j, carry):
        cols = jnp.concatenate(
            [up[pl.ds(pl.multiple_of((2 * j + s) * SLAB, SLAB), SLAB), :] for s in range(2)], axis=1
        )
        delta = lax.dot_general(spread[...], cols, (((0,), (0,)), ((), ())), preferred_element_type=F32)
        rows = base[2 + j] + ADAPTER_SCALE * delta
        q_own[j] = jnp.concatenate([rope(rows[:, :HEAD]), rope(rows[:, HEAD:])], axis=1).astype(BF16)
        return carry

    def value(i, carry):
        at = pl.ds(pl.multiple_of(i * ROWS, ROWS), ROWS)
        spread_out(shrunk_v[i].astype(F32), (me - BACK + i) * ROWS)
        delta = lax.dot_general(
            spread[...], table(up, 8, 2), (((0,), (0,)), ((), ())), preferred_element_type=F32
        )
        own = jnp.where(i == BACK, base[1], v_win[at, :].astype(F32))
        v_win[at, :] = (own + ADAPTER_SCALE * delta).astype(BF16)
        return carry

    def wait_keys():
        for slot in range(2):
            share(k_win, 0, slot)
        for slot in range(2):
            share_copy(k_win, 0, slot).wait()

    def wait_values():
        for slot in range(2):
            share(v_win, 1, slot)
        for slot in range(2):
            share_copy(v_win, 1, slot).wait()
        for c in shrunk_copies():
            c.wait()
        lax.fori_loop(0, BACK + 1, value, 0)

    def write(u):
        group, part = u // 2, u % 2
        at = (pl.ds(pl.multiple_of(part * QT, QT), QT), pl.ds(pl.multiple_of(group * 512, 512), 512))
        return pltpu.make_async_copy(out.at[at], out_hbm.at[at], out_sem.at[u])

    def last_part(scores):
        wait_keys()

        def ahead(u, carry):
            score(u, q_own, k_win, q_mark, k_mark, marked, scores, highest, peak)
            return carry

        lax.fori_loop(0, AHEAD, ahead, 0)
        wait_values()

        def behind(u, carry):
            mix(u, v_win, out, scores, peak, sums, mixed)
            write(u).start()

            @pl.when(u + AHEAD < UNITS)
            def _():
                score(u + AHEAD, q_own, k_win, q_mark, k_mark, marked, scores, highest, peak)

            return carry

        lax.fori_loop(0, UNITS, behind, 0)
        for u in range(UNITS):
            write(u).wait()

    def first_part(x, normed, w, qd, vd, qu, vu):
        loads = [
            pltpu.make_async_copy(src, dst, ad_sem.at[i])
            for i, (src, dst) in enumerate([(qd_hbm, qd), (vd_hbm, vd), (qu_hbm, qu), (vu_hbm, vu)])
        ]
        for c in loads:
            c.start()
        x_loads = [
            pltpu.make_async_copy(x_hbm.at[pl.ds(64 * i, 64)], x.at[pl.ds(64 * i, 64)], x_sem.at[i])
            for i in range(8)
        ]
        gain_load = pltpu.make_async_copy(gain_hbm, gain_ref, gain_sem.at[0])
        gain_load.start()
        for c in x_loads:
            c.start()
        w_loads = [
            pltpu.make_async_copy(wk_hbm, w.at[0], w_sem.at[0]),
            pltpu.make_async_copy(wv_hbm, w.at[1], w_sem.at[1]),
        ] + [
            pltpu.make_async_copy(wq_hbm.at[:, pl.ds(256 * i, 256)], w.at[2 + i], w_sem.at[2 + i])
            for i in range(4)
        ]
        for c in w_loads:
            c.start()


        def gather(target, pieces):
            def one(t, carry):
                local = table_ref[tid_ref[t]] - me * HELD
                held = jnp.logical_and(local >= 0, local < HELD)
                at = jnp.clip(local, 0, HELD - 1)
                for stored, first, slabs in pieces:
                    for s in range(slabs):
                        tile = stored[at, :, s * 128 : (s + 1) * 128]
                        row = pl.multiple_of((first + s) * SLAB + t * RANK, RANK)
                        target[pl.ds(row, RANK), :] = jnp.where(held, tile, jnp.zeros_like(tile))
                return carry

            lax.fori_loop(0, TENANTS, one, 0)


        for c in loads[:2]:
            c.wait()
        gather(mine_d, [(qd, 0, 8), (vd, 8, 8)])
        lax.fori_loop(0, 8, angles, 0)
        marks(starts, ends, me, q_mark, k_mark)
        pl.semaphore_wait(barrier, len(greeted))
        red_d.start(0)
        for c in loads[2:]:
            c.wait()
        gather(mine_u, [(qu, 0, 8), (vu, 8, 2)])
        red_u.start(0)

        def normalise(first, count):
            def one(i, carry):
                at = pl.ds(pl.multiple_of(i * NORM_STEP, NORM_STEP), NORM_STEP)
                wide = x[at, :].astype(F32)
                scale = lax.rsqrt(jnp.mean(wide * wide, axis=1, keepdims=True) + NORM_EPS)
                normed[at, :] = (wide * scale * gain_ref[...]).astype(BF16)
                return carry

            lax.fori_loop(first, first + count, one, 0)


        red_d.step(0)
        gain_load.wait()
        for i in range(4):
            x_loads[i].wait()
        normalise(0, 8)
        for i in range(4, 8):
            x_loads[i].wait()
        normalise(8, 8)
        quarter[...] = normed[:, pl.ds(pl.multiple_of(z * 1024, 1024), 1024)]
        red_u.step(0)

        def product(j):
            w_loads_j = pltpu.make_async_copy(wk_hbm, w.at[j], w_sem.at[j])
            w_loads_j.wait()
            base[j] = jnp.dot(normed[...], w[j], preferred_element_type=F32)


        plan = [
            [keys, step(red_d, 1), send_k(0, 1)],
            [values, turn_v(0, 1), send_k(2, 3)],
            [step(red_d, 2), step(red_u, 1), pass_v(0, 1), turn_v(2, 3)],
            [pass_v(2, 3)],
            [step(red_d, 3), step(red_u, 2), forward_k(0, 1, 2, 3), after_turn(0, 1)],
            [forward_v(0, 1), send_v(0, 1, 2, 3), after_turn(2, 3)],
        ]

        def work(j, carry):
            product(j)
            for at, acts in enumerate(plan):

                @pl.when(j == at)
                def _(acts=acts):
                    for act in acts:
                        act()

            return carry

        lax.fori_loop(0, 6, work, 0)
        red_d.arrive(4)
        shrink()
        red_u.step(3)
        forward_v(2, 3)()
        shrunk()
        red_u.arrive(4)
        lax.fori_loop(0, 4, query, 0)

    pl.run_scoped(
        first_part,
        pltpu.VMEM((ROWS, WIDTH), BF16),
        pltpu.VMEM((ROWS, WIDTH), BF16),
        pltpu.VMEM((6, WIDTH, 256), BF16),
        pltpu.VMEM((HELD, RANK, 1024), BF16),
        pltpu.VMEM((HELD, RANK, 1024), BF16),
        pltpu.VMEM((HELD, RANK, QCOLS), BF16),
        pltpu.VMEM((HELD, RANK, KVCOLS), BF16),
    )
    pl.run_scoped(last_part, pltpu.VMEM((AHEAD, CHUNKS, 4 * QT, KC), F32))


def marks(starts, ends, me, q_mark, k_mark):
    lane = lax.broadcasted_iota(jnp.int32, (1, HEAD), 1)
    begin = jnp.full((1, HEAD), 2**30, jnp.int32)
    end = jnp.full((1, HEAD), 2**30, jnp.int32)
    for t in range(TENANTS):
        begin = jnp.where(lane == t, starts[t], begin)
        end = jnp.where(lane == t, ends[t], end)
    begin = jnp.where(lane == TENANTS, -(2**30), begin)
    end = jnp.where(lane == TENANTS, 0, end)

    def inside(first, row):
        token = first + row + lax.broadcasted_iota(jnp.int32, (128, HEAD), 0)
        return jnp.logical_and(token >= begin, token < end)

    def keys(i, carry):
        row = pl.multiple_of(i * 128, 128)
        k_mark[pl.ds(row, 128), :] = jnp.where(inside((me - BACK) * ROWS, row), 1.0, 0.0).astype(BF16)
        return carry

    lax.fori_loop(0, SPAN // 128, keys, 0)

    def queries(i, carry):
        row = pl.multiple_of(i * 128, 128)
        open_to = jnp.logical_or(inside(me * ROWS, row), lane > TENANTS)
        q_mark[pl.ds(row, 128), :] = jnp.where(open_to, 0.0, -FAR).astype(BF16)
        return carry

    lax.fori_loop(0, ROWS // 128, queries, 0)


def unit_of(u):
    group, part = u // 2, lax.rem(u, 2)
    rows = pl.ds(pl.multiple_of(part * QT, QT), QT)
    head_cols = pl.ds(pl.multiple_of(group * HEAD, HEAD), HEAD)
    return group, part, rows, head_cols


def score(u, q_ref, k_win, q_mark, k_mark, marked, scores, highest, peak):
    group, part, rows, head_cols = unit_of(u)
    slot = lax.rem(u, AHEAD)
    for h in range(4):
        marked[h * QT : (h + 1) * QT, :HEAD] = q_ref[
            2 * group + h // 2, rows, (h % 2) * HEAD : (h % 2 + 1) * HEAD
        ]
        marked[h * QT : (h + 1) * QT, HEAD:] = q_mark[rows, :]
    for i in range(CHUNKS):
        at = pl.multiple_of(part * QT + i * KC, 128)
        keys = jnp.concatenate([k_win[pl.ds(at, KC), head_cols], k_mark[pl.ds(at, KC), :]], axis=1)
        s = lax.dot_general(marked[...], keys, (((1,), (1,)), ((), ())), preferred_element_type=F32) * SCALE
        if i == CHUNKS - 1:
            seen = lax.broadcasted_iota(jnp.int32, (QT, QT), 0) >= lax.broadcasted_iota(jnp.int32, (QT, QT), 1)
            tail = s[:, KC - QT :]
            tail = jnp.concatenate(
                [jnp.where(seen, tail[h * QT : (h + 1) * QT, :], -FAR) for h in range(4)], axis=0
            )
            s = jnp.concatenate([s[:, : KC - QT], tail], axis=1)
        scores[slot, i] = s
        top = s[:, :128]
        for c in range(1, KC // 128):
            top = jnp.maximum(top, s[:, c * 128 : (c + 1) * 128])
        highest[...] = top if i == 0 else jnp.maximum(highest[...], top)
    peak[slot] = jnp.broadcast_to(jnp.max(highest[...], axis=1, keepdims=True), highest.shape)


def mix(u, v_win, out, scores, peak, sums, mixed):
    group, part, rows, head_cols = unit_of(u)
    slot = lax.rem(u, AHEAD)
    for i in range(CHUNKS):
        at = pl.multiple_of(part * QT + i * KC, 128)
        s = scores[slot, i]
        top = peak[slot]
        ps = [jnp.exp2(s[:, c * 128 : (c + 1) * 128] - top) for c in range(KC // 128)]
        total = ps[0]
        for p in ps[1:]:
            total = total + p
        probs = jnp.concatenate([p.astype(BF16) for p in ps], axis=1)
        product = jnp.dot(probs, v_win[pl.ds(at, KC), head_cols], preferred_element_type=F32)
        sums[...] = total if i == 0 else sums[...] + total
        mixed[...] = product if i == 0 else mixed[...] + product
    result = mixed[...] / jnp.sum(sums[...], axis=1, keepdims=True)
    for h in range(4):
        cols = pl.ds(pl.multiple_of(group * 512 + h * HEAD, HEAD), HEAD)
        out[rows, cols] = result[h * QT : (h + 1) * QT, :].astype(BF16)


def block(x, gain, wq, wk, wv, qd, vd, qu, vu, lengths, tid, slots):
    any_space = pl.BlockSpec(memory_space=pl.ANY)
    smem = pl.BlockSpec(memory_space=pltpu.SMEM)
    dma = pltpu.SemaphoreType.DMA

    def reduce_scratch(rows):
        return [
            pltpu.VMEM((rows, 128), BF16),
            pltpu.VMEM((rows // 2, 128), BF16),
            pltpu.VMEM((3, rows // 8, 128), BF16),
            pltpu.VMEM((3, rows // 8, 128), BF16),
            pltpu.VMEM((rows, 128), BF16),
        ]

    return pl.pallas_call(
        block_kernel,
        out_shape=jax.ShapeDtypeStruct((ROWS, QCOLS), BF16),
        in_specs=[smem] * 3 + [any_space] * 9,
        out_specs=any_space,
        scratch_shapes=[
            pltpu.VMEM((ROWS, QCOLS), BF16),
            pltpu.VMEM((1, WIDTH), F32),
            pltpu.VMEM((6, ROWS, 256), F32),
            pltpu.VMEM((ROWS, 1024), BF16),
        ]
        + reduce_scratch(DOWN_ROWS)
        + reduce_scratch(UP_ROWS)
        + [
            pltpu.VMEM((ROWS, HEAD), F32),
            pltpu.VMEM((ROWS, HEAD), F32),
            pltpu.VMEM((2 * RANK, ROWS), F32),
            pltpu.VMEM((3, 2 * RANK, ROWS), F32),
            pltpu.VMEM((BACK + 1, RANK, ROWS), BF16),
            pltpu.VMEM((SLAB, ROWS), BF16),
            pltpu.VMEM((SPAN, KVCOLS), BF16),
            pltpu.VMEM((SPAN, KVCOLS), BF16),
            pltpu.VMEM((ROWS, KVCOLS), BF16),
            pltpu.VMEM((ROWS, KVCOLS), BF16),
            pltpu.VMEM((4, ROWS, 256), BF16),
            pltpu.VMEM((ROWS, HEAD), BF16),
            pltpu.VMEM((SPAN, HEAD), BF16),
            pltpu.VMEM((4 * QT, 2 * HEAD), BF16),
            pltpu.VMEM((4 * QT, HEAD), F32),
            pltpu.VMEM((AHEAD, 4 * QT, HEAD), F32),
        ]
        + [pltpu.VMEM((4 * QT, HEAD), F32)] * 2
        + [
            dma((4,)), dma((8,)), dma((6,)),
            *[dma((COPIES,))] * 4,
            dma((1,)), dma((UNITS,)), dma((3,)), dma((3,)), dma((4 * PARTS,)), dma((4 * PARTS,)), *[dma((PARTS,))] * 5,
            dma((4,)), dma((4,)), dma((4,)), dma((4,)),
        ],
        compiler_params=pltpu.CompilerParams(
            collective_id=0, has_side_effects=True, vmem_limit_bytes=60 * 1024 * 1024
        ),
        name="block",
    )(lengths, tid, slots, x, gain, wq, wk, wv, qd, vd, qu, vu)


def body(
    layer_input, input_norm_gain, query_weight, key_weight, value_weight,
    query_down_maps, value_down_maps, query_up_maps, value_up_maps,
    tenant_prompt_length, tenant_adapter_id, adapter_storage_slot,
):
    return block(
        layer_input, input_norm_gain.reshape(1, WIDTH), query_weight, key_weight, value_weight,
        query_down_maps, value_down_maps, query_up_maps, value_up_maps,
        tenant_prompt_length, tenant_adapter_id, adapter_storage_slot,
    )


def solution(mesh):
    placed = (
        P("tok", None), P(), P(None, "mlp"), P(None, "mlp"), P(None, "mlp"),
        P("tok", None, "mlp"), P("tok", None, "mlp"), P("tok", None, "mlp"), P("tok", None, "mlp"),
        P(), P(), P(),
    )
    return jax.shard_map(
        body, mesh=mesh, in_specs=placed, out_specs=P("tok", "mlp"), check_vma=False
    )
```

```python
import functools

import jax
import jax.numpy as jnp
import numpy as np
from jax import lax
from jax.experimental import pallas as pl
from jax.experimental.pallas import tpu as pltpu
from jax.sharding import PartitionSpec as P

WIDTH = 4096
HEAD = 128
RANK = 16
TENANTS = 16
ROWS = 512
HELD = 8
QCOLS = 1024
KVCOLS = 256
BACK = 4
N_TOK = 32
SIDE = 4
NORM_EPS = 1e-05
ROPE_BASE = 500000.0
ADAPTER_SCALE = 0.5
MESH = pl.DeviceIdType.MESH
F32 = jnp.float32
BF16 = jnp.bfloat16
SLAB = TENANTS * RANK
DOWN_ROWS = 2 * 1024 // 128 * SLAB
UP_ROWS = (QCOLS + KVCOLS) // 128 * SLAB
AHEAD = 3
NORM_STEP = 32
SPAN = (BACK + 1) * ROWS
FAR = 1e30
QT = 256
KC = 1152
CHUNKS = (BACK * ROWS + QT) // KC
UNITS = 4
SCALE = np.float32(HEAD**-0.5 * np.log2(np.e))
COPIES = 11
PARTS = 4


def prompt_bounds(len_ref):
    starts, ends = [], []
    at = jnp.int32(0)
    for t in range(TENANTS):
        starts.append(at)
        at = at + len_ref[t]
        ends.append(at)
    return starts, ends


class AllReduce:
    def __init__(self, place, rows, mine, from_core, from_a, from_b, full, send, recv):
        self.place, self.rows = place, rows
        self.mine, self.from_core, self.from_a, self.from_b = mine, from_core, from_a, from_b
        self.full, self.send, self.recv = full, send, recv
        p = place
        half, quarter = rows // 2, rows // 8
        self.half_at = pl.multiple_of(p["core"] * half, 16)
        self.other_at = pl.multiple_of((1 - p["core"]) * half, 16)
        self.a_at = pl.multiple_of(p["core"] * half + p["ca"] * quarter, 16)

    def copy(self, slot, src, dst, dev):
        return pltpu.make_async_remote_copy(
            src_ref=src, dst_ref=dst, send_sem=self.send.at[slot], recv_sem=self.recv.at[slot],
            device_id=dev, device_id_type=MESH,
        )

    def copies(self, stage):
        p = self.place
        half, quarter = self.rows // 2, self.rows // 8
        if stage == 0:
            return [self.copy(0, self.mine.at[pl.ds(self.other_at, half)], self.from_core, p["sib"])]
        if stage == 4:
            ref = self.full.at[pl.ds(self.half_at, half)]
            return [self.copy(10, ref, ref, p["sib"])]
        out = []
        for k in range(1, SIDE):
            if stage == 1:
                a = (p["ca"] + k) % SIDE
                at = pl.multiple_of(p["core"] * half + a * quarter, 16)
                out.append(self.copy(k, self.mine.at[pl.ds(at, quarter)], self.from_a.at[k - 1], p["peer_a"][k]))
            if stage == 2:
                ref = self.mine.at[pl.ds(self.a_at, quarter)]
                out.append(self.copy(3 + k, ref, self.from_b.at[k - 1], p["peer_b"][k]))
            if stage == 3:
                ref = self.full.at[pl.ds(self.a_at, quarter)]
                out.append(self.copy(6 + k, ref, ref, p["peer_a"][k]))
        return out

    def start(self, stage):
        for c in self.copies(stage):
            c.start()

    def arrive(self, stage):
        for c in self.copies(stage):
            c.wait()
        half, quarter = self.rows // 2, self.rows // 8
        if stage == 0:
            at = pl.ds(self.half_at, half)
            self.mine[at, :] = self.mine[at, :] + self.from_core[...]
        if stage == 1:
            at = pl.ds(self.a_at, quarter)
            self.mine[at, :] = (self.mine[at, :] + self.from_a[0]) + (self.from_a[1] + self.from_a[2])
        if stage == 2:
            at = pl.ds(self.a_at, quarter)
            self.full[at, :] = (self.mine[at, :] + self.from_b[0]) + (self.from_b[1] + self.from_b[2])

    def step(self, stage):
        self.arrive(stage)
        self.start(stage + 1)


def block_kernel(
    len_ref, tid_ref, table_ref,
    x_hbm, gain_hbm, wq_hbm, wk_hbm, wv_hbm, qd_hbm, vd_hbm, qu_hbm, vu_hbm,
    out_hbm,
    out, gain_ref, base, quarter,
    mine_d, core_d, a_d, b_d, down,
    mine_u, core_u, a_u, b_u, up,
    cosine, sine, fold, got, shrunk_v, spread, k_win, v_win, passing, turning, q_own,
    q_mark, k_mark, marked, highest, peak, sums, mixed,
    ad_sem, x_sem, w_sem, sd, rd, su, ru, gain_sem, out_sem, z_send, z_recv, kv_send, kv_recv, pass_send, pass_recv, turn_send, turn_recv, turned, share_send, share_recv, s_send, s_recv,
):
    me = lax.axis_index("tok")
    z = lax.axis_index("mlp")
    core = lax.rem(me, 2)
    chip = me // 2
    px, py = lax.rem(chip, SIDE), chip // SIDE

    def tok_of(yy, xx, cc):
        return (yy * SIDE + xx) * 2 + cc

    sib = (me + 1 - 2 * core, z)
    x_first = 1 - core
    ca = px * x_first + py * (1 - x_first)
    cb = py * x_first + px * (1 - x_first)
    peer_a, peer_b, peer_z = {}, {}, {}
    for k in range(1, SIDE):
        xk, yk = (px + k) % SIDE, (py + k) % SIDE
        along_x = tok_of(py, xk, core)
        along_y = tok_of(yk, px, core)
        peer_a[k] = (along_x * x_first + along_y * (1 - x_first), z)
        peer_b[k] = (along_y * x_first + along_x * (1 - x_first), z)
        peer_z[k] = (me, (z + k) % SIDE)
    later = {k: ((me + k) % N_TOK, z) for k in range(1, BACK + 1)}
    earlier = {k: ((me + N_TOK - k) % N_TOK, z) for k in range(1, BACK + 1)}
    place = dict(core=core, ca=ca, cb=cb, sib=sib, peer_a=peer_a, peer_b=peer_b)

    barrier = pltpu.get_barrier_semaphore()
    over = (tok_of((py + px // 2) % SIDE, (px + 3) % SIDE, core), z)
    goal = (tok_of(py, (px + 3) % SIDE, core), z)
    under_x = (px + 1) % SIDE
    under = (tok_of((py + SIDE - under_x // 2) % SIDE, under_x, core), z)
    greeted = [sib, over, under] + [d[k] for d in (peer_a, peer_b, peer_z) for k in range(1, SIDE)]
    greeted += [d[k] for d in (later, earlier) for k in range(1, BACK + 1)]
    for dev in greeted:
        pl.semaphore_signal(barrier, inc=1, device_id=dev, device_id_type=MESH)

    starts, ends = prompt_bounds(len_ref)
    red_d = AllReduce(place, DOWN_ROWS, mine_d, core_d, a_d, b_d, down, sd, rd)
    red_u = AllReduce(place, UP_ROWS, mine_u, core_u, a_u, b_u, up, su, ru)

    def angles(i, carry):
        row = pl.multiple_of(i * 64, 64)
        token = me * ROWS + row + lax.broadcasted_iota(jnp.int32, (64, HEAD), 0)
        begin = jnp.zeros((64, HEAD), jnp.int32)
        for t in range(TENANTS):
            begin = jnp.where(token >= starts[t], starts[t], begin)
        lane = lax.broadcasted_iota(jnp.int32, (64, HEAD), 1)
        pair = jnp.where(lane >= HEAD // 2, lane - HEAD // 2, lane)
        inverse = jnp.exp(-(pair.astype(F32) * (2.0 / HEAD)) * np.float32(np.log(np.float32(ROPE_BASE))))
        angle = (token - begin).astype(F32) * inverse
        cosine[pl.ds(row, 64), :] = jnp.cos(angle)
        s = jnp.sin(angle)
        sine[pl.ds(row, 64), :] = jnp.where(lane >= HEAD // 2, s, -s)
        return carry


    def rope(block):
        return block * cosine[...] + pltpu.roll(block, HEAD // 2, 1) * sine[...]

    def rows_of(win, block, part, parts):
        size = ROWS // parts
        return win.at[pl.ds(pl.multiple_of(block * ROWS + part * size, size), size)]

    def win_copy(win, which, slot, part):
        at = (2 * which + slot) * PARTS + part
        if which == 0 or slot == 0:
            src, dst = rows_of(win, BACK - 2 * slot, part, PARTS), rows_of(win, 2 - 2 * slot, part, PARTS)
            dev = later[2]
        else:
            src, dst = rows_of(passing, 0, part, PARTS), rows_of(win, 0, part, PARTS)
            dev = goal
        return pltpu.make_async_remote_copy(
            src_ref=src, dst_ref=dst, send_sem=kv_send.at[at], recv_sem=kv_recv.at[at],
            device_id=dev, device_id_type=MESH,
        )

    def pass_copy(part):
        return pltpu.make_async_remote_copy(
            src_ref=rows_of(v_win, BACK, part, PARTS), dst_ref=rows_of(passing, 0, part, PARTS),
            send_sem=pass_send.at[part], recv_sem=pass_recv.at[part], device_id=over, device_id_type=MESH,
        )

    at_turn = px == SIDE - 1
    below = (tok_of((py + 1) % SIDE, px, core), z)
    row_start = (tok_of(py, 0, core), z)

    def turn_copy(part):
        return pltpu.make_async_remote_copy(
            src_ref=rows_of(v_win, BACK, part, PARTS), dst_ref=rows_of(turning, 0, part, PARTS),
            send_sem=turn_send.at[part], recv_sem=turn_recv.at[part], device_id=below, device_id_type=MESH,
        )

    def turned_copy(part):
        return pltpu.make_async_remote_copy(
            src_ref=rows_of(turning, 0, part, PARTS), dst_ref=rows_of(v_win, 2, part, PARTS),
            send_sem=turned.at[part], recv_sem=kv_recv.at[2 * PARTS + part], device_id=row_start,
            device_id_type=MESH,
        )

    def share_copy(win, which, slot):
        src, dst = (4 - 2 * core, 3) if slot == 0 else (2 - 2 * core, 1)
        at = 2 * which + slot
        return pltpu.make_async_remote_copy(
            src_ref=rows_of(win, src, 0, 1), dst_ref=rows_of(win, dst, 0, 1),
            send_sem=share_send.at[at], recv_sem=share_recv.at[at], device_id=sib, device_id_type=MESH,
        )

    def table(full, first, slabs):
        return jnp.concatenate([full[(first + s) * SLAB : (first + s + 1) * SLAB, :] for s in range(slabs)], axis=1)

    def members(first):
        token = first + lax.broadcasted_iota(jnp.int32, (RANK, ROWS), 1)
        return [jnp.logical_and(token >= starts[t], token < ends[t]) for t in range(TENANTS)]

    def z_copies():
        return [
            pltpu.make_async_remote_copy(
                src_ref=fold, dst_ref=got.at[k - 1], send_sem=z_send.at[k - 1], recv_sem=z_recv.at[k - 1],
                device_id=peer_z[k], device_id_type=MESH,
            )
            for k in range(1, SIDE)
        ]

    def shrunk_copies():
        return [
            pltpu.make_async_remote_copy(
                src_ref=shrunk_v.at[BACK], dst_ref=shrunk_v.at[BACK - k], send_sem=s_send.at[k - 1],
                recv_sem=s_recv.at[k - 1], device_id=later[k], device_id_type=MESH,
            )
            for k in range(1, BACK + 1)
        ]

    def shrink():
        maps = jnp.concatenate([table(down, 0, 8), table(down, 8, 8)], axis=0)
        part = lax.dot_general(maps, quarter[...], (((1,), (1,)), ((), ())), preferred_element_type=F32)
        mask = members(me * ROWS)
        for i in range(2):
            total = jnp.zeros((RANK, ROWS), F32)
            for t in range(TENANTS):
                row = i * SLAB + t * RANK
                total = total + jnp.where(mask[t], part[row : row + RANK, :], 0.0)
            fold[i * RANK : (i + 1) * RANK, :] = total
        for c in z_copies():
            c.start()

    def shrunk():
        for c in z_copies():
            c.wait()
        total = ((fold[...] + got[0]) + (got[1] + got[2])).astype(BF16)
        shrunk_v[BACK] = total[RANK:, :]
        for c in shrunk_copies():
            c.start()
        spread_out(total[:RANK, :].astype(F32), me * ROWS)

    def step(reduction, stage):
        return lambda: reduction.step(stage)

    def spread_out(values, first):
        mask = members(first)
        for t in range(TENANTS):
            spread[t * RANK : (t + 1) * RANK, :] = jnp.where(mask[t], values, 0.0).astype(BF16)

    def keys():
        for h in range(2):
            cols = slice(h * HEAD, (h + 1) * HEAD)
            k_win[BACK * ROWS :, cols] = rope(base[0, :, cols]).astype(BF16)

    def values():
        v_win[BACK * ROWS :, :] = base[1].astype(BF16)

    def send(win, which, slot, *parts):
        def act():
            for part in parts:
                win_copy(win, which, slot, part).start()

        return act

    def send_k(*parts):
        return send(k_win, 0, 0, *parts)

    def send_v(*parts):
        def act():
            @pl.when(jnp.logical_not(at_turn))
            def _():
                send(v_win, 1, 0, *parts)()

        return act

    def turn_v(*parts):
        def act():
            @pl.when(at_turn)
            def _():
                for part in parts:
                    turn_copy(part).start()

        return act

    def after_turn(*parts):
        def act():
            @pl.when(at_turn)
            def _():
                for part in parts:
                    turn_copy(part).wait()
                    turned_copy(part).start()

        return act

    def forward_k(*parts):
        def act():
            for part in parts:
                win_copy(k_win, 0, 0, part).wait()
                win_copy(k_win, 0, 1, part).start()

        return act

    def pass_v(*parts):
        def act():
            for part in parts:
                pass_copy(part).start()

        return act

    def forward_v(*parts):
        def act():
            for part in parts:
                pass_copy(part).wait()
                win_copy(v_win, 1, 1, part).start()

        return act

    def share(win, which, slot):
        for part in range(PARTS):
            if which == 1 and slot == 0:
                win_copy(win, which, slot, part).wait_recv()

                @pl.when(at_turn)
                def _(part=part):
                    turned_copy(part).wait_send()

                @pl.when(jnp.logical_not(at_turn))
                def _(part=part):
                    win_copy(win, which, slot, part).wait_send()

            elif which or slot:
                win_copy(win, which, slot, part).wait()
        share_copy(win, which, slot).start()

    def query(j, carry):
        cols = jnp.concatenate(
            [up[pl.ds(pl.multiple_of((2 * j + s) * SLAB, SLAB), SLAB), :] for s in range(2)], axis=1
        )
        delta = lax.dot_general(spread[...], cols, (((0,), (0,)), ((), ())), preferred_element_type=F32)
        rows = base[2 + j] + ADAPTER_SCALE * delta
        q_own[j] = jnp.concatenate([rope(rows[:, :HEAD]), rope(rows[:, HEAD:])], axis=1).astype(BF16)
        return carry

    def value(i, carry):
        at = pl.ds(pl.multiple_of(i * ROWS, ROWS), ROWS)
        spread_out(shrunk_v[i].astype(F32), (me - BACK + i) * ROWS)
        delta = lax.dot_general(
            spread[...], table(up, 8, 2), (((0,), (0,)), ((), ())), preferred_element_type=F32
        )
        own = jnp.where(i == BACK, base[1], v_win[at, :].astype(F32))
        v_win[at, :] = (own + ADAPTER_SCALE * delta).astype(BF16)
        return carry

    def wait_keys():
        for slot in range(2):
            share_copy(k_win, 0, slot).wait()

    def wait_values():
        for slot in range(2):
            share_copy(v_win, 1, slot).wait()
        for c in shrunk_copies():
            c.wait()
        lax.fori_loop(0, BACK + 1, value, 0)

    def write(u):
        group, part = u // 2, u % 2
        at = (pl.ds(pl.multiple_of(part * QT, QT), QT), pl.ds(pl.multiple_of(group * 512, 512), 512))
        return pltpu.make_async_copy(out.at[at], out_hbm.at[at], out_sem.at[u])

    def last_part(scores):
        wait_keys()

        def ahead(u, carry):
            score(u, q_own, k_win, q_mark, k_mark, marked, scores, highest, peak)
            for slot in range(2):

                @pl.when(u == slot)
                def _(slot=slot):
                    share(v_win, 1, slot)

            return carry

        lax.fori_loop(0, AHEAD, ahead, 0)
        wait_values()

        def behind(u, carry):
            mix(u, v_win, out, scores, peak, sums, mixed)
            write(u).start()

            @pl.when(u + AHEAD < UNITS)
            def _():
                score(u + AHEAD, q_own, k_win, q_mark, k_mark, marked, scores, highest, peak)

            return carry

        lax.fori_loop(0, UNITS, behind, 0)
        for u in range(UNITS):
            write(u).wait()

    def first_part(x, normed, w, qd, vd, qu, vu):
        loads = [
            pltpu.make_async_copy(src, dst, ad_sem.at[i])
            for i, (src, dst) in enumerate([(qd_hbm, qd), (vd_hbm, vd), (qu_hbm, qu), (vu_hbm, vu)])
        ]
        for c in loads:
            c.start()
        x_loads = [
            pltpu.make_async_copy(x_hbm.at[pl.ds(64 * i, 64)], x.at[pl.ds(64 * i, 64)], x_sem.at[i])
            for i in range(8)
        ]
        gain_load = pltpu.make_async_copy(gain_hbm, gain_ref, gain_sem.at[0])
        gain_load.start()
        for c in x_loads:
            c.start()
        w_loads = [
            pltpu.make_async_copy(wk_hbm, w.at[0], w_sem.at[0]),
            pltpu.make_async_copy(wv_hbm, w.at[1], w_sem.at[1]),
        ] + [
            pltpu.make_async_copy(wq_hbm.at[:, pl.ds(256 * i, 256)], w.at[2 + i], w_sem.at[2 + i])
            for i in range(4)
        ]
        for c in w_loads:
            c.start()


        def gather(target, pieces):
            def one(t, carry):
                local = table_ref[tid_ref[t]] - me * HELD
                held = jnp.logical_and(local >= 0, local < HELD)
                at = jnp.clip(local, 0, HELD - 1)
                for stored, first, slabs in pieces:
                    for s in range(slabs):
                        tile = stored[at, :, s * 128 : (s + 1) * 128]
                        row = pl.multiple_of((first + s) * SLAB + t * RANK, RANK)
                        target[pl.ds(row, RANK), :] = jnp.where(held, tile, jnp.zeros_like(tile))
                return carry

            lax.fori_loop(0, TENANTS, one, 0)


        for c in loads[:2]:
            c.wait()
        gather(mine_d, [(qd, 0, 8), (vd, 8, 8)])
        lax.fori_loop(0, 8, angles, 0)
        marks(starts, ends, me, q_mark, k_mark)
        pl.semaphore_wait(barrier, len(greeted))
        red_d.start(0)
        for c in loads[2:]:
            c.wait()
        gather(mine_u, [(qu, 0, 8), (vu, 8, 2)])
        red_u.start(0)

        def normalise(first, count):
            def one(i, carry):
                at = pl.ds(pl.multiple_of(i * NORM_STEP, NORM_STEP), NORM_STEP)
                wide = x[at, :].astype(F32)
                scale = lax.rsqrt(jnp.mean(wide * wide, axis=1, keepdims=True) + NORM_EPS)
                normed[at, :] = (wide * scale * gain_ref[...]).astype(BF16)
                return carry

            lax.fori_loop(first, first + count, one, 0)


        red_d.step(0)
        gain_load.wait()
        for i in range(4):
            x_loads[i].wait()
        normalise(0, 8)
        for i in range(4, 8):
            x_loads[i].wait()
        normalise(8, 8)
        quarter[...] = normed[:, pl.ds(pl.multiple_of(z * 1024, 1024), 1024)]
        red_u.step(0)

        def product(j):
            w_loads_j = pltpu.make_async_copy(wk_hbm, w.at[j], w_sem.at[j])
            w_loads_j.wait()
            base[j] = jnp.dot(normed[...], w[j], preferred_element_type=F32)


        plan = [
            [keys, step(red_d, 1), send_k(0, 1)],
            [values, turn_v(0, 1), send_k(2, 3)],
            [step(red_d, 2), step(red_u, 1), pass_v(0, 1), turn_v(2, 3)],
            [pass_v(2, 3), forward_k(0, 1)],
            [step(red_d, 3), step(red_u, 2), forward_k(2, 3), after_turn(0, 1)],
            [forward_v(0, 1), send_v(0, 1, 2, 3), after_turn(2, 3), lambda: share(k_win, 0, 0)],
        ]

        def work(j, carry):
            product(j)
            for at, acts in enumerate(plan):

                @pl.when(j == at)
                def _(acts=acts):
                    for act in acts:
                        act()

            return carry

        lax.fori_loop(0, 6, work, 0)
        red_d.arrive(4)
        shrink()
        red_u.step(3)
        forward_v(2, 3)()
        shrunk()
        red_u.arrive(4)
        share(k_win, 0, 1)
        lax.fori_loop(0, 4, query, 0)

    pl.run_scoped(
        first_part,
        pltpu.VMEM((ROWS, WIDTH), BF16),
        pltpu.VMEM((ROWS, WIDTH), BF16),
        pltpu.VMEM((6, WIDTH, 256), BF16),
        pltpu.VMEM((HELD, RANK, 1024), BF16),
        pltpu.VMEM((HELD, RANK, 1024), BF16),
        pltpu.VMEM((HELD, RANK, QCOLS), BF16),
        pltpu.VMEM((HELD, RANK, KVCOLS), BF16),
    )
    pl.run_scoped(last_part, pltpu.VMEM((AHEAD, CHUNKS, 4 * QT, KC), F32))


def marks(starts, ends, me, q_mark, k_mark):
    lane = lax.broadcasted_iota(jnp.int32, (1, HEAD), 1)
    begin = jnp.full((1, HEAD), 2**30, jnp.int32)
    end = jnp.full((1, HEAD), 2**30, jnp.int32)
    for t in range(TENANTS):
        begin = jnp.where(lane == t, starts[t], begin)
        end = jnp.where(lane == t, ends[t], end)
    begin = jnp.where(lane == TENANTS, -(2**30), begin)
    end = jnp.where(lane == TENANTS, 0, end)

    def inside(first, row):
        token = first + row + lax.broadcasted_iota(jnp.int32, (128, HEAD), 0)
        return jnp.logical_and(token >= begin, token < end)

    def keys(i, carry):
        row = pl.multiple_of(i * 128, 128)
        k_mark[pl.ds(row, 128), :] = jnp.where(inside((me - BACK) * ROWS, row), 1.0, 0.0).astype(BF16)
        return carry

    lax.fori_loop(0, SPAN // 128, keys, 0)

    def queries(i, carry):
        row = pl.multiple_of(i * 128, 128)
        open_to = jnp.logical_or(inside(me * ROWS, row), lane > TENANTS)
        q_mark[pl.ds(row, 128), :] = jnp.where(open_to, 0.0, -FAR).astype(BF16)
        return carry

    lax.fori_loop(0, ROWS // 128, queries, 0)


def unit_of(u):
    group, part = u // 2, lax.rem(u, 2)
    rows = pl.ds(pl.multiple_of(part * QT, QT), QT)
    head_cols = pl.ds(pl.multiple_of(group * HEAD, HEAD), HEAD)
    return group, part, rows, head_cols


def score(u, q_ref, k_win, q_mark, k_mark, marked, scores, highest, peak):
    group, part, rows, head_cols = unit_of(u)
    slot = lax.rem(u, AHEAD)
    for h in range(4):
        marked[h * QT : (h + 1) * QT, :HEAD] = q_ref[
            2 * group + h // 2, rows, (h % 2) * HEAD : (h % 2 + 1) * HEAD
        ]
        marked[h * QT : (h + 1) * QT, HEAD:] = q_mark[rows, :]
    for i in range(CHUNKS):
        at = pl.multiple_of(part * QT + i * KC, 128)
        keys = jnp.concatenate([k_win[pl.ds(at, KC), head_cols], k_mark[pl.ds(at, KC), :]], axis=1)
        s = lax.dot_general(marked[...], keys, (((1,), (1,)), ((), ())), preferred_element_type=F32) * SCALE
        if i == CHUNKS - 1:
            seen = lax.broadcasted_iota(jnp.int32, (QT, QT), 0) >= lax.broadcasted_iota(jnp.int32, (QT, QT), 1)
            tail = s[:, KC - QT :]
            tail = jnp.concatenate(
                [jnp.where(seen, tail[h * QT : (h + 1) * QT, :], -FAR) for h in range(4)], axis=0
            )
            s = jnp.concatenate([s[:, : KC - QT], tail], axis=1)
        scores[slot, i] = s
        top = s[:, :128]
        for c in range(1, KC // 128):
            top = jnp.maximum(top, s[:, c * 128 : (c + 1) * 128])
        highest[...] = top if i == 0 else jnp.maximum(highest[...], top)
    peak[slot] = jnp.broadcast_to(jnp.max(highest[...], axis=1, keepdims=True), highest.shape)


def mix(u, v_win, out, scores, peak, sums, mixed):
    group, part, rows, head_cols = unit_of(u)
    slot = lax.rem(u, AHEAD)
    for i in range(CHUNKS):
        at = pl.multiple_of(part * QT + i * KC, 128)
        s = scores[slot, i]
        top = peak[slot]
        ps = [jnp.exp2(s[:, c * 128 : (c + 1) * 128] - top) for c in range(KC // 128)]
        total = ps[0]
        for p in ps[1:]:
            total = total + p
        probs = jnp.concatenate([p.astype(BF16) for p in ps], axis=1)
        product = jnp.dot(probs, v_win[pl.ds(at, KC), head_cols], preferred_element_type=F32)
        sums[...] = total if i == 0 else sums[...] + total
        mixed[...] = product if i == 0 else mixed[...] + product
    result = mixed[...] / jnp.sum(sums[...], axis=1, keepdims=True)
    for h in range(4):
        cols = pl.ds(pl.multiple_of(group * 512 + h * HEAD, HEAD), HEAD)
        out[rows, cols] = result[h * QT : (h + 1) * QT, :].astype(BF16)


def block(x, gain, wq, wk, wv, qd, vd, qu, vu, lengths, tid, slots):
    any_space = pl.BlockSpec(memory_space=pl.ANY)
    smem = pl.BlockSpec(memory_space=pltpu.SMEM)
    dma = pltpu.SemaphoreType.DMA

    def reduce_scratch(rows):
        return [
            pltpu.VMEM((rows, 128), BF16),
            pltpu.VMEM((rows // 2, 128), BF16),
            pltpu.VMEM((3, rows // 8, 128), BF16),
            pltpu.VMEM((3, rows // 8, 128), BF16),
            pltpu.VMEM((rows, 128), BF16),
        ]

    return pl.pallas_call(
        block_kernel,
        out_shape=jax.ShapeDtypeStruct((ROWS, QCOLS), BF16),
        in_specs=[smem] * 3 + [any_space] * 9,
        out_specs=any_space,
        scratch_shapes=[
            pltpu.VMEM((ROWS, QCOLS), BF16),
            pltpu.VMEM((1, WIDTH), F32),
            pltpu.VMEM((6, ROWS, 256), F32),
            pltpu.VMEM((ROWS, 1024), BF16),
        ]
        + reduce_scratch(DOWN_ROWS)
        + reduce_scratch(UP_ROWS)
        + [
            pltpu.VMEM((ROWS, HEAD), F32),
            pltpu.VMEM((ROWS, HEAD), F32),
            pltpu.VMEM((2 * RANK, ROWS), F32),
            pltpu.VMEM((3, 2 * RANK, ROWS), F32),
            pltpu.VMEM((BACK + 1, RANK, ROWS), BF16),
            pltpu.VMEM((SLAB, ROWS), BF16),
            pltpu.VMEM((SPAN, KVCOLS), BF16),
            pltpu.VMEM((SPAN, KVCOLS), BF16),
            pltpu.VMEM((ROWS, KVCOLS), BF16),
            pltpu.VMEM((ROWS, KVCOLS), BF16),
            pltpu.VMEM((4, ROWS, 256), BF16),
            pltpu.VMEM((ROWS, HEAD), BF16),
            pltpu.VMEM((SPAN, HEAD), BF16),
            pltpu.VMEM((4 * QT, 2 * HEAD), BF16),
            pltpu.VMEM((4 * QT, HEAD), F32),
            pltpu.VMEM((AHEAD, 4 * QT, HEAD), F32),
        ]
        + [pltpu.VMEM((4 * QT, HEAD), F32)] * 2
        + [
            dma((4,)), dma((8,)), dma((6,)),
            *[dma((COPIES,))] * 4,
            dma((1,)), dma((UNITS,)), dma((3,)), dma((3,)), dma((4 * PARTS,)), dma((4 * PARTS,)), *[dma((PARTS,))] * 5,
            dma((4,)), dma((4,)), dma((4,)), dma((4,)),
        ],
        compiler_params=pltpu.CompilerParams(
            collective_id=0, has_side_effects=True, vmem_limit_bytes=60 * 1024 * 1024
        ),
        name="block",
    )(lengths, tid, slots, x, gain, wq, wk, wv, qd, vd, qu, vu)


def body(
    layer_input, input_norm_gain, query_weight, key_weight, value_weight,
    query_down_maps, value_down_maps, query_up_maps, value_up_maps,
    tenant_prompt_length, tenant_adapter_id, adapter_storage_slot,
):
    return block(
        layer_input, input_norm_gain.reshape(1, WIDTH), query_weight, key_weight, value_weight,
        query_down_maps, value_down_maps, query_up_maps, value_up_maps,
        tenant_prompt_length, tenant_adapter_id, adapter_storage_slot,
    )


def solution(mesh):
    placed = (
        P("tok", None), P(), P(None, "mlp"), P(None, "mlp"), P(None, "mlp"),
        P("tok", None, "mlp"), P("tok", None, "mlp"), P("tok", None, "mlp"), P("tok", None, "mlp"),
        P(), P(), P(),
    )
    return jax.shard_map(
        body, mesh=mesh, in_specs=placed, out_specs=P("tok", "mlp"), check_vma=False
    )
```

```python
import functools

import jax
import jax.numpy as jnp
import numpy as np
from jax import lax
from jax.experimental import pallas as pl
from jax.experimental.pallas import tpu as pltpu
from jax.sharding import PartitionSpec as P

WIDTH = 4096
HEAD = 128
RANK = 16
TENANTS = 16
ROWS = 512
HELD = 8
QCOLS = 1024
KVCOLS = 256
BACK = 4
N_TOK = 32
SIDE = 4
NORM_EPS = 1e-05
ROPE_BASE = 500000.0
ADAPTER_SCALE = 0.5
MESH = pl.DeviceIdType.MESH
F32 = jnp.float32
BF16 = jnp.bfloat16
SLAB = TENANTS * RANK
DOWN_ROWS = 2 * 1024 // 128 * SLAB
UP_ROWS = (QCOLS + KVCOLS) // 128 * SLAB
AHEAD = 3
NORM_STEP = 32
SPAN = (BACK + 1) * ROWS
FAR = 1e30
QT = 256
KC = 1152
CHUNKS = (BACK * ROWS + QT) // KC
UNITS = 4
SCALE = np.float32(HEAD**-0.5 * np.log2(np.e))
COPIES = 11
PARTS = 4


def prompt_bounds(len_ref):
    starts, ends = [], []
    at = jnp.int32(0)
    for t in range(TENANTS):
        starts.append(at)
        at = at + len_ref[t]
        ends.append(at)
    return starts, ends


class AllReduce:
    def __init__(self, place, rows, mine, from_core, from_a, from_b, full, send, recv):
        self.place, self.rows = place, rows
        self.mine, self.from_core, self.from_a, self.from_b = mine, from_core, from_a, from_b
        self.full, self.send, self.recv = full, send, recv
        p = place
        half, quarter = rows // 2, rows // 8
        self.half_at = pl.multiple_of(p["core"] * half, 16)
        self.other_at = pl.multiple_of((1 - p["core"]) * half, 16)
        self.a_at = pl.multiple_of(p["core"] * half + p["ca"] * quarter, 16)

    def copy(self, slot, src, dst, dev):
        return pltpu.make_async_remote_copy(
            src_ref=src, dst_ref=dst, send_sem=self.send.at[slot], recv_sem=self.recv.at[slot],
            device_id=dev, device_id_type=MESH,
        )

    def copies(self, stage):
        p = self.place
        half, quarter = self.rows // 2, self.rows // 8
        if stage == 0:
            return [self.copy(0, self.mine.at[pl.ds(self.other_at, half)], self.from_core, p["sib"])]
        if stage == 4:
            ref = self.full.at[pl.ds(self.half_at, half)]
            return [self.copy(10, ref, ref, p["sib"])]
        out = []
        for k in range(1, SIDE):
            if stage == 1:
                a = (p["ca"] + k) % SIDE
                at = pl.multiple_of(p["core"] * half + a * quarter, 16)
                out.append(self.copy(k, self.mine.at[pl.ds(at, quarter)], self.from_a.at[k - 1], p["peer_a"][k]))
            if stage == 2:
                ref = self.mine.at[pl.ds(self.a_at, quarter)]
                out.append(self.copy(3 + k, ref, self.from_b.at[k - 1], p["peer_b"][k]))
            if stage == 3:
                ref = self.full.at[pl.ds(self.a_at, quarter)]
                out.append(self.copy(6 + k, ref, ref, p["peer_a"][k]))
        return out

    def start(self, stage):
        for c in self.copies(stage):
            c.start()

    def arrive(self, stage):
        for c in self.copies(stage):
            c.wait()
        half, quarter = self.rows // 2, self.rows // 8
        if stage == 0:
            at = pl.ds(self.half_at, half)
            self.mine[at, :] = self.mine[at, :] + self.from_core[...]
        if stage == 1:
            at = pl.ds(self.a_at, quarter)
            self.mine[at, :] = (self.mine[at, :] + self.from_a[0]) + (self.from_a[1] + self.from_a[2])
        if stage == 2:
            at = pl.ds(self.a_at, quarter)
            self.full[at, :] = (self.mine[at, :] + self.from_b[0]) + (self.from_b[1] + self.from_b[2])

    def step(self, stage):
        self.arrive(stage)
        self.start(stage + 1)


def block_kernel(
    len_ref, tid_ref, table_ref,
    x_hbm, gain_hbm, wq_hbm, wk_hbm, wv_hbm, qd_hbm, vd_hbm, qu_hbm, vu_hbm,
    out_hbm,
    out, gain_ref, base, quarter,
    mine_d, core_d, a_d, b_d, down,
    mine_u, core_u, a_u, b_u, up,
    cosine, sine, fold, got, shrunk_v, spread, k_win, v_win, passing, turning, q_own,
    q_mark, k_mark, marked, highest, peak, sums, mixed,
    ad_sem, x_sem, w_sem, sd, rd, su, ru, gain_sem, out_sem, z_send, z_recv, kv_send, kv_recv, pass_send, pass_recv, turn_send, turn_recv, turned, share_send, share_recv, s_send, s_recv,
):
    me = lax.axis_index("tok")
    z = lax.axis_index("mlp")
    core = lax.rem(me, 2)
    chip = me // 2
    px, py = lax.rem(chip, SIDE), chip // SIDE

    def tok_of(yy, xx, cc):
        return (yy * SIDE + xx) * 2 + cc

    sib = (me + 1 - 2 * core, z)
    x_first = 1 - core
    ca = px * x_first + py * (1 - x_first)
    cb = py * x_first + px * (1 - x_first)
    peer_a, peer_b, peer_z = {}, {}, {}
    for k in range(1, SIDE):
        xk, yk = (px + k) % SIDE, (py + k) % SIDE
        along_x = tok_of(py, xk, core)
        along_y = tok_of(yk, px, core)
        peer_a[k] = (along_x * x_first + along_y * (1 - x_first), z)
        peer_b[k] = (along_y * x_first + along_x * (1 - x_first), z)
        peer_z[k] = (me, (z + k) % SIDE)
    later = {k: ((me + k) % N_TOK, z) for k in range(1, BACK + 1)}
    earlier = {k: ((me + N_TOK - k) % N_TOK, z) for k in range(1, BACK + 1)}
    place = dict(core=core, ca=ca, cb=cb, sib=sib, peer_a=peer_a, peer_b=peer_b)

    barrier = pltpu.get_barrier_semaphore()
    over = (tok_of((py + px // 2) % SIDE, (px + 3) % SIDE, core), z)
    goal = (tok_of(py, (px + 3) % SIDE, core), z)
    under_x = (px + 1) % SIDE
    under = (tok_of((py + SIDE - under_x // 2) % SIDE, under_x, core), z)
    greeted = [sib, over, under] + [d[k] for d in (peer_a, peer_b, peer_z) for k in range(1, SIDE)]
    greeted += [d[k] for d in (later, earlier) for k in range(1, BACK + 1)]
    for dev in greeted:
        pl.semaphore_signal(barrier, inc=1, device_id=dev, device_id_type=MESH)

    starts, ends = prompt_bounds(len_ref)
    red_d = AllReduce(place, DOWN_ROWS, mine_d, core_d, a_d, b_d, down, sd, rd)
    red_u = AllReduce(place, UP_ROWS, mine_u, core_u, a_u, b_u, up, su, ru)

    def angles(i, carry):
        row = pl.multiple_of(i * 64, 64)
        token = me * ROWS + row + lax.broadcasted_iota(jnp.int32, (64, HEAD), 0)
        begin = jnp.zeros((64, HEAD), jnp.int32)
        for t in range(TENANTS):
            begin = jnp.where(token >= starts[t], starts[t], begin)
        lane = lax.broadcasted_iota(jnp.int32, (64, HEAD), 1)
        pair = jnp.where(lane >= HEAD // 2, lane - HEAD // 2, lane)
        inverse = jnp.exp(-(pair.astype(F32) * (2.0 / HEAD)) * np.float32(np.log(np.float32(ROPE_BASE))))
        angle = (token - begin).astype(F32) * inverse
        cosine[pl.ds(row, 64), :] = jnp.cos(angle)
        s = jnp.sin(angle)
        sine[pl.ds(row, 64), :] = jnp.where(lane >= HEAD // 2, s, -s)
        return carry


    def rope(block):
        return block * cosine[...] + pltpu.roll(block, HEAD // 2, 1) * sine[...]

    def rows_of(win, block, part, parts):
        size = ROWS // parts
        return win.at[pl.ds(pl.multiple_of(block * ROWS + part * size, size), size)]

    def win_copy(win, which, slot, part):
        at = (2 * which + slot) * PARTS + part
        if which == 0 or slot == 0:
            src, dst = rows_of(win, BACK - 2 * slot, part, PARTS), rows_of(win, 2 - 2 * slot, part, PARTS)
            dev = later[2]
        else:
            src, dst = rows_of(passing, 0, part, PARTS), rows_of(win, 0, part, PARTS)
            dev = goal
        return pltpu.make_async_remote_copy(
            src_ref=src, dst_ref=dst, send_sem=kv_send.at[at], recv_sem=kv_recv.at[at],
            device_id=dev, device_id_type=MESH,
        )

    def pass_copy(part):
        return pltpu.make_async_remote_copy(
            src_ref=rows_of(v_win, BACK, part, PARTS), dst_ref=rows_of(passing, 0, part, PARTS),
            send_sem=pass_send.at[part], recv_sem=pass_recv.at[part], device_id=over, device_id_type=MESH,
        )

    at_turn = px == SIDE - 1
    below = (tok_of((py + 1) % SIDE, px, core), z)
    row_start = (tok_of(py, 0, core), z)

    def turn_copy(part):
        return pltpu.make_async_remote_copy(
            src_ref=rows_of(v_win, BACK, part, PARTS), dst_ref=rows_of(turning, 0, part, PARTS),
            send_sem=turn_send.at[part], recv_sem=turn_recv.at[part], device_id=below, device_id_type=MESH,
        )

    def turned_copy(part):
        return pltpu.make_async_remote_copy(
            src_ref=rows_of(turning, 0, part, PARTS), dst_ref=rows_of(v_win, 2, part, PARTS),
            send_sem=turned.at[part], recv_sem=kv_recv.at[2 * PARTS + part], device_id=row_start,
            device_id_type=MESH,
        )

    def share_copy(win, which, slot):
        src, dst = (4 - 2 * core, 3) if slot == 0 else (2 - 2 * core, 1)
        at = 2 * which + slot
        return pltpu.make_async_remote_copy(
            src_ref=rows_of(win, src, 0, 1), dst_ref=rows_of(win, dst, 0, 1),
            send_sem=share_send.at[at], recv_sem=share_recv.at[at], device_id=sib, device_id_type=MESH,
        )

    def table(full, first, slabs):
        return jnp.concatenate([full[(first + s) * SLAB : (first + s + 1) * SLAB, :] for s in range(slabs)], axis=1)

    def members(first):
        token = first + lax.broadcasted_iota(jnp.int32, (RANK, ROWS), 1)
        return [jnp.logical_and(token >= starts[t], token < ends[t]) for t in range(TENANTS)]

    def z_copies():
        return [
            pltpu.make_async_remote_copy(
                src_ref=fold, dst_ref=got.at[k - 1], send_sem=z_send.at[k - 1], recv_sem=z_recv.at[k - 1],
                device_id=peer_z[k], device_id_type=MESH,
            )
            for k in range(1, SIDE)
        ]

    def shrunk_copies():
        return [
            pltpu.make_async_remote_copy(
                src_ref=shrunk_v.at[BACK], dst_ref=shrunk_v.at[BACK - k], send_sem=s_send.at[k - 1],
                recv_sem=s_recv.at[k - 1], device_id=later[k], device_id_type=MESH,
            )
            for k in range(1, BACK + 1)
        ]

    def shrink():
        maps = jnp.concatenate([table(down, 0, 8), table(down, 8, 8)], axis=0)
        part = lax.dot_general(maps, quarter[...], (((1,), (1,)), ((), ())), preferred_element_type=F32)
        mask = members(me * ROWS)
        for i in range(2):
            total = jnp.zeros((RANK, ROWS), F32)
            for t in range(TENANTS):
                row = i * SLAB + t * RANK
                total = total + jnp.where(mask[t], part[row : row + RANK, :], 0.0)
            fold[i * RANK : (i + 1) * RANK, :] = total
        for c in z_copies():
            c.start()

    def shrunk():
        for c in z_copies():
            c.wait()
        total = ((fold[...] + got[0]) + (got[1] + got[2])).astype(BF16)
        shrunk_v[BACK] = total[RANK:, :]
        for c in shrunk_copies():
            c.start()
        spread_out(total[:RANK, :].astype(F32), me * ROWS)

    def step(reduction, stage):
        return lambda: reduction.step(stage)

    def spread_out(values, first):
        mask = members(first)
        for t in range(TENANTS):
            spread[t * RANK : (t + 1) * RANK, :] = jnp.where(mask[t], values, 0.0).astype(BF16)

    def keys():
        for h in range(2):
            cols = slice(h * HEAD, (h + 1) * HEAD)
            k_win[BACK * ROWS :, cols] = rope(base[0, :, cols]).astype(BF16)

    def values():
        v_win[BACK * ROWS :, :] = base[1].astype(BF16)

    def send(win, which, slot, *parts):
        def act():
            for part in parts:
                win_copy(win, which, slot, part).start()

        return act

    def send_k(*parts):
        return send(k_win, 0, 0, *parts)

    def send_v(*parts):
        def act():
            @pl.when(jnp.logical_not(at_turn))
            def _():
                send(v_win, 1, 0, *parts)()

        return act

    def turn_v(*parts):
        def act():
            @pl.when(at_turn)
            def _():
                for part in parts:
                    turn_copy(part).start()

        return act

    def after_turn(*parts):
        def act():
            @pl.when(at_turn)
            def _():
                for part in parts:
                    turn_copy(part).wait()
                    turned_copy(part).start()

        return act

    def forward_k(*parts):
        def act():
            for part in parts:
                win_copy(k_win, 0, 0, part).wait()
                win_copy(k_win, 0, 1, part).start()

        return act

    def pass_v(*parts):
        def act():
            for part in parts:
                pass_copy(part).start()

        return act

    def forward_v(*parts):
        def act():
            for part in parts:
                pass_copy(part).wait()
                win_copy(v_win, 1, 1, part).start()

        return act

    def share(win, which, slot):
        for part in range(PARTS):
            if which == 1 and slot == 0:
                win_copy(win, which, slot, part).wait_recv()

                @pl.when(at_turn)
                def _(part=part):
                    turned_copy(part).wait_send()

                @pl.when(jnp.logical_not(at_turn))
                def _(part=part):
                    win_copy(win, which, slot, part).wait_send()

            elif which or slot:
                win_copy(win, which, slot, part).wait()
        share_copy(win, which, slot).start()

    def query(j, carry):
        cols = jnp.concatenate(
            [up[pl.ds(pl.multiple_of((2 * j + s) * SLAB, SLAB), SLAB), :] for s in range(2)], axis=1
        )
        delta = lax.dot_general(spread[...], cols, (((0,), (0,)), ((), ())), preferred_element_type=F32)
        rows = base[2 + j] + ADAPTER_SCALE * delta
        q_own[j] = jnp.concatenate([rope(rows[:, :HEAD]), rope(rows[:, HEAD:])], axis=1).astype(BF16)
        return carry

    def value(i, carry):
        at = pl.ds(pl.multiple_of(i * ROWS, ROWS), ROWS)
        spread_out(shrunk_v[i].astype(F32), (me - BACK + i) * ROWS)
        delta = lax.dot_general(
            spread[...], table(up, 8, 2), (((0,), (0,)), ((), ())), preferred_element_type=F32
        )
        own = jnp.where(i == BACK, base[1], v_win[at, :].astype(F32))
        v_win[at, :] = (own + ADAPTER_SCALE * delta).astype(BF16)
        return carry

    def wait_keys():
        for slot in range(2):
            share_copy(k_win, 0, slot).wait()

    def wait_values():
        for slot in range(2):
            share_copy(v_win, 1, slot).wait()
        for c in shrunk_copies():
            c.wait()
        lax.fori_loop(0, BACK + 1, value, 0)

    def write(u):
        group, part = u // 2, u % 2
        at = (pl.ds(pl.multiple_of(part * QT, QT), QT), pl.ds(pl.multiple_of(group * 512, 512), 512))
        return pltpu.make_async_copy(out.at[at], out_hbm.at[at], out_sem.at[u])

    def last_part(scores):
        wait_keys()

        def ahead(u, carry):
            score(u, q_own, k_win, q_mark, k_mark, marked, scores, highest, peak)
            for slot in range(2):

                @pl.when(u == slot)
                def _(slot=slot):
                    share(v_win, 1, slot)

            return carry

        lax.fori_loop(0, AHEAD, ahead, 0)
        wait_values()

        def behind(u, carry):
            mix(u, v_win, out, scores, peak, sums, mixed)
            write(u).start()

            @pl.when(u + AHEAD < UNITS)
            def _():
                score(u + AHEAD, q_own, k_win, q_mark, k_mark, marked, scores, highest, peak)

            return carry

        lax.fori_loop(0, UNITS, behind, 0)
        for u in range(UNITS):
            write(u).wait()

    def first_part(x, normed, w, qd, vd, qu, vu):
        loads = [
            pltpu.make_async_copy(src, dst, ad_sem.at[i])
            for i, (src, dst) in enumerate([(qd_hbm, qd), (vd_hbm, vd), (qu_hbm, qu), (vu_hbm, vu)])
        ]
        for c in loads:
            c.start()
        x_loads = [
            pltpu.make_async_copy(x_hbm.at[pl.ds(64 * i, 64)], x.at[pl.ds(64 * i, 64)], x_sem.at[i])
            for i in range(8)
        ]
        gain_load = pltpu.make_async_copy(gain_hbm, gain_ref, gain_sem.at[0])
        gain_load.start()
        for c in x_loads:
            c.start()
        w_loads = [
            pltpu.make_async_copy(wk_hbm, w.at[0], w_sem.at[0]),
            pltpu.make_async_copy(wv_hbm, w.at[1], w_sem.at[1]),
        ] + [
            pltpu.make_async_copy(wq_hbm.at[:, pl.ds(256 * i, 256)], w.at[2 + i], w_sem.at[2 + i])
            for i in range(4)
        ]
        for c in w_loads:
            c.start()


        def gather(target, pieces):
            def one(t, carry):
                local = table_ref[tid_ref[t]] - me * HELD
                held = jnp.logical_and(local >= 0, local < HELD)
                at = jnp.clip(local, 0, HELD - 1)
                for stored, first, slabs in pieces:
                    for s in range(slabs):
                        tile = stored[at, :, s * 128 : (s + 1) * 128]
                        row = pl.multiple_of((first + s) * SLAB + t * RANK, RANK)
                        target[pl.ds(row, RANK), :] = jnp.where(held, tile, jnp.zeros_like(tile))
                return carry

            lax.fori_loop(0, TENANTS, one, 0)


        for c in loads[:2]:
            c.wait()
        gather(mine_d, [(qd, 0, 8), (vd, 8, 8)])
        lax.fori_loop(0, 8, angles, 0)
        marks(starts, ends, me, q_mark, k_mark)
        pl.semaphore_wait(barrier, len(greeted))
        red_d.start(0)
        for c in loads[2:]:
            c.wait()
        gather(mine_u, [(qu, 0, 8), (vu, 8, 2)])
        red_u.start(0)

        def normalise(first, count):
            def one(i, carry):
                at = pl.ds(pl.multiple_of(i * NORM_STEP, NORM_STEP), NORM_STEP)
                wide = x[at, :].astype(F32)
                scale = lax.rsqrt(jnp.mean(wide * wide, axis=1, keepdims=True) + NORM_EPS)
                normed[at, :] = (wide * scale * gain_ref[...]).astype(BF16)
                return carry

            lax.fori_loop(first, first + count, one, 0)


        red_d.step(0)
        gain_load.wait()
        for i in range(4):
            x_loads[i].wait()
        normalise(0, 8)
        for i in range(4, 8):
            x_loads[i].wait()
        normalise(8, 8)
        quarter[...] = normed[:, pl.ds(pl.multiple_of(z * 1024, 1024), 1024)]
        red_u.step(0)

        def product(j):
            w_loads_j = pltpu.make_async_copy(wk_hbm, w.at[j], w_sem.at[j])
            w_loads_j.wait()
            base[j] = jnp.dot(normed[...], w[j], preferred_element_type=F32)


        plan = [
            [keys, step(red_d, 1), send_k(0, 1)],
            [values, turn_v(0, 1), send_k(2, 3)],
            [step(red_d, 2), step(red_u, 1), pass_v(0, 1), turn_v(2, 3)],
            [pass_v(2, 3), forward_k(0, 1)],
            [step(red_d, 3), forward_k(2, 3), step(red_u, 2), after_turn(0, 1)],
            [forward_v(0, 1), send_v(0, 1, 2, 3), after_turn(2, 3), lambda: share(k_win, 0, 0)],
        ]

        def work(j, carry):
            product(j)
            for at, acts in enumerate(plan):

                @pl.when(j == at)
                def _(acts=acts):
                    for act in acts:
                        act()

            return carry

        lax.fori_loop(0, 6, work, 0)
        red_d.arrive(4)
        shrink()
        red_u.step(3)
        forward_v(2, 3)()
        shrunk()
        red_u.arrive(4)
        share(k_win, 0, 1)
        lax.fori_loop(0, 4, query, 0)

    pl.run_scoped(
        first_part,
        pltpu.VMEM((ROWS, WIDTH), BF16),
        pltpu.VMEM((ROWS, WIDTH), BF16),
        pltpu.VMEM((6, WIDTH, 256), BF16),
        pltpu.VMEM((HELD, RANK, 1024), BF16),
        pltpu.VMEM((HELD, RANK, 1024), BF16),
        pltpu.VMEM((HELD, RANK, QCOLS), BF16),
        pltpu.VMEM((HELD, RANK, KVCOLS), BF16),
    )
    pl.run_scoped(last_part, pltpu.VMEM((AHEAD, CHUNKS, 4 * QT, KC), F32))


def marks(starts, ends, me, q_mark, k_mark):
    lane = lax.broadcasted_iota(jnp.int32, (1, HEAD), 1)
    begin = jnp.full((1, HEAD), 2**30, jnp.int32)
    end = jnp.full((1, HEAD), 2**30, jnp.int32)
    for t in range(TENANTS):
        begin = jnp.where(lane == t, starts[t], begin)
        end = jnp.where(lane == t, ends[t], end)
    begin = jnp.where(lane == TENANTS, -(2**30), begin)
    end = jnp.where(lane == TENANTS, 0, end)

    def inside(first, row):
        token = first + row + lax.broadcasted_iota(jnp.int32, (128, HEAD), 0)
        return jnp.logical_and(token >= begin, token < end)

    def keys(i, carry):
        row = pl.multiple_of(i * 128, 128)
        k_mark[pl.ds(row, 128), :] = jnp.where(inside((me - BACK) * ROWS, row), 1.0, 0.0).astype(BF16)
        return carry

    lax.fori_loop(0, SPAN // 128, keys, 0)

    def queries(i, carry):
        row = pl.multiple_of(i * 128, 128)
        open_to = jnp.logical_or(inside(me * ROWS, row), lane > TENANTS)
        q_mark[pl.ds(row, 128), :] = jnp.where(open_to, 0.0, -FAR).astype(BF16)
        return carry

    lax.fori_loop(0, ROWS // 128, queries, 0)


def unit_of(u):
    group, part = u // 2, lax.rem(u, 2)
    rows = pl.ds(pl.multiple_of(part * QT, QT), QT)
    head_cols = pl.ds(pl.multiple_of(group * HEAD, HEAD), HEAD)
    return group, part, rows, head_cols


def score(u, q_ref, k_win, q_mark, k_mark, marked, scores, highest, peak):
    group, part, rows, head_cols = unit_of(u)
    slot = lax.rem(u, AHEAD)
    for h in range(4):
        marked[h * QT : (h + 1) * QT, :HEAD] = q_ref[
            2 * group + h // 2, rows, (h % 2) * HEAD : (h % 2 + 1) * HEAD
        ]
        marked[h * QT : (h + 1) * QT, HEAD:] = q_mark[rows, :]
    for i in range(CHUNKS):
        at = pl.multiple_of(part * QT + i * KC, 128)
        keys = jnp.concatenate([k_win[pl.ds(at, KC), head_cols], k_mark[pl.ds(at, KC), :]], axis=1)
        s = lax.dot_general(marked[...], keys, (((1,), (1,)), ((), ())), preferred_element_type=F32) * SCALE
        if i == CHUNKS - 1:
            seen = lax.broadcasted_iota(jnp.int32, (QT, QT), 0) >= lax.broadcasted_iota(jnp.int32, (QT, QT), 1)
            tail = s[:, KC - QT :]
            tail = jnp.concatenate(
                [jnp.where(seen, tail[h * QT : (h + 1) * QT, :], -FAR) for h in range(4)], axis=0
            )
            s = jnp.concatenate([s[:, : KC - QT], tail], axis=1)
        scores[slot, i] = s
        top = s[:, :128]
        for c in range(1, KC // 128):
            top = jnp.maximum(top, s[:, c * 128 : (c + 1) * 128])
        highest[...] = top if i == 0 else jnp.maximum(highest[...], top)
    peak[slot] = jnp.broadcast_to(jnp.max(highest[...], axis=1, keepdims=True), highest.shape)


def mix(u, v_win, out, scores, peak, sums, mixed):
    group, part, rows, head_cols = unit_of(u)
    slot = lax.rem(u, AHEAD)
    for i in range(CHUNKS):
        at = pl.multiple_of(part * QT + i * KC, 128)
        s = scores[slot, i]
        top = peak[slot]
        ps = [jnp.exp2(s[:, c * 128 : (c + 1) * 128] - top) for c in range(KC // 128)]
        total = ps[0]
        for p in ps[1:]:
            total = total + p
        probs = jnp.concatenate([p.astype(BF16) for p in ps], axis=1)
        product = jnp.dot(probs, v_win[pl.ds(at, KC), head_cols], preferred_element_type=F32)
        sums[...] = total if i == 0 else sums[...] + total
        mixed[...] = product if i == 0 else mixed[...] + product
    result = mixed[...] / jnp.sum(sums[...], axis=1, keepdims=True)
    for h in range(4):
        cols = pl.ds(pl.multiple_of(group * 512 + h * HEAD, HEAD), HEAD)
        out[rows, cols] = result[h * QT : (h + 1) * QT, :].astype(BF16)


def block(x, gain, wq, wk, wv, qd, vd, qu, vu, lengths, tid, slots):
    any_space = pl.BlockSpec(memory_space=pl.ANY)
    smem = pl.BlockSpec(memory_space=pltpu.SMEM)
    dma = pltpu.SemaphoreType.DMA

    def reduce_scratch(rows):
        return [
            pltpu.VMEM((rows, 128), BF16),
            pltpu.VMEM((rows // 2, 128), BF16),
            pltpu.VMEM((3, rows // 8, 128), BF16),
            pltpu.VMEM((3, rows // 8, 128), BF16),
            pltpu.VMEM((rows, 128), BF16),
        ]

    return pl.pallas_call(
        block_kernel,
        out_shape=jax.ShapeDtypeStruct((ROWS, QCOLS), BF16),
        in_specs=[smem] * 3 + [any_space] * 9,
        out_specs=any_space,
        scratch_shapes=[
            pltpu.VMEM((ROWS, QCOLS), BF16),
            pltpu.VMEM((1, WIDTH), F32),
            pltpu.VMEM((6, ROWS, 256), F32),
            pltpu.VMEM((ROWS, 1024), BF16),
        ]
        + reduce_scratch(DOWN_ROWS)
        + reduce_scratch(UP_ROWS)
        + [
            pltpu.VMEM((ROWS, HEAD), F32),
            pltpu.VMEM((ROWS, HEAD), F32),
            pltpu.VMEM((2 * RANK, ROWS), F32),
            pltpu.VMEM((3, 2 * RANK, ROWS), F32),
            pltpu.VMEM((BACK + 1, RANK, ROWS), BF16),
            pltpu.VMEM((SLAB, ROWS), BF16),
            pltpu.VMEM((SPAN, KVCOLS), BF16),
            pltpu.VMEM((SPAN, KVCOLS), BF16),
            pltpu.VMEM((ROWS, KVCOLS), BF16),
            pltpu.VMEM((ROWS, KVCOLS), BF16),
            pltpu.VMEM((4, ROWS, 256), BF16),
            pltpu.VMEM((ROWS, HEAD), BF16),
            pltpu.VMEM((SPAN, HEAD), BF16),
            pltpu.VMEM((4 * QT, 2 * HEAD), BF16),
            pltpu.VMEM((4 * QT, HEAD), F32),
            pltpu.VMEM((AHEAD, 4 * QT, HEAD), F32),
        ]
        + [pltpu.VMEM((4 * QT, HEAD), F32)] * 2
        + [
            dma((4,)), dma((8,)), dma((6,)),
            *[dma((COPIES,))] * 4,
            dma((1,)), dma((UNITS,)), dma((3,)), dma((3,)), dma((4 * PARTS,)), dma((4 * PARTS,)), *[dma((PARTS,))] * 5,
            dma((4,)), dma((4,)), dma((4,)), dma((4,)),
        ],
        compiler_params=pltpu.CompilerParams(
            collective_id=0, has_side_effects=True, vmem_limit_bytes=60 * 1024 * 1024
        ),
        name="block",
    )(lengths, tid, slots, x, gain, wq, wk, wv, qd, vd, qu, vu)


def body(
    layer_input, input_norm_gain, query_weight, key_weight, value_weight,
    query_down_maps, value_down_maps, query_up_maps, value_up_maps,
    tenant_prompt_length, tenant_adapter_id, adapter_storage_slot,
):
    return block(
        layer_input, input_norm_gain.reshape(1, WIDTH), query_weight, key_weight, value_weight,
        query_down_maps, value_down_maps, query_up_maps, value_up_maps,
        tenant_prompt_length, tenant_adapter_id, adapter_storage_slot,
    )


def solution(mesh):
    placed = (
        P("tok", None), P(), P(None, "mlp"), P(None, "mlp"), P(None, "mlp"),
        P("tok", None, "mlp"), P("tok", None, "mlp"), P("tok", None, "mlp"), P("tok", None, "mlp"),
        P(), P(), P(),
    )
    return jax.shard_map(
        body, mesh=mesh, in_specs=placed, out_specs=P("tok", "mlp"), check_vma=False
    )
```
